32 devices in a mesh: dp: 8 (over z, y), tensor: 4 (over x, core).
Axes of the slice: x: 2, y: 2, z: 4, core: 2. Of those that a mesh axis runs over, the one named last changes fastest.
Arguments:
- inputs: bfloat16 [8192, 512], P(('dp', 'tensor')), may hold values from -13 to 13
- lengths: int32 [8], P('dp'), may hold values from 256 to 1024, as said below
- cotangent: bfloat16 [8192, 512], P(('dp', 'tensor')), may hold values from -6 to 6
- query_weight: bfloat16 [512, 512], P('dp', 'tensor'), may hold values from -0.25 to 0.25
- key_weight: bfloat16 [512, 512], P('dp', 'tensor'), may hold values from -0.25 to 0.25
- value_weight: bfloat16 [512, 512], P('dp', 'tensor'), may hold values from -0.25 to 0.25
- output_weight: bfloat16 [512, 512], P('tensor', 'dp'), may hold values from -1 to 1
- inner_weight: bfloat16 [512, 2048], P('dp', 'tensor'), may hold values from -0.25 to 0.25
- outer_weight: bfloat16 [2048, 512], P('tensor', 'dp'), may hold values from -0.125 to 0.125
- first_gain: bfloat16 [512], P('dp'), may hold values from 0.099609375 to 1.8984375
- second_gain: bfloat16 [512], P('dp'), may hold values from 0.099609375 to 1.8984375
Outputs:
- outputs: bfloat16 [8192, 512], P(('dp', 'tensor'))
- input_grad: bfloat16 [8192, 512], P(('dp', 'tensor'))
- query_weight_grad: float32 [512, 512], P('dp', 'tensor')
- key_weight_grad: float32 [512, 512], P('dp', 'tensor')
- value_weight_grad: float32 [512, 512], P('dp', 'tensor')
- output_weight_grad: float32 [512, 512], P('tensor', 'dp')
- inner_weight_grad: float32 [512, 2048], P('dp', 'tensor')
- outer_weight_grad: float32 [2048, 512], P('tensor', 'dp')
- first_gain_grad: float32 [512], P('dp')
- second_gain_grad: float32 [512], P('dp')
- root_mean_squares: float32 [3], replicated
The draws below stay inside these ranges and needn't reach their ends.
Inputs may be any that keep to these rules, and one draw needn't show every extreme that they name: `lengths`: one sequence of every draw is whole.
All inputs are finite; a program needn't handle non-finite values.
Results may differ from the reference program's by a relative error of at most 0.017.
Values may be sent and summed in bfloat16 or wider, within the bound.
A program may use at most 320 MiB of HBM per device.

```python
import jax
import jax.numpy as jnp
from jax import lax

D = 512
HEADS = 8
HEAD_DIM = 64
FF = 2048
BLOCK = 16
LENGTH = 1024
SEQS = 8
TOKENS = 8192


def draw_inputs(key, part):
    noise_key, direction_key = jax.random.split(jax.random.fold_in(key, 11), 2)
    ramp = jnp.arange(SEQS, dtype=jnp.float32) / (SEQS - 1)
    direction = jnp.clip(jax.random.normal(direction_key, (SEQS, D), jnp.float32), -3.0, 3.0)
    noise = jnp.clip(jax.random.normal(noise_key, (SEQS, LENGTH, D), jnp.float32), -4.0, 4.0)
    strength = 3.0 * ramp
    values = noise + direction[:, None, :] * strength[:, None, None]
    return values.reshape(TOKENS, D).astype(jnp.bfloat16)


def draw_lengths(key, part):
    pick_key, length_key = jax.random.split(jax.random.fold_in(key, 23))
    drawn = jax.random.randint(length_key, (SEQS,), LENGTH // 4, LENGTH + 1)
    whole_one = jax.random.randint(pick_key, (), 0, SEQS)
    return jnp.where(jnp.arange(SEQS) == whole_one, LENGTH, drawn).astype(jnp.int32)


def levels(stream_key, extent, shards, smallest, top_value):
    def one(position, blocks):
        draws = jax.random.uniform(jax.random.fold_in(jax.random.fold_in(stream_key, 6), position), (blocks,), jnp.float32, smallest / len(shards), top_value / len(shards))
        return jnp.repeat(jnp.exp(draws), extent[position] // blocks).reshape((-1,) + (1,) * (len(extent) - position - 1))

    factor_of = one(*shards[0])
    for cut in shards[1:]:
        factor_of = factor_of * one(*cut)
    return factor_of


def gaussian(rng, dims, deviation, most, cuts=(), kind=jnp.bfloat16):
    level = levels(rng, dims, cuts, -0.22, 0.18) if cuts else 1.0
    values = jax.random.normal(rng, dims, jnp.float32) * deviation * level
    return jnp.minimum(jnp.maximum(values, -most), most).astype(kind)


def setup_inputs(seed: int = 0) -> dict:
    splits = jax.random.split(jax.random.key(seed), 12)
    inputs = draw_inputs(jax.random.fold_in(splits[11], 71), 0)
    lengths = draw_lengths(jax.random.fold_in(splits[11], 71), 0)
    cotangent = gaussian(splits[2], (TOKENS, D), 1.0, 6.0, ((0, 32),))
    query_weight = gaussian(splits[3], (D, HEADS * HEAD_DIM), D ** -0.5, 0.25, ((0, 8), (1, 4)))
    key_weight = gaussian(splits[4], (D, HEADS * HEAD_DIM), D ** -0.5, 0.25, ((0, 8), (1, 4)))
    value_weight = gaussian(splits[5], (D, HEADS * HEAD_DIM), D ** -0.5, 0.25, ((0, 8), (1, 4)))
    output_weight = gaussian(splits[6], (HEADS * HEAD_DIM, D), (D // 16) ** -0.5, 1.0, ((0, 4), (1, 8)))
    inner_weight = gaussian(splits[7], (D, FF), D ** -0.5, 0.25, ((0, 8), (1, 4)))
    outer_weight = gaussian(splits[8], (FF, D), FF ** -0.5, 0.125, ((0, 4), (1, 8)))
    first_gain = jnp.clip(1.0 + 0.18 * jax.random.normal(splits[9], (D,), jnp.float32), 0.099609375, 1.8984375).astype(jnp.bfloat16)
    second_gain = jnp.clip(1.0 + 0.18 * jax.random.normal(splits[10], (D,), jnp.float32), 0.099609375, 1.8984375).astype(jnp.bfloat16)
    return dict(inputs=inputs, lengths=lengths, cotangent=cotangent, query_weight=query_weight, key_weight=key_weight, value_weight=value_weight, output_weight=output_weight, inner_weight=inner_weight, outer_weight=outer_weight, first_gain=first_gain, second_gain=second_gain)


@jax.custom_vjp
def low(v):
    return lax.optimization_barrier(v.astype(jnp.bfloat16)).astype(jnp.float32)

@jax.custom_vjp
def low_back(v):
    return v

def low_keep(v):
    return (low(v), None)

def low_pass(kept, grad):
    return (grad,)

def back_keep(v):
    return (v, None)

def back_low(kept, grad):
    return (low(grad),)
low.defvjp(low_keep, low_pass)
low_back.defvjp(back_keep, back_low)
top_level = lax.Precision.HIGHEST

def neighbours(blocks):
    padded = jnp.pad(blocks, ((1, 1),) + ((0, 0),) * (blocks.ndim - 1))
    return jnp.concatenate([padded[:-2], padded[1:-1], padded[2:]], axis=1)

def level_terms(queries, key_rows, value_rows, valid_rows, factor):
    sequence_len, width_per_head = queries.shape
    pooled_level = sequence_len // factor
    coarse_q = lax.optimization_barrier(jnp.mean(queries.reshape(pooled_level, factor, width_per_head), axis=1))
    counts = lax.optimization_barrier(jnp.sum(valid_rows.reshape(pooled_level, factor), axis=1))
    divisor = jnp.maximum(counts, 1.0)[:, None]
    coarse_k = lax.optimization_barrier(jnp.sum((key_rows * valid_rows[:, None]).reshape(pooled_level, factor, width_per_head), axis=1)) / divisor
    coarse_v = lax.optimization_barrier(jnp.sum((value_rows * valid_rows[:, None]).reshape(pooled_level, factor, width_per_head), axis=1)) / divisor
    blocks = pooled_level // BLOCK
    query_block_rows = coarse_q.reshape(blocks, BLOCK, width_per_head)
    nearby_key_rows = neighbours(coarse_k.reshape(blocks, BLOCK, width_per_head))
    nearby_value_rows = neighbours(coarse_v.reshape(blocks, BLOCK, width_per_head))
    c_near = neighbours(counts.reshape(blocks, BLOCK))
    logit_scores = jnp.einsum('une,uhe->unh', query_block_rows, nearby_key_rows, precision=top_level) * width_per_head ** (-0.5)
    weights = jnp.broadcast_to(c_near[:, None, :], logit_scores.shape)
    if factor > 1:
        block_ids = jnp.arange(blocks, dtype=jnp.int32)[:, None]
        q_pos = block_ids * BLOCK + jnp.arange(BLOCK, dtype=jnp.int32)[None, :]
        k_pos = (block_ids - 1) * BLOCK + jnp.arange(3 * BLOCK, dtype=jnp.int32)[None, :]
        half_block = BLOCK // 2
        apart = jnp.abs(q_pos[:, :, None] // half_block - k_pos[:, None, :] // half_block) > 1
        weights = jnp.where(apart, weights, 0.0)
    is_live = weights > 0.0
    row_top = lax.optimization_barrier(jnp.max(jnp.where(is_live, logit_scores, -1e+30), axis=-1))
    safe_top = jnp.where(row_top > -1e+29, row_top, 0.0)
    weighted_values = weights * jnp.exp(logit_scores - safe_top[..., None])
    softmax_numerator = jnp.einsum('vwg,vgi->vwi', weighted_values, nearby_value_rows, precision=top_level).reshape(pooled_level, width_per_head)
    denominator = lax.optimization_barrier(jnp.sum(weighted_values, axis=-1)).reshape(pooled_level)
    row_top = row_top.reshape(pooled_level)
    return (jnp.repeat(softmax_numerator, factor, axis=0), jnp.repeat(denominator, factor), jnp.repeat(row_top, factor))

def hierarchy(queries, key_rows, value_rows, valid_len):
    sequence_len = queries.shape[0]
    valid_rows = (jnp.arange(sequence_len, dtype=jnp.int32) < valid_len).astype(jnp.float32)
    depth = (sequence_len // BLOCK).bit_length() - 1
    levels_out = [level_terms(queries, key_rows, value_rows, valid_rows, 2 ** level) for level in range(depth)]
    overall = levels_out[0][2]
    for entry in levels_out[1:]:
        overall = jnp.maximum(overall, entry[2])
    softmax_numerator = levels_out[0][0] * jnp.exp(levels_out[0][2] - overall)[:, None]
    denominator = levels_out[0][1] * jnp.exp(levels_out[0][2] - overall)
    for entry in levels_out[1:]:
        factor_now = jnp.exp(entry[2] - overall)
        softmax_numerator = softmax_numerator + entry[0] * factor_now[:, None]
        denominator = denominator + entry[1] * factor_now
    return softmax_numerator / denominator[:, None]

def layer_norm(residual, gain_values):
    row_mean = lax.optimization_barrier(jnp.mean(residual, axis=-1, keepdims=True))
    centred = residual - row_mean
    variance = lax.optimization_barrier(jnp.mean(centred * centred, axis=-1, keepdims=True))
    return centred * lax.rsqrt(variance + 1e-05) * gain_values

def gelu_tanh(values):
    return jax.nn.gelu(values, approximate=True)

def matmul(left, right):
    return jnp.dot(left, right, precision=top_level, preferred_element_type=jnp.float32)

def forward(residual, seq_lens, query_weight, key_weight, value_weight, output_weight, inner_weight, outer_weight, first_gain, second_gain):
    sequences = seq_lens.shape[0]
    sequence_len = residual.shape[0] // sequences
    head_count = query_weight.shape[1] // HEAD_DIM
    normed_one = low(layer_norm(residual, first_gain))
    queries = low_back(low(matmul(normed_one, query_weight)))
    key_rows = low_back(low(matmul(normed_one, key_weight)))
    value_rows = low_back(low(matmul(normed_one, value_weight)))

    def split_heads(matrix):
        return matrix.reshape(sequences, sequence_len, head_count, HEAD_DIM).transpose(0, 2, 1, 3).reshape(sequences * head_count, sequence_len, HEAD_DIM)
    head_lens = jnp.repeat(seq_lens, head_count)

    def one_head(items):
        return hierarchy(items[0], items[1], items[2], items[3])
    attended = lax.map(jax.checkpoint(one_head), (split_heads(queries), split_heads(key_rows), split_heads(value_rows), head_lens))
    attended = attended.reshape(sequences, head_count, sequence_len, HEAD_DIM).transpose(0, 2, 1, 3).reshape(sequences * sequence_len, head_count * HEAD_DIM)
    attended = low(attended)
    attention_branch = low_back(matmul(attended, output_weight))
    middle = residual + attention_branch
    normed_two = low(layer_norm(middle, second_gain))
    pre_act = low_back(matmul(normed_two, inner_weight))
    activated = low(gelu_tanh(pre_act))
    dense_branch = low_back(matmul(activated, outer_weight))
    return (middle + dense_branch, (attention_branch, dense_branch))

def reference(inputs, lengths, cotangent, query_weight, key_weight, value_weight, output_weight, inner_weight, outer_weight, first_gain, second_gain):
    params = tuple((param.astype(jnp.float32) for param in (query_weight, key_weight, value_weight, output_weight, inner_weight, outer_weight, first_gain, second_gain)))
    rows_all = inputs.astype(jnp.float32).reshape(SEQS, LENGTH, D)
    cot_all = cotangent.astype(jnp.float32).reshape(SEQS, LENGTH, D)
    lens_all = lengths.reshape(SEQS, 1)

    def one_sequence(carry, item):
        grad_sums, stat_sums = carry
        seq_rows, seq_lens, seq_cot = item

        def layer_of(rows_in, *weights_in):
            return forward(rows_in, seq_lens, *weights_in)
        result, pullback, branches = jax.vjp(layer_of, seq_rows, *params, has_aux=True)
        grads = pullback(seq_cot)
        valid_rows = (jnp.arange(LENGTH, dtype=jnp.int32) < seq_lens[0]).astype(jnp.float32)
        squares = jnp.stack([jnp.sum(valid_rows * lax.optimization_barrier(jnp.sum(result * result, axis=1))), jnp.sum(valid_rows * lax.optimization_barrier(jnp.sum(branches[0] * branches[0], axis=1))), jnp.sum(valid_rows * lax.optimization_barrier(jnp.sum(branches[1] * branches[1], axis=1))), jnp.sum(valid_rows)])
        new_grads = tuple((left + right for left, right in zip(grad_sums, grads[1:])))
        return ((new_grads, stat_sums + squares), (result.astype(jnp.bfloat16), grads[0].astype(jnp.bfloat16)))
    start_state = (tuple((jnp.zeros(param.shape, jnp.float32) for param in params)), jnp.zeros((4,), jnp.float32))
    (grad_sums, stat_sums), (results, input_grads) = lax.scan(one_sequence, start_state, (rows_all, lens_all, cot_all))
    root_mean_squares = jnp.sqrt(stat_sums[:3] / (stat_sums[3] * D))
    return (results.reshape(TOKENS, D), input_grads.reshape(TOKENS, D), grad_sums[0], grad_sums[1], grad_sums[2], grad_sums[3], grad_sums[4], grad_sums[5], grad_sums[6], grad_sums[7], root_mean_squares)
```

```python
import functools

import jax
import jax.numpy as jnp
from jax import lax
from jax.experimental import pallas as pl
from jax.experimental.pallas import tpu as pltpu
from jax.sharding import PartitionSpec as P

MESH = pl.DeviceIdType.MESH
F32, BF = jnp.float32, jnp.bfloat16
HEAD_DIM = 64
EPS = 1e-05

ROWS, PAIRS, LEVELS = 256, 4, 6
COUNT = (256, 128, 64, 32, 16, 8)
AT = (0, 256, 384, 448, 480, 496)
STACK = 512
OWN = (32, 352, 544, 656)
LEFT = (16, 336, 528, 640, 704)
RIGHT = (288, 480, 608, 688, 720)
FAR = 736
KEYS = 768
BLANK = ((0, 16), (304, 32), (496, 32), (624, 16))
TILE_AT = (0, 64, 128, 192, 320, 384, 512, 640)
TILES = 8
HALO = 80


def nn(a, b):
    return lax.dot_general(a, b, (((1,), (0,)), ((), ())), preferred_element_type=F32)


def nt(a, b):
    return lax.dot_general(a, b, (((1,), (1,)), ((), ())), preferred_element_type=F32)


def tn(a, b):
    return lax.dot_general(a, b, (((0,), (0,)), ((), ())), preferred_element_type=F32)


def iota(shape, dim):
    return lax.broadcasted_iota(jnp.int32, shape, dim)


def level_counts(index, level, total, valid_len):
    factor = 1 << level
    c = jnp.clip(valid_len - index * factor, 0, factor)
    return jnp.where((index >= 0) & (index < total), c, 0).astype(F32)


def tile_weights(k, me, tensors, valid_len):
    i, j = iota((64, 128), 0), iota((64, 128), 1)
    if k < 7:
        level = 0 if k < 4 else 1 if k < 6 else 2
        first = 64 * (k - AT[level] // 64)
        n = COUNT[level]
        c = level_counts(me * n + first - 32 + j, level, n * tensors, valid_len)
        near = jnp.abs((i >> 4) - (j >> 4) + 2) <= 1
        if level:
            near = near & (jnp.abs((i >> 3) - (j >> 3) + 4) > 1)
        return jnp.where(near, c, 0.0)
    c3 = level_counts(me * 32 + j - 16, 3, 32 * tensors, valid_len)
    near3 = (jnp.abs((i >> 4) - (j >> 4) + 1) <= 1) & (jnp.abs((i >> 3) - (j >> 3) + 2) > 1)
    near3 = near3 & (i < 32) & (j < 64)
    key4 = jnp.where(j < 80, j - 80, j - 64)
    c4 = level_counts(me * 16 + key4, 4, 16 * tensors, valid_len)
    near4 = (jnp.abs(((i - 32) >> 3) - (key4 >> 3)) > 1) & (i >= 32) & (i < 48) & (j >= 64) & (j < 96)
    key5 = j - 96
    c5 = level_counts(key5, 5, 8 * tensors, valid_len)
    near5 = (jnp.abs(me - (key5 >> 3)) > 1) & (i >= 48) & (i < 56) & (j >= 96)
    return jnp.where(near3, c3, 0.0) + jnp.where(near4, c4, 0.0) + jnp.where(near5, c5, 0.0)


def row_divisors(me, tensors, valid_len):
    i = iota((STACK, 128), 0)
    out = jnp.ones((STACK, 128), F32)
    for level in range(1, LEVELS):
        c = level_counts(i - AT[level] + me * COUNT[level], level, COUNT[level] * tensors, valid_len)
        here = (i >= AT[level]) & (i < AT[level] + COUNT[level])
        out = jnp.where(here, 1.0 / jnp.maximum(c, 1.0), out)
    return out


def stack_factors():
    i = iota((STACK, 128), 0)
    out = jnp.full((STACK, 128), HEAD_DIM ** (-0.5), F32)
    for level in range(1, LEVELS):
        out = jnp.where(i >= AT[level], HEAD_DIM ** (-0.5) / (1 << level), out)
    return out


def pairs_of(ref, start, n):
    return ref[pl.ds(start, n, stride=2), :], ref[pl.ds(start + 1, n, stride=2), :]


def pool(ref):
    for level in range(LEVELS - 1):
        n = COUNT[level + 1]
        even, odd = pairs_of(ref, AT[level], n)
        ref[AT[level + 1] : AT[level + 1] + n, :] = even + odd


def doubled(ref, value, n):
    ref[pl.ds(0, n, stride=2), :] = value
    ref[pl.ds(1, n, stride=2), :] = value
    return ref[0 : 2 * n, :]


def normalised(v):
    centred = v - jnp.mean(v, axis=-1, keepdims=True)
    r = lax.rsqrt(jnp.mean(centred * centred, axis=-1, keepdims=True) + EPS)
    return centred * r, r


def norm_back(n, r, hg):
    return r * (hg - jnp.mean(hg, axis=-1, keepdims=True) - n * jnp.mean(hg * n, axis=-1, keepdims=True))


def gelu_both(u):
    c = 0.7978845608028654
    square = u * u
    th = jnp.tanh(c * (u + 0.044715 * (square * u)))
    half = 0.5 * (1.0 + th)
    slope = half + (0.5 * c) * u * (1.0 - th * th) * (1.0 + 0.134145 * square)
    return u * half, slope


def layer_kernel(
    tensors,
    len_ref,
    x_ref,
    cot_ref,
    wa_ref,
    wb_ref,
    out_ref,
    ingrad_ref,
    ga_ref,
    gb_ref,
    small_ref,
    qs,
    ks,
    vs,
    qb,
    kw,
    vw,
    wt,
    rdiv,
    edge_l,
    edge_r,
    halo_l,
    halo_r,
    far,
    eb,
    ns,
    ml,
    ds_,
    att,
    mm,
    tmp_a,
    tmp_b,
    tmp_c,
    n1s,
    n2s,
    dacc,
    us,
    mus,
    dqs,
    dkw,
    back_l,
    back_r,
    got_l,
    got_r,
    dfar,
    gfar,
    send_sem,
    recv_sem,
):
    me = lax.axis_index("tensor")
    valid_len = len_ref[0]
    barrier = pltpu.get_barrier_semaphore()
    for k in range(1, tensors):
        pl.semaphore_signal(barrier, inc=1, device_id={"tensor": lax.rem(me + k, tensors)}, device_id_type=MESH)
    pl.semaphore_wait(barrier, tensors - 1)

    lane = iota((64, 128), 1)
    low_lanes = lane < 64
    low_b = low_lanes.astype(F32).astype(BF)
    high_b = (1.0 - low_lanes.astype(F32)).astype(BF)

    def both(v):
        return jnp.concatenate([v * low_b, v * high_b], axis=0)

    def joined(v):
        return jnp.where(low_lanes, v[:64], v[64:])

    n1, r1 = normalised(x_ref[...].astype(F32))
    n1s[...] = n1
    n1b = n1.astype(BF)
    valid = (iota((ROWS, 128), 0) + me * ROWS < valid_len).astype(F32)
    for t in range(PAIRS):
        joint = nn(n1b[:, :256], wa_ref[t, 0]) + nn(n1b[:, 256:], wa_ref[t, 1])
        joint = joint.astype(BF).astype(F32)
        qs[t, 0:ROWS, :] = joint[:, :128]
        ks[t, 0:ROWS, :] = joint[:, 128:256] * valid
        vs[t, 0:ROWS, :] = joint[:, 256:] * valid
    rdiv[...] = row_divisors(me, tensors, valid_len)
    for k in range(TILES):
        wt[k] = tile_weights(k, me, tensors, valid_len)

    def pooling(p, carry):
        pool(qs.at[p])
        qs[p, 504:STACK, :] = jnp.zeros((8, 128), F32)
        qb[p] = (qs[p] * stack_factors()).astype(BF)
        for which, (raw, windows) in enumerate(((ks, kw), (vs, vw))):
            raw_p = raw.at[p]
            pool(raw_p)
            row = which * PAIRS + p
            for start, n in BLANK:
                windows[p, start : start + n, :] = jnp.zeros((n, 128), BF)
            for level in range(LEVELS - 1):
                n = COUNT[level]
                rows = slice(AT[level], AT[level] + n)
                coarse = (raw_p[rows, :] * rdiv[rows, :]).astype(BF)
                if level < 4:
                    windows[p, OWN[level] : OWN[level] + n, :] = coarse
                edge_l[row, 16 * level : 16 * level + 16, :] = coarse[:16]
                edge_r[row, 16 * level : 16 * level + 16, :] = coarse[n - 16 :]
            rows = slice(AT[5], AT[5] + 8)
            far[me, row] = raw_p[rows, :] * rdiv[rows, :]
        return carry

    lax.fori_loop(0, PAIRS, pooling, 0)

    def to_left(src, dst, sem):
        return pltpu.make_async_remote_copy(
            src, dst, send_sem.at[sem], recv_sem.at[sem], device_id={"tensor": jnp.maximum(me - 1, 0)}, device_id_type=MESH
        )

    def to_right(src, dst, sem):
        return pltpu.make_async_remote_copy(
            src,
            dst,
            send_sem.at[sem],
            recv_sem.at[sem],
            device_id={"tensor": jnp.minimum(me + 1, tensors - 1)},
            device_id_type=MESH,
        )

    def to_peer(k, src, dst, sem):
        return pltpu.make_async_remote_copy(
            src, dst, send_sem.at[sem], recv_sem.at[sem], device_id={"tensor": lax.rem(me + k, tensors)}, device_id_type=MESH
        )

    def exchange(base, left_src, left_dst, right_src, right_dst, far_src, far_dst):
        for k in range(1, tensors):
            to_peer(k, far_src(k), far_dst(k), base + 1 + k).start()

        @pl.when(me > 0)
        def _():
            to_left(left_src, left_dst, base).start()

        @pl.when(me < tensors - 1)
        def _():
            to_right(right_src, right_dst, base + 1).start()

    def exchanged(base, left_src, left_dst, right_src, right_dst, far_src, far_dst):
        @pl.when(me > 0)
        def _():
            to_left(left_src, left_dst, base).wait_send()
            to_right(right_src, right_dst, base + 1).wait_recv()

        @pl.when(me == 0)
        def _():
            right_dst[...] = jnp.zeros(right_dst.shape, BF)

        @pl.when(me < tensors - 1)
        def _():
            to_right(right_src, right_dst, base + 1).wait_send()
            to_left(left_src, left_dst, base).wait_recv()

        @pl.when(me == tensors - 1)
        def _():
            left_dst[...] = jnp.zeros(left_dst.shape, BF)

        for k in range(1, tensors):
            to_peer(k, far_src(k), far_dst(k), base + 1 + k).wait()

    halos = (0, edge_l, halo_r, edge_r, halo_l, lambda k: far.at[me], lambda k: far.at[me])
    exchange(*halos)
    exchanged(*halos)

    def attend(p, carry):
        for which, windows in enumerate((kw, vw)):
            row = which * PAIRS + p
            for level in range(LEVELS - 1):
                windows[p, LEFT[level] : LEFT[level] + 16, :] = halo_l[row, 16 * level : 16 * level + 16, :]
                windows[p, RIGHT[level] : RIGHT[level] + 16, :] = halo_r[row, 16 * level : 16 * level + 16, :]
            groups = jnp.concatenate([far[g, row] for g in range(tensors)], axis=0)
            windows[p, FAR:KEYS, :] = groups.astype(BF)
        for k in range(TILES):
            here = slice(64 * k, 64 * k + 64)
            keys = slice(TILE_AT[k], TILE_AT[k] + 128)
            s = nt(both(qb[p, here, :]), kw[p, keys, :])
            w = wt[k]
            w = jnp.concatenate([w, w], axis=0)
            s = jnp.where(w > 0.0, s, -1e30)
            m = jnp.max(s, axis=-1, keepdims=True)
            e = w * jnp.exp(s - m)
            low = e.astype(BF)
            total = jnp.sum(low.astype(F32), axis=-1, keepdims=True)
            eb[p, k] = low
            ns[here, :] = joined(nn(low, vw[p, keys, :]))
            ml[p, here, :] = joined(jnp.broadcast_to(m, (128, 128)))
            ds_[here, :] = joined(jnp.broadcast_to(total, (128, 128)))
        rows = slice(AT[5], AT[5] + 8)
        num, top, den = ns[rows, :], ml[p, rows, :], ds_[rows, :]
        for level in range(LEVELS - 2, -1, -1):
            n = COUNT[level]
            rows = slice(AT[level], AT[level] + n)
            num, top, den = doubled(tmp_a, num, n // 2), doubled(tmp_b, top, n // 2), doubled(tmp_c, den, n // 2)
            own = ml[p, rows, :]
            both_top = jnp.maximum(own, top)
            left, right = jnp.exp(own - both_top), jnp.exp(top - both_top)
            num = ns[rows, :] * left + num * right
            den = ds_[rows, :] * left + den * right
            top = both_top
        inverse = 1.0 / den
        att[p] = num * inverse
        mm[p] = top
        dacc[p] = inverse
        return carry

    lax.fori_loop(0, PAIRS, attend, 0)

    attb = [att[t].astype(BF) for t in range(PAIRS)]
    branch = []
    for y in range(2):
        total = nt(attb[0], wb_ref[0, y, :, 0:128])
        for t in range(1, PAIRS):
            total = total + nt(attb[t], wb_ref[t, y, :, 0:128])
        branch.append(total)
    branch = jnp.concatenate(branch, axis=1)
    middle = x_ref[...].astype(F32) + branch
    n2, r2 = normalised(middle)
    n2s[...] = n2
    n2b = n2.astype(BF)
    n2t = n2b.T
    cotb = cot_ref[...]
    cott = cotb.T

    dense, dn2 = [0.0, 0.0], [0.0, 0.0]
    for t in range(PAIRS):
        pre = nn(n2b[:, :256], wb_ref[t, 0, :, 128:640]) + nn(n2b[:, 256:], wb_ref[t, 1, :, 128:640])
        act, slope = gelu_both(pre)
        act = act.astype(BF)
        act_grad = nn(cotb[:, :256], wb_ref[t, 0, :, 640:1152]) + nn(cotb[:, 256:], wb_ref[t, 1, :, 640:1152])
        pre_grad = (act_grad * slope).astype(BF)
        for y in range(2):
            half = slice(256 * y, 256 * y + 256)
            dense[y] = dense[y] + nt(act, wb_ref[t, y, :, 640:1152])
            dn2[y] = dn2[y] + nt(pre_grad, wb_ref[t, y, :, 128:640])
            gb_ref[t, y, :, 128:640] = nn(n2t[half, :], pre_grad).astype(BF)
            gb_ref[t, y, :, 640:1152] = nn(cott[half, :], act).astype(BF)
    dense = jnp.concatenate(dense, axis=1)
    dn2 = jnp.concatenate(dn2, axis=1)
    result = middle + dense
    out_ref[...] = result.astype(BF)
    live = (iota((ROWS, 512), 0) + me * ROWS < valid_len).astype(F32)
    small_ref[2:3, :] = jnp.sum(live * result * result, axis=0, keepdims=True)
    small_ref[3:4, :] = jnp.sum(live * branch * branch, axis=0, keepdims=True)
    small_ref[4:5, :] = jnp.sum(live * dense * dense, axis=0, keepdims=True)
    small_ref[5:6, :] = jnp.sum(live, axis=0, keepdims=True)
    small_ref[6:8, :] = jnp.zeros((2, 512), F32)
    n2 = n2s[...]
    small_ref[1:2, :] = jnp.sum(dn2 * n2, axis=0, keepdims=True)
    middle_grad = cotb.astype(F32) + norm_back(n2, r2, dn2)
    n2s[...] = middle_grad
    mgb = middle_grad.astype(BF)
    mgt = mgb.T
    for t in range(PAIRS):
        us[t, 0:ROWS, :] = nn(mgb[:, :256], wb_ref[t, 0, :, 0:128]) + nn(mgb[:, 256:], wb_ref[t, 1, :, 0:128])
        for y in range(2):
            gb_ref[t, y, :, 0:128] = nn(mgt[256 * y : 256 * y + 256, :], att[t].astype(BF)).astype(BF)

    def head_sums(v):
        first = jnp.sum(jnp.where(iota(v.shape, 1) < 64, v, 0.0), axis=-1, keepdims=True)
        second = jnp.sum(jnp.where(iota(v.shape, 1) < 64, 0.0, v), axis=-1, keepdims=True)
        return jnp.where(iota(v.shape, 1) < 64, first, second)

    def attend_back(p, carry):
        up = us.at[p]
        grad, inverse = up[0:ROWS, :], dacc[p]
        delta = head_sums(grad * att[p])
        up[0:ROWS, :] = grad * inverse
        ns[0:ROWS, :] = delta * inverse
        mus[0:ROWS, :] = mm[p]
        for level in range(LEVELS - 1):
            n = COUNT[level + 1]
            after = slice(AT[level + 1], AT[level + 1] + n)
            top_e, top_o = pairs_of(mus, AT[level], n)
            top = jnp.minimum(top_e, top_o)
            fe, fo = jnp.exp(top - top_e), jnp.exp(top - top_o)
            u_e, u_o = pairs_of(up, AT[level], n)
            d_e, d_o = pairs_of(ns, AT[level], n)
            up[after, :] = u_e * fe + u_o * fo
            ns[after, :] = d_e * fe + d_o * fo
            mus[after, :] = top
        for rows in (slice(504, STACK),):
            up[rows, :] = jnp.zeros((8, 128), F32)
            ns[rows, :] = jnp.zeros((8, 128), F32)
            mus[rows, :] = jnp.zeros((8, 128), F32)
        for which in range(2):
            dkw[which * PAIRS + p, 0:512, :] = jnp.zeros((512, 128), F32)
        for k in range(TILES):
            here = slice(64 * k, 64 * k + 64)
            keys = slice(TILE_AT[k], TILE_AT[k] + 128)
            factor = jnp.exp(ml[p, here, :] - mus[here, :])
            g = up[here, :] * factor
            g_high = g.astype(BF)
            g2 = both(g_high)
            g4 = jnp.concatenate([g2, both((g - g_high.astype(F32)).astype(BF))], axis=1)
            v2 = vw[p, keys, :]
            v2 = jnp.concatenate([v2, v2], axis=1)
            h = ns[here, :] * factor
            h2 = jnp.concatenate([h[:, 0:1], h[:, 64:65]], axis=0)
            q2 = both(qb[p, here, :])
            low = eb[p, k]
            d = low.astype(F32) * (nt(g4, v2) - h2)
            d = d.astype(BF)
            dv = tn(low, g2)
            dk = tn(d, q2)
            if k < 6:
                dkw[p, keys, :] = dkw[p, keys, :] + dk
                dkw[PAIRS + p, keys, :] = dkw[PAIRS + p, keys, :] + dv
            else:
                dkw[p, keys, :] = dk
                dkw[PAIRS + p, keys, :] = dv
            dqs[p, here, :] = joined(nn(d, kw[p, keys, :]))
        for which in range(2):
            row = which * PAIRS + p
            for level in range(LEVELS - 1):
                part = slice(16 * level, 16 * level + 16)
                back_l[row, part, :] = dkw[row, LEFT[level] : LEFT[level] + 16, :].astype(BF)
                back_r[row, part, :] = dkw[row, RIGHT[level] : RIGHT[level] + 16, :].astype(BF)
            for g in range(tensors):
                dfar[g, row] = dkw[row, FAR + 8 * g : FAR + 8 * g + 8, :]
        return carry

    lax.fori_loop(0, PAIRS, attend_back, 0)

    back = (
        8,
        back_l,
        got_r,
        back_r,
        got_l,
        lambda k: dfar.at[lax.rem(me + k, tensors)],
        lambda k: gfar.at[k],
    )
    exchange(*back)
    exchanged(*back)

    def unpool(p, carry):
        factors = stack_factors()
        cur = dqs[p, AT[5] : AT[5] + 8, :] * factors[AT[5] : AT[5] + 8]
        for level in range(LEVELS - 2, -1, -1):
            rows = slice(AT[level], AT[level] + COUNT[level])
            cur = doubled(tmp_a, cur, COUNT[level] // 2) + dqs[p, rows, :] * factors[rows]
        qs[p, 0:ROWS, :] = cur
        for which, raw in enumerate((ks, vs)):
            row = which * PAIRS + p
            raw_p = raw.at[p]
            cur = gfar[1, row]
            for k in range(2, tensors):
                cur = cur + gfar[k, row]
            cur = cur * rdiv[AT[5] : AT[5] + 8, :]
            for level in range(LEVELS - 2, -1, -1):
                n = COUNT[level]
                rows = slice(AT[level], AT[level] + n)
                part = slice(16 * level, 16 * level + 16)
                if level < 4:
                    raw_p[rows, :] = dkw[row, OWN[level] : OWN[level] + n, :]
                else:
                    raw_p[rows, :] = jnp.zeros((n, 128), F32)
                first = slice(AT[level], AT[level] + 16)
                last = slice(AT[level] + n - 16, AT[level] + n)
                raw_p[first, :] = raw_p[first, :] + got_l[row, part, :].astype(F32)
                raw_p[last, :] = raw_p[last, :] + got_r[row, part, :].astype(F32)
                cur = doubled(tmp_a, cur, n // 2) + raw_p[rows, :] * rdiv[rows, :]
            raw_p[0:ROWS, :] = cur * (iota((ROWS, 128), 0) + me * ROWS < valid_len).astype(F32)
        return carry

    lax.fori_loop(0, PAIRS, unpool, 0)

    n1 = n1s[...]
    n1t = n1.astype(BF).T
    dn1 = [0.0, 0.0]
    for t in range(PAIRS):
        joint = jnp.concatenate(
            [qs[t, 0:ROWS, :].astype(BF), ks[t, 0:ROWS, :].astype(BF), vs[t, 0:ROWS, :].astype(BF)], axis=1
        )
        for y in range(2):
            ga_ref[t, y] = nn(n1t[256 * y : 256 * y + 256, :], joint).astype(BF)
            dn1[y] = dn1[y] + nt(joint, wa_ref[t, y])
    dn1 = jnp.concatenate(dn1, axis=1)
    small_ref[0:1, :] = jnp.sum(dn1 * n1, axis=0, keepdims=True)
    r1 = lax.rsqrt(row_variance(x_ref[...].astype(F32)) + EPS)
    ingrad_ref[...] = (n2s[...] + norm_back(n1, r1, dn1)).astype(BF)


def row_variance(v):
    centred = v - jnp.mean(v, axis=-1, keepdims=True)
    return jnp.mean(centred * centred, axis=-1, keepdims=True)


def run_layer(tensors, lengths, inputs, cotangent, wa, wb):
    vmem = pl.BlockSpec(memory_space=pltpu.VMEM)
    f = lambda *shape: pltpu.VMEM(shape, F32)
    b = lambda *shape: pltpu.VMEM(shape, BF)
    return pl.pallas_call(
        functools.partial(layer_kernel, tensors),
        out_shape=(
            jax.ShapeDtypeStruct((ROWS, 512), BF),
            jax.ShapeDtypeStruct((ROWS, 512), BF),
            jax.ShapeDtypeStruct(wa.shape, BF),
            jax.ShapeDtypeStruct(wb.shape, BF),
            jax.ShapeDtypeStruct((8, 512), F32),
        ),
        in_specs=[pl.BlockSpec(memory_space=pltpu.SMEM), vmem, vmem, vmem, vmem],
        out_specs=(vmem,) * 5,
        scratch_shapes=[
            f(PAIRS, STACK, 128),
            f(PAIRS, STACK, 128),
            f(PAIRS, STACK, 128),
            b(PAIRS, STACK, 128),
            b(PAIRS, KEYS, 128),
            b(PAIRS, KEYS, 128),
            f(TILES, 64, 128),
            f(STACK, 128),
            b(2 * PAIRS, HALO, 128),
            b(2 * PAIRS, HALO, 128),
            b(2 * PAIRS, HALO, 128),
            b(2 * PAIRS, HALO, 128),
            f(tensors, 2 * PAIRS, 8, 128),
            b(PAIRS, TILES, 128, 128),
            f(STACK, 128),
            f(PAIRS, STACK, 128),
            f(STACK, 128),
            f(PAIRS, ROWS, 128),
            f(PAIRS, ROWS, 128),
            f(ROWS, 128),
            f(ROWS, 128),
            f(ROWS, 128),
            f(ROWS, 512),
            f(ROWS, 512),
            f(PAIRS, ROWS, 128),
            f(PAIRS, STACK, 128),
            f(STACK, 128),
            f(PAIRS, STACK, 128),
            f(2 * PAIRS, KEYS, 128),
            b(2 * PAIRS, HALO, 128),
            b(2 * PAIRS, HALO, 128),
            b(2 * PAIRS, HALO, 128),
            b(2 * PAIRS, HALO, 128),
            f(tensors, 2 * PAIRS, 8, 128),
            f(tensors, 2 * PAIRS, 8, 128),
            pltpu.SemaphoreType.DMA((16,)),
            pltpu.SemaphoreType.DMA((16,)),
        ],
        compiler_params=pltpu.CompilerParams(
            collective_id=0, has_side_effects=True, vmem_limit_bytes=60 * 1024 * 1024
        ),
        name="layer",
    )(lengths, inputs, cotangent, wa, wb)


def per_device(
    inputs,
    lengths,
    cotangent,
    query_weight,
    key_weight,
    value_weight,
    output_weight,
    inner_weight,
    outer_weight,
    first_gain,
    second_gain,
):
    tensors, groups = lax.axis_size("tensor"), lax.axis_size("dp")
    everyone = ("tensor", "dp")
    g1 = first_gain.astype(F32)[:, None]
    g2 = second_gain.astype(F32)[:, None]
    scaled = lambda g, w: (g * w.astype(F32)).astype(BF)
    part_a = scaled(g1, jnp.concatenate([query_weight, key_weight, value_weight], axis=1))
    part_b = jnp.concatenate([output_weight.T, scaled(g2, inner_weight), outer_weight.T], axis=1)
    wa = lax.all_gather(part_a, everyone, axis=0, tiled=True).reshape(tensors, 2, 256, 384)
    wb = lax.all_gather(part_b, everyone, axis=0, tiled=True).reshape(tensors, 2, 256, 1152)
    out, input_grad, ga, gb, small = run_layer(tensors, lengths, inputs, cotangent, wa, wb)
    width = first_gain.shape[0]

    def reduced(g):
        return lax.psum_scatter(
            g.reshape(tensors * 512, g.shape[-1]).astype(F32), everyone, scatter_dimension=0, tiled=True
        )

    ga, gb, small = reduced(ga), reduced(gb), lax.psum(small, everyone)
    at = lax.axis_index("dp") * width
    gains = lax.dynamic_slice(small, (0, at), (2, width))
    sums = jnp.sum(small, axis=1)
    root_mean_squares = jnp.sqrt(sums[2:5] / sums[5])
    ga = ga * g1
    return (
        out,
        input_grad,
        ga[:, 0:128],
        ga[:, 128:256],
        ga[:, 256:384],
        gb[:, 0:128].T,
        gb[:, 128:640] * g2,
        gb[:, 640:1152].T,
        gains[0] / first_gain.astype(F32),
        gains[1] / second_gain.astype(F32),
        root_mean_squares,
    )


def solution(mesh):
    return jax.shard_map(
        per_device,
        mesh=mesh,
        in_specs=(
            P(("dp", "tensor"), None),
            P("dp"),
            P(("dp", "tensor"), None),
            P("dp", "tensor"),
            P("dp", "tensor"),
            P("dp", "tensor"),
            P("tensor", "dp"),
            P("dp", "tensor"),
            P("tensor", "dp"),
            P("dp"),
            P("dp"),
        ),
        out_specs=(
            P(("dp", "tensor"), None),
            P(("dp", "tensor"), None),
            P("dp", "tensor"),
            P("dp", "tensor"),
            P("dp", "tensor"),
            P("tensor", "dp"),
            P("dp", "tensor"),
            P("tensor", "dp"),
            P("dp"),
            P("dp"),
            P(),
        ),
        check_vma=False,
    )
```

```python
import functools

import jax
import jax.numpy as jnp
from jax import lax
from jax.experimental import pallas as pl
from jax.experimental.pallas import tpu as pltpu
from jax.sharding import PartitionSpec as P

MESH = pl.DeviceIdType.MESH
F32, BF = jnp.float32, jnp.bfloat16
HEAD_DIM = 64
EPS = 1e-05

ROWS, PAIRS, LEVELS = 256, 4, 6
COUNT = (256, 128, 64, 32, 16, 8)
AT = (0, 256, 384, 448, 480, 496)
STACK = 512
OWN = (32, 352, 544, 656)
LEFT = (16, 336, 528, 640, 704)
RIGHT = (288, 480, 608, 688, 720)
FAR = 736
KEYS = 768
BLANK = ((0, 16), (304, 32), (496, 32), (624, 16))
TILE_AT = (0, 64, 128, 192, 320, 384, 512, 640)
TILES = 8
HALO = 80


def nn(a, b):
    return lax.dot_general(a, b, (((1,), (0,)), ((), ())), preferred_element_type=F32)


def nt(a, b):
    return lax.dot_general(a, b, (((1,), (1,)), ((), ())), preferred_element_type=F32)


def tn(a, b):
    return lax.dot_general(a, b, (((0,), (0,)), ((), ())), preferred_element_type=F32)


def iota(shape, dim):
    return lax.broadcasted_iota(jnp.int32, shape, dim)


def level_counts(index, level, total, valid_len):
    factor = 1 << level
    c = jnp.clip(valid_len - index * factor, 0, factor)
    return jnp.where((index >= 0) & (index < total), c, 0).astype(F32)


def tile_weights(k, me, tensors, valid_len):
    i, j = iota((64, 128), 0), iota((64, 128), 1)
    if k < 7:
        level = 0 if k < 4 else 1 if k < 6 else 2
        first = 64 * (k - AT[level] // 64)
        n = COUNT[level]
        c = level_counts(me * n + first - 32 + j, level, n * tensors, valid_len)
        near = jnp.abs((i >> 4) - (j >> 4) + 2) <= 1
        if level:
            near = near & (jnp.abs((i >> 3) - (j >> 3) + 4) > 1)
        return jnp.where(near, c, 0.0)
    c3 = level_counts(me * 32 + j - 16, 3, 32 * tensors, valid_len)
    near3 = (jnp.abs((i >> 4) - (j >> 4) + 1) <= 1) & (jnp.abs((i >> 3) - (j >> 3) + 2) > 1)
    near3 = near3 & (i < 32) & (j < 64)
    key4 = jnp.where(j < 80, j - 80, j - 64)
    c4 = level_counts(me * 16 + key4, 4, 16 * tensors, valid_len)
    near4 = (jnp.abs(((i - 32) >> 3) - (key4 >> 3)) > 1) & (i >= 32) & (i < 48) & (j >= 64) & (j < 96)
    key5 = j - 96
    c5 = level_counts(key5, 5, 8 * tensors, valid_len)
    near5 = (jnp.abs(me - (key5 >> 3)) > 1) & (i >= 48) & (i < 56) & (j >= 96)
    return jnp.where(near3, c3, 0.0) + jnp.where(near4, c4, 0.0) + jnp.where(near5, c5, 0.0)


def row_divisors(me, tensors, valid_len):
    i = iota((STACK, 128), 0)
    out = jnp.ones((STACK, 128), F32)
    for level in range(1, LEVELS):
        c = level_counts(i - AT[level] + me * COUNT[level], level, COUNT[level] * tensors, valid_len)
        here = (i >= AT[level]) & (i < AT[level] + COUNT[level])
        out = jnp.where(here, 1.0 / jnp.maximum(c, 1.0), out)
    return out


def stack_factors():
    i = iota((STACK, 128), 0)
    out = jnp.full((STACK, 128), HEAD_DIM ** (-0.5), F32)
    for level in range(1, LEVELS):
        out = jnp.where(i >= AT[level], HEAD_DIM ** (-0.5) / (1 << level), out)
    return out


def pairs_of(ref, start, n):
    return ref[pl.ds(start, n, stride=2), :], ref[pl.ds(start + 1, n, stride=2), :]


def pool(ref):
    for level in range(LEVELS - 1):
        n = COUNT[level + 1]
        even, odd = pairs_of(ref, AT[level], n)
        ref[AT[level + 1] : AT[level + 1] + n, :] = even + odd


def doubled(ref, value, n):
    ref[pl.ds(0, n, stride=2), :] = value
    ref[pl.ds(1, n, stride=2), :] = value
    return ref[0 : 2 * n, :]


def normalised(v):
    centred = v - jnp.mean(v, axis=-1, keepdims=True)
    r = lax.rsqrt(jnp.mean(centred * centred, axis=-1, keepdims=True) + EPS)
    return centred * r, r


def norm_back(n, r, hg):
    return r * (hg - jnp.mean(hg, axis=-1, keepdims=True) - n * jnp.mean(hg * n, axis=-1, keepdims=True))


def gelu_both(u):
    c = 0.7978845608028654
    square = u * u
    th = jnp.tanh(c * (u + 0.044715 * (square * u)))
    half = 0.5 * (1.0 + th)
    slope = half + (0.5 * c) * u * (1.0 - th * th) * (1.0 + 0.134145 * square)
    return u * half, slope


class Place:
    def __init__(self):
        self.d, self.t = lax.axis_index("dp"), lax.axis_index("tensor")
        self.z, self.y = self.d // 2, self.d % 2
        self.x, self.c = self.t // 2, self.t % 2
        self.a = self.x + self.c * (self.y - self.x)
        self.b = self.y + self.c * (self.x - self.y)
        flip_x, flip_y = 2 - 4 * self.x, 1 - 2 * self.y
        self.to_x, self.to_y = (self.d, self.t + flip_x), (self.d + flip_y, self.t)
        self.to_a = (self.d + self.c * flip_y, self.t + (1 - self.c) * flip_x)
        self.to_b = (self.d + (1 - self.c) * flip_y, self.t + self.c * flip_x)
        self.to_other = (self.d, self.t + 1 - 2 * self.c)
        self.to_across = (self.d, 3 - self.t)

    def to_z(self, k):
        return (2 * ((self.z + k) % 4) + self.y, self.t)


def flipped(bit, by):
    return 1 - bit if by else bit


class Remote:
    def __init__(self, send_sem, recv_sem):
        self.send_sem, self.recv_sem, self.started = send_sem, recv_sem, set()

    def copy(self, i, src, dst, to):
        return pltpu.make_async_remote_copy(
            src, dst, self.send_sem.at[i], self.recv_sem.at[i], device_id=to, device_id_type=MESH
        )

    def send(self, i, src, dst, to):
        self.copy(i, src, dst, to).start()
        self.started.add(i)

    def arrived(self, i, dst, to):
        self.copy(i, dst, dst, to).wait_recv()

    def drain(self, like, to):
        for i in sorted(self.started):
            self.copy(i, like, like, to).wait_send()


class Gather(Remote):
    def __init__(self, at, own, w, send_sem, recv_sem):
        super().__init__(send_sem, recv_sem)
        self.at, self.own, self.w = at, own, w

    def shard(self, j, aa=0, bb=0, plane=0):
        at = self.at
        a, b = (at.b, at.a) if plane else (at.a, at.b)
        return self.w.at[flipped(at.c, plane), flipped(a, aa), flipped(b, bb), (at.z + 4 - j) % 4]

    def source(self, j, aa=0, bb=0):
        return self.own if (j, aa, bb) == (0, 0, 0) else self.shard(j, aa, bb)

    def along_z(self):
        for k in (1, 3, 2):
            self.send(k - 1, self.own, self.shard(0), self.at.to_z(k))

    def along_b(self, j):
        self.send(3 + j, self.source(j), self.shard(j), self.at.to_b)

    def along_a(self, j, bb):
        self.send(7 + 4 * bb + j, self.source(j, 0, bb), self.shard(j, 0, bb), self.at.to_a)

    def across(self, j, aa, bb):
        self.send(15 + 8 * aa + 4 * bb + j, self.source(j, aa, bb), self.shard(j, aa, bb), self.at.to_other)

    def own_on(self):
        self.along_b(0)
        self.along_a(0, 0)
        self.across(0, 0, 0)

    def after_z(self):
        for j in (1, 3, 2):
            self.arrived(j - 1, self.shard(j), self.at.to_b)
            self.along_b(j)
            self.along_a(j, 0)
            self.across(j, 0, 0)

    def after_b(self):
        for j in (0, 1, 3, 2):
            self.arrived(3 + j, self.shard(j, 0, 1), self.at.to_b)
            self.along_a(j, 1)
            self.across(j, 0, 1)

    def after_a(self, bb):
        for j in (0, 1, 3, 2):
            self.arrived(7 + 4 * bb + j, self.shard(j, 1, bb), self.at.to_b)
            self.across(j, 1, bb)

    def after_across(self):
        for aa in range(2):
            for bb in range(2):
                for j in range(4):
                    self.arrived(15 + 8 * aa + 4 * bb + j, self.shard(j, aa, bb, 1), self.at.to_b)


class Reduce(Remote):
    def __init__(self, at, g, r0, r1, r2, r3, send_sem, recv_sem):
        super().__init__(send_sem, recv_sem)
        self.at, self.g, self.r0, self.r1, self.r2, self.r3 = at, g, r0, r1, r2, r3

    def across(self, t, lo, hi, base):
        @pl.when(self.at.c != t % 2)
        def _():
            for a, b in ((t // 2, 0), (t // 2, 1)) if t % 2 == 0 else ((0, t // 2), (1, t // 2)):
                self.copy(
                    base + 2 * a + b,
                    self.g.at[t % 2, a, b, :, :, lo:hi],
                    self.r0.at[a, b, :, :, lo:hi],
                    self.at.to_other,
                ).start()

    def across_wait(self, a, b, lo, hi, base):
        piece = self.r0.at[a, b, :, :, lo:hi]
        copy = self.copy(base + 2 * a + b, piece, piece, self.at.to_other)
        copy.wait_recv()

    def across_drain(self, lo, hi, base):
        for i in range(4):
            piece = self.r0.at[i // 2, i % 2, :, :, lo:hi]
            self.copy(base + i, piece, piece, self.at.to_other).wait_send()

    def far_half(self, parts):
        at = self.at
        for bb in (1, 0):
            b = flipped(at.b, bb)
            for lo, hi, base in parts:
                self.across_wait(1 - at.a, b, lo, hi, base)
            for j in range(4):
                z = (at.z + j) % 4
                here = self.g.at[at.c, 1 - at.a, b, z]
                here[...] = (here[...].astype(F32) + self.r0[1 - at.a, b, z].astype(F32)).astype(BF)
                self.send(8 + 4 * bb + j, here, self.r1.at[b, z], at.to_a)

    def near_half(self, parts):
        at = self.at
        b = 1 - at.b
        for lo, hi, base in parts:
            self.across_wait(at.a, b, lo, hi, base)
        for j in range(4):
            z = (at.z + j) % 4
            here = self.g.at[at.c, at.a, b, z]
            self.arrived(12 + j, self.r1.at[b, z], at.to_a)
            total = here[...].astype(F32) + self.r0[at.a, b, z].astype(F32) + self.r1[b, z].astype(F32)
            here[...] = total.astype(BF)
            self.send(16 + j, here, self.r2.at[z], at.to_b)

    def own_quarter(self, parts, out):
        at = self.at
        b = at.b
        for lo, hi, base in parts:
            self.across_wait(at.a, b, lo, hi, base)
        for j in (1, 3, 2, 0):
            z = (at.z + j) % 4
            here = self.g.at[at.c, at.a, b, z]
            self.arrived(8 + j, self.r1.at[b, z], at.to_a)
            self.arrived(16 + j, self.r2.at[z], at.to_b)
            total = here[...].astype(F32) + self.r0[at.a, b, z].astype(F32)
            total = total + self.r1[b, z].astype(F32) + self.r2[z].astype(F32)
            if j:
                here[...] = total.astype(BF)
                self.send(20 + j - 1, here, self.r3.at[j - 1], at.to_z(j))
            else:
                out[...] = total

    def finish(self, out):
        for k in (1, 3, 2):
            self.arrived(20 + k - 1, self.r3.at[k - 1], self.at.to_b)
        total = out[...] + self.r3[0].astype(F32)
        out[...] = total + self.r3[1].astype(F32) + self.r3[2].astype(F32)


def mixed(v, into):
    tiles = [v[:, 128 * i : 128 * i + 128] for i in range(4)]
    rolled = [pltpu.roll(tile, 64, 1) for tile in tiles]
    low = iota(tiles[0].shape, 1) < 64
    if into:
        pairs = ((0, 1, 0), (2, 3, 0), (0, 1, 1), (2, 3, 1))
    else:
        pairs = ((0, 2, 0), (0, 2, 1), (1, 3, 0), (1, 3, 1))
    out = []
    for i, k, high in pairs:
        out.append(jnp.where(low, rolled[i], tiles[k]) if high else jnp.where(low, tiles[i], rolled[k]))
    return jnp.concatenate(out, axis=1)


def layer_kernel(fast, tensors, names, *refs):
    ref = dict(zip(names, refs, strict=True))
    len_ref, x_ref, cot_ref, out_ref, ingrad_ref = (ref[n] for n in ("lengths", "x", "cot", "out", "ingrad"))
    qs, ks, vs, qb, kw, vw, wt, rdiv = (ref[n] for n in ("qs", "ks", "vs", "qb", "kw", "vw", "wt", "rdiv"))
    edge_l, edge_r, halo_l, halo_r, far = (ref[n] for n in ("edge_l", "edge_r", "halo_l", "halo_r", "far"))
    eb, ns, ml, ds_, att, mm = (ref[n] for n in ("eb", "ns", "ml", "ds", "att", "mm"))
    tmp_a, tmp_b, tmp_c, n1s, n2s, dacc = (ref[n] for n in ("tmp_a", "tmp_b", "tmp_c", "n1s", "n2s", "dacc"))
    us, mus, dqs, dkw = (ref[n] for n in ("us", "mus", "dqs", "dkw"))
    back_l, back_r, got_l, got_r, dfar, gfar = (
        ref[n] for n in ("back_l", "back_r", "got_l", "got_r", "dfar", "gfar")
    )
    send_sem, recv_sem, small_ref = ref["send_sem"], ref["recv_sem"], ref["small"]
    ga, gb = ref["ga"], ref["gb"]
    wa, wb = (ref["wa"], ref["wb"])

    def view(r, t, y):
        if not fast:
            return r.at[t, y]
        return r.at[0, t // 2, y] if t % 2 == 0 else r.at[1, y, t // 2]

    def get(r, t, y, lo, hi):
        return view(r, t, y)[..., lo:hi].reshape(256, hi - lo)

    def put(r, t, y, lo, hi, value):
        v = view(r, t, y)
        v[..., lo:hi] = value.astype(BF).reshape(*v.shape[:-1], hi - lo)

    me = lax.axis_index("tensor")
    valid_len = len_ref[0]
    barrier = pltpu.get_barrier_semaphore()
    if fast:
        at = Place()
        peers = [at.to_z(1), at.to_z(2), at.to_z(3), at.to_y, at.to_x, at.to_other, at.to_across]
    else:
        peers = [{"tensor": lax.rem(me + k, tensors)} for k in range(1, tensors)]
    for peer in peers:
        pl.semaphore_signal(barrier, inc=1, device_id=peer, device_id_type=MESH)
    pl.semaphore_wait(barrier, len(peers))
    if fast:
        first = Gather(at, ref["part_a"], wa, ref["gather_send"].at[0], ref["gather_recv"].at[0])
        second = Gather(at, ref["part_b"], wb, ref["gather_send"].at[1], ref["gather_recv"].at[1])
        first.along_z()
        first.own_on()
        wa[at.c, at.a, at.b, at.z] = ref["part_a"][...]
        wb[at.c, at.a, at.b, at.z] = ref["part_b"][...]

    lane = iota((64, 128), 1)
    low_lanes = lane < 64
    low_b = low_lanes.astype(F32).astype(BF)
    high_b = (1.0 - low_lanes.astype(F32)).astype(BF)

    def both(v):
        return jnp.concatenate([v * low_b, v * high_b], axis=0)

    def joined(v):
        return jnp.where(low_lanes, v[:64], v[64:])

    x = x_ref[...].astype(F32)
    cot = cot_ref[...].astype(F32)
    if fast:
        x, cot = mixed(x, True), mixed(cot, True)
    ref["xs"][...] = x
    ref["cots"][...] = cot
    n1, r1 = normalised(x)
    n1s[...] = n1
    n1b = n1.astype(BF)
    valid = (iota((ROWS, 128), 0) + me * ROWS < valid_len).astype(F32)
    rdiv[...] = row_divisors(me, tensors, valid_len)
    for k in range(TILES):
        wt[k] = tile_weights(k, me, tensors, valid_len)
    if fast:
        first.after_z()
        second.along_z()
        first.after_b()
        first.after_a(0)
        first.after_a(1)
        second.own_on()
        first.after_across()
    for t in range(PAIRS):
        joint = nn(n1b[:, :256], get(wa, t, 0, 0, 384)) + nn(n1b[:, 256:], get(wa, t, 1, 0, 384))
        joint = joint.astype(BF).astype(F32)
        qs[t, 0:ROWS, :] = joint[:, :128]
        ks[t, 0:ROWS, :] = joint[:, 128:256] * valid
        vs[t, 0:ROWS, :] = joint[:, 256:] * valid

    def pooling(p, carry):
        pool(qs.at[p])
        qs[p, 504:STACK, :] = jnp.zeros((8, 128), F32)
        qb[p] = (qs[p] * stack_factors()).astype(BF)
        for which, (raw, windows) in enumerate(((ks, kw), (vs, vw))):
            raw_p = raw.at[p]
            pool(raw_p)
            row = which * PAIRS + p
            for start, n in BLANK:
                windows[p, start : start + n, :] = jnp.zeros((n, 128), BF)
            for level in range(LEVELS - 1):
                n = COUNT[level]
                rows = slice(AT[level], AT[level] + n)
                coarse = (raw_p[rows, :] * rdiv[rows, :]).astype(BF)
                if level < 4:
                    windows[p, OWN[level] : OWN[level] + n, :] = coarse
                edge_l[row, 16 * level : 16 * level + 16, :] = coarse[:16]
                edge_r[row, 16 * level : 16 * level + 16, :] = coarse[n - 16 :]
            rows = slice(AT[5], AT[5] + 8)
            far[me, row] = raw_p[rows, :] * rdiv[rows, :]
        return carry

    lax.fori_loop(0, PAIRS, pooling, 0)

    def to_left(src, dst, sem):
        return pltpu.make_async_remote_copy(
            src, dst, send_sem.at[sem], recv_sem.at[sem], device_id={"tensor": jnp.maximum(me - 1, 0)}, device_id_type=MESH
        )

    def to_right(src, dst, sem):
        return pltpu.make_async_remote_copy(
            src,
            dst,
            send_sem.at[sem],
            recv_sem.at[sem],
            device_id={"tensor": jnp.minimum(me + 1, tensors - 1)},
            device_id_type=MESH,
        )

    def to_peer(k, src, dst, sem):
        return pltpu.make_async_remote_copy(
            src, dst, send_sem.at[sem], recv_sem.at[sem], device_id={"tensor": lax.rem(me + k, tensors)}, device_id_type=MESH
        )

    def exchange(base, left_src, left_dst, right_src, right_dst, far_src, far_dst):
        for k in range(1, tensors):
            to_peer(k, far_src(k), far_dst(k), base + 1 + k).start()

        @pl.when(me > 0)
        def _():
            to_left(left_src, left_dst, base).start()

        @pl.when(me < tensors - 1)
        def _():
            to_right(right_src, right_dst, base + 1).start()

    def exchanged(base, left_src, left_dst, right_src, right_dst, far_src, far_dst):
        @pl.when(me > 0)
        def _():
            to_left(left_src, left_dst, base).wait_send()
            to_right(right_src, right_dst, base + 1).wait_recv()

        @pl.when(me == 0)
        def _():
            right_dst[...] = jnp.zeros(right_dst.shape, BF)

        @pl.when(me < tensors - 1)
        def _():
            to_right(right_src, right_dst, base + 1).wait_send()
            to_left(left_src, left_dst, base).wait_recv()

        @pl.when(me == tensors - 1)
        def _():
            left_dst[...] = jnp.zeros(left_dst.shape, BF)

        for k in range(1, tensors):
            to_peer(k, far_src(k), far_dst(k), base + 1 + k).wait()

    halos = (0, edge_l, halo_r, edge_r, halo_l, lambda k: far.at[me], lambda k: far.at[me])
    exchange(*halos)
    if fast:
        second.after_z()
    exchanged(*halos)

    def attend(p, carry):
        for which, windows in enumerate((kw, vw)):
            row = which * PAIRS + p
            for level in range(LEVELS - 1):
                windows[p, LEFT[level] : LEFT[level] + 16, :] = halo_l[row, 16 * level : 16 * level + 16, :]
                windows[p, RIGHT[level] : RIGHT[level] + 16, :] = halo_r[row, 16 * level : 16 * level + 16, :]
            groups = jnp.concatenate([far[g, row] for g in range(tensors)], axis=0)
            windows[p, FAR:KEYS, :] = groups.astype(BF)
        for k in range(TILES):
            here = slice(64 * k, 64 * k + 64)
            keys = slice(TILE_AT[k], TILE_AT[k] + 128)
            s = nt(both(qb[p, here, :]), kw[p, keys, :])
            w = wt[k]
            w = jnp.concatenate([w, w], axis=0)
            s = jnp.where(w > 0.0, s, -1e30)
            m = jnp.max(s, axis=-1, keepdims=True)
            e = w * jnp.exp(s - m)
            low = e.astype(BF)
            total = jnp.sum(low.astype(F32), axis=-1, keepdims=True)
            eb[p, k] = low
            ns[here, :] = joined(nn(low, vw[p, keys, :]))
            ml[p, here, :] = joined(jnp.broadcast_to(m, (128, 128)))
            ds_[here, :] = joined(jnp.broadcast_to(total, (128, 128)))
        rows = slice(AT[5], AT[5] + 8)
        num, top, den = ns[rows, :], ml[p, rows, :], ds_[rows, :]
        for level in range(LEVELS - 2, -1, -1):
            n = COUNT[level]
            rows = slice(AT[level], AT[level] + n)
            num, top, den = doubled(tmp_a, num, n // 2), doubled(tmp_b, top, n // 2), doubled(tmp_c, den, n // 2)
            own = ml[p, rows, :]
            both_top = jnp.maximum(own, top)
            left, right = jnp.exp(own - both_top), jnp.exp(top - both_top)
            num = ns[rows, :] * left + num * right
            den = ds_[rows, :] * left + den * right
            top = both_top
        inverse = 1.0 / den
        att[p] = num * inverse
        mm[p] = top
        dacc[p] = inverse
        if fast:
            pl.when(p == 0)(second.after_b)
            pl.when(p == 1)(lambda: second.after_a(0))
            pl.when(p == 3)(lambda: second.after_a(1))
        return carry

    lax.fori_loop(0, PAIRS, attend, 0)

    if fast:
        second.after_across()
    attb = [att[t].astype(BF) for t in range(PAIRS)]
    branch = []
    for y in range(2):
        total = nt(attb[0], get(wb, 0, y, 0, 128))
        for t in range(1, PAIRS):
            total = total + nt(attb[t], get(wb, t, y, 0, 128))
        branch.append(total)
    branch = jnp.concatenate(branch, axis=1)
    middle = ref["xs"][...] + branch
    n2, r2 = normalised(middle)
    n2s[...] = n2
    n2b = n2.astype(BF)
    n2t = n2b.T
    cotb = ref["cots"][...].astype(BF)
    cott = cotb.T

    if fast:
        reduce_sems = lambda i: (ref["reduce_send"].at[i], ref["reduce_recv"].at[i])
        late = Reduce(at, gb, ref["b0"], ref["b1"], ref["b2"], ref["b3"], *reduce_sems(1))
        early = Reduce(at, ga, ref["a0"], ref["a1"], ref["a2"], ref["a3"], *reduce_sems(0))
        late_parts = ((128, 1152, 0), (0, 128, 4))
        early_parts = ((0, 384, 0),)
    dense, dn2 = [0.0, 0.0], [0.0, 0.0]
    for t in range(PAIRS):
        pre = nn(n2b[:, :256], get(wb, t, 0, 128, 640)) + nn(n2b[:, 256:], get(wb, t, 1, 128, 640))
        act, slope = gelu_both(pre)
        act = act.astype(BF)
        act_grad = nn(cotb[:, :256], get(wb, t, 0, 640, 1152)) + nn(cotb[:, 256:], get(wb, t, 1, 640, 1152))
        pre_grad = (act_grad * slope).astype(BF)
        for y in range(2):
            half = slice(256 * y, 256 * y + 256)
            dense[y] = dense[y] + nt(act, get(wb, t, y, 640, 1152))
            dn2[y] = dn2[y] + nt(pre_grad, get(wb, t, y, 128, 640))
            put(gb, t, y, 128, 640, nn(n2t[half, :], pre_grad))
            put(gb, t, y, 640, 1152, nn(cott[half, :], act))
        if fast:
            late.across(t, 128, 1152, 0)
    dense = jnp.concatenate(dense, axis=1)
    dn2 = jnp.concatenate(dn2, axis=1)
    result = middle + dense
    out_ref[...] = (mixed(result, False) if fast else result).astype(BF)
    live = (iota((ROWS, 512), 0) + me * ROWS < valid_len).astype(F32)
    small_ref[2:3, :] = jnp.sum(live * result * result, axis=0, keepdims=True)
    small_ref[3:4, :] = jnp.sum(live * branch * branch, axis=0, keepdims=True)
    small_ref[4:5, :] = jnp.sum(live * dense * dense, axis=0, keepdims=True)
    small_ref[5:6, :] = jnp.sum(live, axis=0, keepdims=True)
    small_ref[6:8, :] = jnp.zeros((2, 512), F32)
    n2 = n2s[...]
    small_ref[1:2, :] = jnp.sum(dn2 * n2, axis=0, keepdims=True)
    middle_grad = ref["cots"][...] + norm_back(n2, r2, dn2)
    n2s[...] = middle_grad
    mgb = middle_grad.astype(BF)
    mgt = mgb.T
    for t in range(PAIRS):
        us[t, 0:ROWS, :] = nn(mgb[:, :256], get(wb, t, 0, 0, 128)) + nn(mgb[:, 256:], get(wb, t, 1, 0, 128))
        for y in range(2):
            put(gb, t, y, 0, 128, nn(mgt[256 * y : 256 * y + 256, :], att[t].astype(BF)))
        if fast:
            late.across(t, 0, 128, 4)

    def head_sums(v):
        first = jnp.sum(jnp.where(iota(v.shape, 1) < 64, v, 0.0), axis=-1, keepdims=True)
        second = jnp.sum(jnp.where(iota(v.shape, 1) < 64, 0.0, v), axis=-1, keepdims=True)
        return jnp.where(iota(v.shape, 1) < 64, first, second)

    def attend_back(p, carry):
        up = us.at[p]
        grad, inverse = up[0:ROWS, :], dacc[p]
        delta = head_sums(grad * att[p])
        up[0:ROWS, :] = grad * inverse
        ns[0:ROWS, :] = delta * inverse
        mus[0:ROWS, :] = mm[p]
        for level in range(LEVELS - 1):
            n = COUNT[level + 1]
            after = slice(AT[level + 1], AT[level + 1] + n)
            top_e, top_o = pairs_of(mus, AT[level], n)
            top = jnp.minimum(top_e, top_o)
            fe, fo = jnp.exp(top - top_e), jnp.exp(top - top_o)
            u_e, u_o = pairs_of(up, AT[level], n)
            d_e, d_o = pairs_of(ns, AT[level], n)
            up[after, :] = u_e * fe + u_o * fo
            ns[after, :] = d_e * fe + d_o * fo
            mus[after, :] = top
        for rows in (slice(504, STACK),):
            up[rows, :] = jnp.zeros((8, 128), F32)
            ns[rows, :] = jnp.zeros((8, 128), F32)
            mus[rows, :] = jnp.zeros((8, 128), F32)
        for which in range(2):
            dkw[which * PAIRS + p, 0:512, :] = jnp.zeros((512, 128), F32)
        for k in range(TILES):
            here = slice(64 * k, 64 * k + 64)
            keys = slice(TILE_AT[k], TILE_AT[k] + 128)
            factor = jnp.exp(ml[p, here, :] - mus[here, :])
            g = up[here, :] * factor
            g_high = g.astype(BF)
            g2 = both(g_high)
            g4 = jnp.concatenate([g2, both((g - g_high.astype(F32)).astype(BF))], axis=1)
            v2 = vw[p, keys, :]
            v2 = jnp.concatenate([v2, v2], axis=1)
            h = ns[here, :] * factor
            h2 = jnp.concatenate([h[:, 0:1], h[:, 64:65]], axis=0)
            q2 = both(qb[p, here, :])
            low = eb[p, k]
            d = low.astype(F32) * (nt(g4, v2) - h2)
            d = d.astype(BF)
            dv = tn(low, g2)
            dk = tn(d, q2)
            if k < 6:
                dkw[p, keys, :] = dkw[p, keys, :] + dk
                dkw[PAIRS + p, keys, :] = dkw[PAIRS + p, keys, :] + dv
            else:
                dkw[p, keys, :] = dk
                dkw[PAIRS + p, keys, :] = dv
            dqs[p, here, :] = joined(nn(d, kw[p, keys, :]))
        for which in range(2):
            row = which * PAIRS + p
            for level in range(LEVELS - 1):
                part = slice(16 * level, 16 * level + 16)
                back_l[row, part, :] = dkw[row, LEFT[level] : LEFT[level] + 16, :].astype(BF)
                back_r[row, part, :] = dkw[row, RIGHT[level] : RIGHT[level] + 16, :].astype(BF)
            for g in range(tensors):
                dfar[g, row] = dkw[row, FAR + 8 * g : FAR + 8 * g + 8, :]
        if fast:
            pl.when(p == 0)(lambda: late.far_half(late_parts))
            pl.when(p == 2)(lambda: late.near_half(late_parts))
        return carry

    lax.fori_loop(0, PAIRS, attend_back, 0)

    back = (
        8,
        back_l,
        got_r,
        back_r,
        got_l,
        lambda k: dfar.at[lax.rem(me + k, tensors)],
        lambda k: gfar.at[k],
    )
    exchange(*back)
    if fast:
        late.own_quarter(late_parts, ref["out_b"])
    exchanged(*back)

    def unpool(p, carry):
        factors = stack_factors()
        cur = dqs[p, AT[5] : AT[5] + 8, :] * factors[AT[5] : AT[5] + 8]
        for level in range(LEVELS - 2, -1, -1):
            rows = slice(AT[level], AT[level] + COUNT[level])
            cur = doubled(tmp_a, cur, COUNT[level] // 2) + dqs[p, rows, :] * factors[rows]
        qs[p, 0:ROWS, :] = cur
        for which, raw in enumerate((ks, vs)):
            row = which * PAIRS + p
            raw_p = raw.at[p]
            cur = gfar[1, row]
            for k in range(2, tensors):
                cur = cur + gfar[k, row]
            cur = cur * rdiv[AT[5] : AT[5] + 8, :]
            for level in range(LEVELS - 2, -1, -1):
                n = COUNT[level]
                rows = slice(AT[level], AT[level] + n)
                part = slice(16 * level, 16 * level + 16)
                if level < 4:
                    raw_p[rows, :] = dkw[row, OWN[level] : OWN[level] + n, :]
                else:
                    raw_p[rows, :] = jnp.zeros((n, 128), F32)
                first = slice(AT[level], AT[level] + 16)
                last = slice(AT[level] + n - 16, AT[level] + n)
                raw_p[first, :] = raw_p[first, :] + got_l[row, part, :].astype(F32)
                raw_p[last, :] = raw_p[last, :] + got_r[row, part, :].astype(F32)
                cur = doubled(tmp_a, cur, n // 2) + raw_p[rows, :] * rdiv[rows, :]
            raw_p[0:ROWS, :] = cur * (iota((ROWS, 128), 0) + me * ROWS < valid_len).astype(F32)
        return carry

    lax.fori_loop(0, PAIRS, unpool, 0)

    n1 = n1s[...]
    n1t = n1.astype(BF).T
    dn1 = [0.0, 0.0]
    for t in range(PAIRS):
        joint = jnp.concatenate(
            [qs[t, 0:ROWS, :].astype(BF), ks[t, 0:ROWS, :].astype(BF), vs[t, 0:ROWS, :].astype(BF)], axis=1
        )
        for y in range(2):
            put(ga, t, y, 0, 384, nn(n1t[256 * y : 256 * y + 256, :], joint))
            dn1[y] = dn1[y] + nt(joint, get(wa, t, y, 0, 384))
        if fast:
            early.across(t, 0, 384, 0)
    dn1 = jnp.concatenate(dn1, axis=1)
    small_ref[0:1, :] = jnp.sum(dn1 * n1, axis=0, keepdims=True)
    if fast:
        sums = Remote(ref["sum_send"], ref["sum_recv"])
        got = ref["sums"]
        for i, to in enumerate((at.to_other, at.to_x, at.to_y)):
            if i == 1:
                early.far_half(early_parts)
            if i == 2:
                early.near_half(early_parts)
            got[2 * i] = small_ref[...]
            sums.send(i, got.at[2 * i], got.at[2 * i + 1], to)
            sums.arrived(i, got.at[2 * i + 1], to)
            small_ref[...] = got[2 * i] + got[2 * i + 1]
        got[6 + at.z] = small_ref[...]
        for k in range(1, 4):
            sums.send(2 + k, got.at[6 + at.z], got.at[6 + at.z], at.to_z(k))
        early.own_quarter(early_parts, ref["out_a"])
    r1 = lax.rsqrt(row_variance(ref["xs"][...]) + EPS)
    in_grad = n2s[...] + norm_back(n1, r1, dn1)
    ingrad_ref[...] = (mixed(in_grad, False) if fast else in_grad).astype(BF)
    if fast:
        late.finish(ref["out_b"])
        early.finish(ref["out_a"])
        for k in range(1, 4):
            sums.arrived(2 + k, got.at[6], at.to_b)
        small_ref[...] = ((got[6] + got[7]) + got[8]) + got[9]
        late.across_drain(128, 1152, 0)
        late.across_drain(0, 128, 4)
        early.across_drain(0, 384, 0)
        first.drain(ref["part_a"], at.to_x)
        second.drain(ref["part_b"], at.to_x)
        late.drain(late.r2.at[0], at.to_x)
        early.drain(early.r2.at[0], at.to_x)
        sums.drain(small_ref, at.to_x)


def row_variance(v):
    centred = v - jnp.mean(v, axis=-1, keepdims=True)
    return jnp.mean(centred * centred, axis=-1, keepdims=True)


def run_layer(fast, tensors, lengths, inputs, cotangent, wa, wb):
    vmem = pl.BlockSpec(memory_space=pltpu.VMEM)
    f = lambda *shape: pltpu.VMEM(shape, F32)
    b = lambda *shape: pltpu.VMEM(shape, BF)
    full = (2, 2, 2, 4, 64) if fast else (tensors, 2, 256)
    ca, cb = wa.shape[-1], wb.shape[-1]
    outs = {"out": ((ROWS, 512), BF), "ingrad": ((ROWS, 512), BF), "small": ((8, 512), F32)}
    scratch = {
        "qs": f(PAIRS, STACK, 128),
        "ks": f(PAIRS, STACK, 128),
        "vs": f(PAIRS, STACK, 128),
        "qb": b(PAIRS, STACK, 128),
        "kw": b(PAIRS, KEYS, 128),
        "vw": b(PAIRS, KEYS, 128),
        "wt": f(TILES, 64, 128),
        "rdiv": f(STACK, 128),
        "edge_l": b(2 * PAIRS, HALO, 128),
        "edge_r": b(2 * PAIRS, HALO, 128),
        "halo_l": b(2 * PAIRS, HALO, 128),
        "halo_r": b(2 * PAIRS, HALO, 128),
        "far": f(tensors, 2 * PAIRS, 8, 128),
        "eb": b(PAIRS, TILES, 128, 128),
        "ns": f(STACK, 128),
        "ml": f(PAIRS, STACK, 128),
        "ds": f(STACK, 128),
        "att": f(PAIRS, ROWS, 128),
        "mm": f(PAIRS, ROWS, 128),
        "tmp_a": f(ROWS, 128),
        "tmp_b": f(ROWS, 128),
        "tmp_c": f(ROWS, 128),
        "xs": f(ROWS, 512),
        "cots": f(ROWS, 512),
        "n1s": f(ROWS, 512),
        "n2s": f(ROWS, 512),
        "dacc": f(PAIRS, ROWS, 128),
        "us": f(PAIRS, STACK, 128),
        "mus": f(STACK, 128),
        "dqs": f(PAIRS, STACK, 128),
        "dkw": f(2 * PAIRS, KEYS, 128),
        "back_l": b(2 * PAIRS, HALO, 128),
        "back_r": b(2 * PAIRS, HALO, 128),
        "got_l": b(2 * PAIRS, HALO, 128),
        "got_r": b(2 * PAIRS, HALO, 128),
        "dfar": f(tensors, 2 * PAIRS, 8, 128),
        "gfar": f(tensors, 2 * PAIRS, 8, 128),
        "send_sem": pltpu.SemaphoreType.DMA((16,)),
        "recv_sem": pltpu.SemaphoreType.DMA((16,)),
    }
    if fast:
        ins = ("lengths", "x", "cot", "part_a", "part_b")
        outs |= {"out_a": ((64, ca), F32), "out_b": ((64, cb), F32)}
        for name, c in (("a", ca), ("b", cb)):
            scratch |= {
                "w" + name: b(*full, c),
                "g" + name: b(*full, c),
                name + "0": b(2, 2, 4, 64, c),
                name + "1": b(2, 4, 64, c),
                name + "2": b(4, 64, c),
                name + "3": b(3, 64, c),
            }
        scratch |= {
            "sums": f(10, 8, 512),
            "gather_send": pltpu.SemaphoreType.DMA((2, 31)),
            "gather_recv": pltpu.SemaphoreType.DMA((2, 31)),
            "reduce_send": pltpu.SemaphoreType.DMA((2, 23)),
            "reduce_recv": pltpu.SemaphoreType.DMA((2, 23)),
            "sum_send": pltpu.SemaphoreType.DMA((6,)),
            "sum_recv": pltpu.SemaphoreType.DMA((6,)),
        }
    else:
        ins = ("lengths", "x", "cot", "wa", "wb")
        outs |= {"ga": (wa.shape, BF), "gb": (wb.shape, BF)}
    return pl.pallas_call(
        functools.partial(layer_kernel, fast, tensors, (*ins, *outs, *scratch)),
        out_shape=tuple(jax.ShapeDtypeStruct(*shape) for shape in outs.values()),
        in_specs=[pl.BlockSpec(memory_space=pltpu.SMEM)] + [vmem] * 4,
        out_specs=(vmem,) * 5,
        scratch_shapes=list(scratch.values()),
        compiler_params=pltpu.CompilerParams(
            collective_id=0, has_side_effects=True, vmem_limit_bytes=62 * 1024 * 1024
        ),
        name="layer",
    )(lengths, inputs, cotangent, wa, wb)


def per_device(
    fast,
    inputs,
    lengths,
    cotangent,
    query_weight,
    key_weight,
    value_weight,
    output_weight,
    inner_weight,
    outer_weight,
    first_gain,
    second_gain,
):
    tensors, groups = lax.axis_size("tensor"), lax.axis_size("dp")
    everyone = ("tensor", "dp")
    g1 = first_gain.astype(F32)[:, None]
    g2 = second_gain.astype(F32)[:, None]
    scaled = lambda g, w: (g * w.astype(F32)).astype(BF)
    part_a = scaled(g1, jnp.concatenate([query_weight, key_weight, value_weight], axis=1))
    part_b = jnp.concatenate([output_weight.T, scaled(g2, inner_weight), outer_weight.T], axis=1)
    width, group = first_gain.shape[0], lax.axis_index("dp")
    if fast:
        out, input_grad, small, ga, gb = run_layer(fast, tensors, lengths, inputs, cotangent, part_a, part_b)
        at = (group % 2) * 256 + (group // 2) * 64
    else:
        wa = lax.all_gather(part_a, everyone, axis=0, tiled=True).reshape(tensors, 2, 256, 384)
        wb = lax.all_gather(part_b, everyone, axis=0, tiled=True).reshape(tensors, 2, 256, 1152)
        out, input_grad, small, ga, gb = run_layer(fast, tensors, lengths, inputs, cotangent, wa, wb)

        def reduced(g):
            return lax.psum_scatter(
                g.reshape(tensors * 512, g.shape[-1]).astype(F32), everyone, scatter_dimension=0, tiled=True
            )

        ga, gb, small = reduced(ga), reduced(gb), lax.psum(small, everyone)
        at = group * width
    gains = lax.dynamic_slice(small, (0, at), (2, width))
    sums = jnp.sum(small, axis=1)
    root_mean_squares = jnp.sqrt(sums[2:5] / sums[5])
    ga = ga * g1
    return (
        out,
        input_grad,
        ga[:, 0:128],
        ga[:, 128:256],
        ga[:, 256:384],
        gb[:, 0:128].T,
        gb[:, 128:640] * g2,
        gb[:, 640:1152].T,
        gains[0] / first_gain.astype(F32),
        gains[1] / second_gain.astype(F32),
        root_mean_squares,
    )


def solution(mesh):
    fast = (mesh.shape["dp"], mesh.shape["tensor"]) == (8, 4)
    return jax.shard_map(
        functools.partial(per_device, fast),
        mesh=mesh,
        in_specs=(
            P(("dp", "tensor"), None),
            P("dp"),
            P(("dp", "tensor"), None),
            P("dp", "tensor"),
            P("dp", "tensor"),
            P("dp", "tensor"),
            P("tensor", "dp"),
            P("dp", "tensor"),
            P("tensor", "dp"),
            P("dp"),
            P("dp"),
        ),
        out_specs=(
            P(("dp", "tensor"), None),
            P(("dp", "tensor"), None),
            P("dp", "tensor"),
            P("dp", "tensor"),
            P("dp", "tensor"),
            P("tensor", "dp"),
            P("dp", "tensor"),
            P("tensor", "dp"),
            P("dp"),
            P("dp"),
            P(),
        ),
        check_vma=False,
    )
```

```python
import functools

import jax
import jax.numpy as jnp
from jax import lax
from jax.experimental import pallas as pl
from jax.experimental.pallas import tpu as pltpu
from jax.sharding import PartitionSpec as P

MESH = pl.DeviceIdType.MESH
F32, BF = jnp.float32, jnp.bfloat16
HEAD_DIM = 64
EPS = 1e-05

ROWS, PAIRS, LEVELS = 256, 4, 6
COUNT = (256, 128, 64, 32, 16, 8)
AT = (0, 256, 384, 448, 480, 496)
STACK = 512
OWN = (32, 352, 544, 656)
LEFT = (16, 336, 528, 640, 704)
RIGHT = (288, 480, 608, 688, 720)
FAR = 736
KEYS = 768
BLANK = ((0, 16), (304, 32), (496, 32), (624, 16))
TILE_AT = (0, 64, 128, 192, 320, 384, 512, 640)
TILES = 8
HALO = 80


def nn(a, b):
    return lax.dot_general(a, b, (((1,), (0,)), ((), ())), preferred_element_type=F32)


def nt(a, b):
    return lax.dot_general(a, b, (((1,), (1,)), ((), ())), preferred_element_type=F32)


def tn(a, b):
    return lax.dot_general(a, b, (((0,), (0,)), ((), ())), preferred_element_type=F32)


def iota(shape, dim):
    return lax.broadcasted_iota(jnp.int32, shape, dim)


def level_counts(index, level, total, valid_len):
    factor = 1 << level
    c = jnp.clip(valid_len - index * factor, 0, factor)
    return jnp.where((index >= 0) & (index < total), c, 0).astype(F32)


def tile_weights(k, me, tensors, valid_len):
    i, j = iota((64, 128), 0), iota((64, 128), 1)
    if k < 7:
        level = 0 if k < 4 else 1 if k < 6 else 2
        first = 64 * (k - AT[level] // 64)
        n = COUNT[level]
        c = level_counts(me * n + first - 32 + j, level, n * tensors, valid_len)
        near = jnp.abs((i >> 4) - (j >> 4) + 2) <= 1
        if level:
            near = near & (jnp.abs((i >> 3) - (j >> 3) + 4) > 1)
        return jnp.where(near, c, 0.0)
    c3 = level_counts(me * 32 + j - 16, 3, 32 * tensors, valid_len)
    near3 = (jnp.abs((i >> 4) - (j >> 4) + 1) <= 1) & (jnp.abs((i >> 3) - (j >> 3) + 2) > 1)
    near3 = near3 & (i < 32) & (j < 64)
    key4 = jnp.where(j < 80, j - 80, j - 64)
    c4 = level_counts(me * 16 + key4, 4, 16 * tensors, valid_len)
    near4 = (jnp.abs(((i - 32) >> 3) - (key4 >> 3)) > 1) & (i >= 32) & (i < 48) & (j >= 64) & (j < 96)
    key5 = j - 96
    c5 = level_counts(key5, 5, 8 * tensors, valid_len)
    near5 = (jnp.abs(me - (key5 >> 3)) > 1) & (i >= 48) & (i < 56) & (j >= 96)
    return jnp.where(near3, c3, 0.0) + jnp.where(near4, c4, 0.0) + jnp.where(near5, c5, 0.0)


def row_divisors(me, tensors, valid_len):
    i = iota((STACK, 128), 0)
    out = jnp.ones((STACK, 128), F32)
    for level in range(1, LEVELS):
        c = level_counts(i - AT[level] + me * COUNT[level], level, COUNT[level] * tensors, valid_len)
        here = (i >= AT[level]) & (i < AT[level] + COUNT[level])
        out = jnp.where(here, 1.0 / jnp.maximum(c, 1.0), out)
    return out


def stack_factors():
    i = iota((STACK, 128), 0)
    out = jnp.full((STACK, 128), HEAD_DIM ** (-0.5), F32)
    for level in range(1, LEVELS):
        out = jnp.where(i >= AT[level], HEAD_DIM ** (-0.5) / (1 << level), out)
    return out


def pairs_of(ref, start, n):
    return ref[pl.ds(start, n, stride=2), :], ref[pl.ds(start + 1, n, stride=2), :]


def pool(ref):
    for level in range(LEVELS - 1):
        n = COUNT[level + 1]
        even, odd = pairs_of(ref, AT[level], n)
        ref[AT[level + 1] : AT[level + 1] + n, :] = even + odd


def doubled(ref, value, n):
    ref[pl.ds(0, n, stride=2), :] = value
    ref[pl.ds(1, n, stride=2), :] = value
    return ref[0 : 2 * n, :]


def normalised(v):
    centred = v - jnp.mean(v, axis=-1, keepdims=True)
    r = lax.rsqrt(jnp.mean(centred * centred, axis=-1, keepdims=True) + EPS)
    return centred * r, r


def norm_back(n, r, hg):
    return r * (hg - jnp.mean(hg, axis=-1, keepdims=True) - n * jnp.mean(hg * n, axis=-1, keepdims=True))


def gelu_both(u):
    c = 0.7978845608028654
    square = u * u
    th = jnp.tanh(c * (u + 0.044715 * (square * u)))
    half = 0.5 * (1.0 + th)
    slope = half + (0.5 * c) * u * (1.0 - th * th) * (1.0 + 0.134145 * square)
    return u * half, slope


class Place:
    def __init__(self):
        self.d, self.t = lax.axis_index("dp"), lax.axis_index("tensor")
        self.z, self.y = self.d // 2, self.d % 2
        self.x, self.c = self.t // 2, self.t % 2
        self.a = self.x + self.c * (self.y - self.x)
        self.b = self.y + self.c * (self.x - self.y)
        flip_x, flip_y = 2 - 4 * self.x, 1 - 2 * self.y
        self.to_x, self.to_y = (self.d, self.t + flip_x), (self.d + flip_y, self.t)
        self.to_a = (self.d + self.c * flip_y, self.t + (1 - self.c) * flip_x)
        self.to_b = (self.d + (1 - self.c) * flip_y, self.t + self.c * flip_x)
        self.to_other = (self.d, self.t + 1 - 2 * self.c)
        self.to_across = (self.d, 3 - self.t)

    def to_z(self, k):
        return (2 * ((self.z + k) % 4) + self.y, self.t)


def flipped(bit, by):
    return 1 - bit if by else bit


class Remote:
    def __init__(self, send_sem, recv_sem):
        self.send_sem, self.recv_sem, self.started = send_sem, recv_sem, set()

    def copy(self, i, src, dst, to):
        return pltpu.make_async_remote_copy(
            src, dst, self.send_sem.at[i], self.recv_sem.at[i], device_id=to, device_id_type=MESH
        )

    def send(self, i, src, dst, to):
        self.copy(i, src, dst, to).start()
        self.started.add(i)

    def arrived(self, i, dst, to):
        self.copy(i, dst, dst, to).wait_recv()

    def drain(self, like, to):
        for i in sorted(self.started):
            self.copy(i, like, like, to).wait_send()


class Gather(Remote):
    def __init__(self, at, own, w, send_sem, recv_sem):
        super().__init__(send_sem, recv_sem)
        self.at, self.own, self.w = at, own, w

    def shard(self, j, aa=0, bb=0, plane=0):
        at = self.at
        a, b = (at.b, at.a) if plane else (at.a, at.b)
        return self.w.at[flipped(at.c, plane), flipped(a, aa), flipped(b, bb), (at.z + 4 - j) % 4]

    def source(self, j, aa=0, bb=0):
        return self.own if (j, aa, bb) == (0, 0, 0) else self.shard(j, aa, bb)

    def along_z(self):
        for k in (1, 3, 2):
            self.send(k - 1, self.own, self.shard(0), self.at.to_z(k))

    def along_b(self, j):
        self.send(3 + j, self.source(j), self.shard(j), self.at.to_b)

    def along_a(self, j, bb):
        self.send(7 + 4 * bb + j, self.source(j, 0, bb), self.shard(j, 0, bb), self.at.to_a)

    def across(self, j, aa, bb):
        self.send(15 + 8 * aa + 4 * bb + j, self.source(j, aa, bb), self.shard(j, aa, bb), self.at.to_other)

    def own_on(self):
        self.along_b(0)
        self.along_a(0, 0)
        self.across(0, 0, 0)

    def after_z(self, *js):
        for j in js:
            self.arrived(j - 1, self.shard(j), self.at.to_b)
            self.along_b(j)
            self.along_a(j, 0)
            self.across(j, 0, 0)

    def after_b(self, *js):
        for j in js:
            self.arrived(3 + j, self.shard(j, 0, 1), self.at.to_b)
            self.along_a(j, 1)
            self.across(j, 0, 1)

    def after_a(self, bb, *js):
        for j in js:
            self.arrived(7 + 4 * bb + j, self.shard(j, 1, bb), self.at.to_b)
            self.across(j, 1, bb)

    def after_across(self):
        for aa in range(2):
            for bb in range(2):
                for j in range(4):
                    self.arrived(15 + 8 * aa + 4 * bb + j, self.shard(j, aa, bb, 1), self.at.to_b)


class Reduce(Remote):
    def __init__(self, at, g, r0, r1, r2, r3, send_sem, recv_sem):
        super().__init__(send_sem, recv_sem)
        self.at, self.g, self.r0, self.r1, self.r2, self.r3 = at, g, r0, r1, r2, r3

    def across(self, t, lo, hi, base):
        @pl.when(self.at.c != t % 2)
        def _():
            for a, b in ((t // 2, 0), (t // 2, 1)) if t % 2 == 0 else ((0, t // 2), (1, t // 2)):
                self.copy(
                    base + 2 * a + b,
                    self.g.at[t % 2, a, b, :, :, lo:hi],
                    self.r0.at[a, b, :, :, lo:hi],
                    self.at.to_other,
                ).start()

    def across_wait(self, a, b, lo, hi, base):
        piece = self.r0.at[a, b, :, :, lo:hi]
        copy = self.copy(base + 2 * a + b, piece, piece, self.at.to_other)
        copy.wait_recv()

    def across_drain(self, lo, hi, base):
        for i in range(4):
            piece = self.r0.at[i // 2, i % 2, :, :, lo:hi]
            self.copy(base + i, piece, piece, self.at.to_other).wait_send()

    def across_all(self, parts):
        for a in range(2):
            for b in range(2):
                for lo, hi, base in parts:
                    self.across_wait(a, b, lo, hi, base)

    def far(self, *js):
        at = self.at
        for j in js:
            z = (at.z + j) % 4
            for bb in (1, 0):
                b = flipped(at.b, bb)
                here = self.g.at[at.c, 1 - at.a, b, z]
                here[...] = (here[...].astype(F32) + self.r0[1 - at.a, b, z].astype(F32)).astype(BF)
                self.send(8 + 4 * bb + j, here, self.r1.at[b, z], at.to_a)

    def near(self, *js):
        at = self.at
        b = 1 - at.b
        for j in js:
            z = (at.z + j) % 4
            here = self.g.at[at.c, at.a, b, z]
            self.arrived(12 + j, self.r1.at[b, z], at.to_a)
            total = here[...].astype(F32) + self.r0[at.a, b, z].astype(F32) + self.r1[b, z].astype(F32)
            here[...] = total.astype(BF)
            self.send(16 + j, here, self.r2.at[z], at.to_b)

    def own(self, out, *js):
        at = self.at
        b = at.b
        for j in js:
            z = (at.z + j) % 4
            here = self.g.at[at.c, at.a, b, z]
            self.arrived(8 + j, self.r1.at[b, z], at.to_a)
            self.arrived(16 + j, self.r2.at[z], at.to_b)
            total = here[...].astype(F32) + self.r0[at.a, b, z].astype(F32)
            total = total + self.r1[b, z].astype(F32) + self.r2[z].astype(F32)
            if j:
                here[...] = total.astype(BF)
                self.send(20 + j - 1, here, self.r3.at[j - 1], at.to_z(j))
            else:
                out[...] = total

    def finish(self, out):
        for k in (1, 3, 2):
            self.arrived(20 + k - 1, self.r3.at[k - 1], self.at.to_b)
        total = out[...] + self.r3[0].astype(F32)
        out[...] = total + self.r3[1].astype(F32) + self.r3[2].astype(F32)


def mixed(v, into):
    tiles = [v[:, 128 * i : 128 * i + 128] for i in range(4)]
    rolled = [pltpu.roll(tile, 64, 1) for tile in tiles]
    low = iota(tiles[0].shape, 1) < 64
    if into:
        pairs = ((0, 1, 0), (2, 3, 0), (0, 1, 1), (2, 3, 1))
    else:
        pairs = ((0, 2, 0), (0, 2, 1), (1, 3, 0), (1, 3, 1))
    out = []
    for i, k, high in pairs:
        out.append(jnp.where(low, rolled[i], tiles[k]) if high else jnp.where(low, tiles[i], rolled[k]))
    return jnp.concatenate(out, axis=1)


def layer_kernel(fast, tensors, names, *refs):
    ref = dict(zip(names, refs, strict=True))
    len_ref, x_ref, cot_ref, out_ref, ingrad_ref = (ref[n] for n in ("lengths", "x", "cot", "out", "ingrad"))
    qs, ks, vs, qb, kw, vw, wt, rdiv = (ref[n] for n in ("qs", "ks", "vs", "qb", "kw", "vw", "wt", "rdiv"))
    edge_l, edge_r, halo_l, halo_r, far = (ref[n] for n in ("edge_l", "edge_r", "halo_l", "halo_r", "far"))
    eb, ns, ml, ds_, att, mm = (ref[n] for n in ("eb", "ns", "ml", "ds", "att", "mm"))
    tmp_a, tmp_b, tmp_c, n1s, n2s, dacc = (ref[n] for n in ("tmp_a", "tmp_b", "tmp_c", "n1s", "n2s", "dacc"))
    us, mus, dqs, dkw = (ref[n] for n in ("us", "mus", "dqs", "dkw"))
    back_l, back_r, got_l, got_r, dfar, gfar = (
        ref[n] for n in ("back_l", "back_r", "got_l", "got_r", "dfar", "gfar")
    )
    send_sem, recv_sem, small_ref = ref["send_sem"], ref["recv_sem"], ref["small"]
    ga, gm, gl = ref["ga"], ref["gm"], ref["gl"]
    wa, wm, wl = ref["wa"], ref["wm"], ref["wl"]

    def view(r, t, y):
        if not fast:
            return r.at[t, y]
        return r.at[0, t // 2, y] if t % 2 == 0 else r.at[1, y, t // 2]

    def get(r, t, y, lo, hi):
        return view(r, t, y)[..., lo:hi].reshape(256, hi - lo)

    def put(r, t, y, lo, hi, value):
        v = view(r, t, y)
        v[..., lo:hi] = value.astype(BF).reshape(*v.shape[:-1], hi - lo)

    me = lax.axis_index("tensor")
    valid_len = len_ref[0]
    barrier = pltpu.get_barrier_semaphore()
    if fast:
        at = Place()
        peers = [at.to_z(1), at.to_z(2), at.to_z(3), at.to_y, at.to_x, at.to_other, at.to_across]
    else:
        peers = [{"tensor": lax.rem(me + k, tensors)} for k in range(1, tensors)]
    for peer in peers:
        pl.semaphore_signal(barrier, inc=1, device_id=peer, device_id_type=MESH)
    pl.semaphore_wait(barrier, len(peers))
    if fast:
        first, second, third = (
            Gather(at, ref["part_" + n], ref["w" + n], ref["gather_send"].at[i], ref["gather_recv"].at[i])
            for i, n in enumerate("aml")
        )
        early, middle_sum, late = (
            Reduce(
                at,
                ref["g" + n],
                *(ref[n + str(k)] for k in range(4)),
                ref["reduce_send"].at[i],
                ref["reduce_recv"].at[i],
            )
            for i, n in enumerate("aml")
        )
        early_parts, middle_parts, late_parts = ((0, 384, 0),), ((128, 640, 0), (0, 128, 4)), ((0, 512, 0),)
        first.along_z()
        first.own_on()
        second.own_on()
        for n in "aml":
            ref["w" + n][at.c, at.a, at.b, at.z] = ref["part_" + n][...]

    lane = iota((64, 128), 1)
    low_lanes = lane < 64
    low_b = low_lanes.astype(F32).astype(BF)
    high_b = (1.0 - low_lanes.astype(F32)).astype(BF)

    def both(v):
        return jnp.concatenate([v * low_b, v * high_b], axis=0)

    def joined(v):
        return jnp.where(low_lanes, v[:64], v[64:])

    x = x_ref[...].astype(F32)
    cot = cot_ref[...].astype(F32)
    if fast:
        x, cot = mixed(x, True), mixed(cot, True)
    ref["xs"][...] = x
    ref["cots"][...] = cot
    n1, r1 = normalised(x)
    n1s[...] = n1
    n1b = n1.astype(BF)
    valid = (iota((ROWS, 128), 0) + me * ROWS < valid_len).astype(F32)
    rdiv[...] = row_divisors(me, tensors, valid_len)
    for k in range(TILES):
        wt[k] = tile_weights(k, me, tensors, valid_len)
    if fast:
        first.after_z(1, 3, 2)
        second.along_z()
        first.after_b(0, 1, 3, 2)
        second.after_b(0)
        first.after_a(0, 0, 1, 3, 2)
        first.after_a(1, 0, 1, 3, 2)
        second.after_a(0, 0)
        third.own_on()
        first.after_across()
    for t in range(PAIRS):
        joint = nn(n1b[:, :256], get(wa, t, 0, 0, 384)) + nn(n1b[:, 256:], get(wa, t, 1, 0, 384))
        joint = joint.astype(BF).astype(F32)
        qs[t, 0:ROWS, :] = joint[:, :128]
        ks[t, 0:ROWS, :] = joint[:, 128:256] * valid
        vs[t, 0:ROWS, :] = joint[:, 256:] * valid

    def pooling(p, carry):
        pool(qs.at[p])
        qs[p, 504:STACK, :] = jnp.zeros((8, 128), F32)
        qb[p] = (qs[p] * stack_factors()).astype(BF)
        for which, (raw, windows) in enumerate(((ks, kw), (vs, vw))):
            raw_p = raw.at[p]
            pool(raw_p)
            for start, n in BLANK:
                windows[p, start : start + n, :] = jnp.zeros((n, 128), BF)
            for level in range(LEVELS - 1):
                n = COUNT[level]
                rows = slice(AT[level], AT[level] + n)
                coarse = (raw_p[rows, :] * rdiv[rows, :]).astype(BF)
                if level < 4:
                    windows[p, OWN[level] : OWN[level] + n, :] = coarse
                edge_l[p, which, 16 * level : 16 * level + 16, :] = coarse[:16]
                edge_r[p, which, 16 * level : 16 * level + 16, :] = coarse[n - 16 :]
            rows = slice(AT[5], AT[5] + 8)
            far[me, p, which] = raw_p[rows, :] * rdiv[rows, :]
        exchange(*halos(p))
        return carry

    def to_left(src, dst, sem):
        return pltpu.make_async_remote_copy(
            src, dst, send_sem.at[sem], recv_sem.at[sem], device_id={"tensor": jnp.maximum(me - 1, 0)}, device_id_type=MESH
        )

    def to_right(src, dst, sem):
        return pltpu.make_async_remote_copy(
            src,
            dst,
            send_sem.at[sem],
            recv_sem.at[sem],
            device_id={"tensor": jnp.minimum(me + 1, tensors - 1)},
            device_id_type=MESH,
        )

    def to_peer(k, src, dst, sem):
        return pltpu.make_async_remote_copy(
            src, dst, send_sem.at[sem], recv_sem.at[sem], device_id={"tensor": lax.rem(me + k, tensors)}, device_id_type=MESH
        )

    def exchange(base, left_src, left_dst, right_src, right_dst, far_src, far_dst):
        for k in range(1, tensors):
            to_peer(k, far_src(k), far_dst(k), base + 1 + k).start()

        @pl.when(me > 0)
        def _():
            to_left(left_src, left_dst, base).start()

        @pl.when(me < tensors - 1)
        def _():
            to_right(right_src, right_dst, base + 1).start()

    def exchanged(base, left_src, left_dst, right_src, right_dst, far_src, far_dst):
        @pl.when(me > 0)
        def _():
            to_left(left_src, left_dst, base).wait_send()
            to_right(right_src, right_dst, base + 1).wait_recv()

        @pl.when(me == 0)
        def _():
            right_dst[...] = jnp.zeros(right_dst.shape, BF)

        @pl.when(me < tensors - 1)
        def _():
            to_right(right_src, right_dst, base + 1).wait_send()
            to_left(left_src, left_dst, base).wait_recv()

        @pl.when(me == tensors - 1)
        def _():
            left_dst[...] = jnp.zeros(left_dst.shape, BF)

        for k in range(1, tensors):
            to_peer(k, far_src(k), far_dst(k), base + 1 + k).wait()

    def halos(p):
        block = lambda k: far.at[me, p]
        return (5 * p, edge_l.at[p], halo_r.at[p], edge_r.at[p], halo_l.at[p], block, block)

    lax.fori_loop(0, PAIRS, pooling, 0)
    if fast:
        second.after_z(1, 3)
        third.along_z()

    def attend(p, carry):
        exchanged(*halos(p))
        for which, windows in enumerate((kw, vw)):
            for level in range(LEVELS - 1):
                windows[p, LEFT[level] : LEFT[level] + 16, :] = halo_l[p, which, 16 * level : 16 * level + 16, :]
                windows[p, RIGHT[level] : RIGHT[level] + 16, :] = halo_r[p, which, 16 * level : 16 * level + 16, :]
            groups = jnp.concatenate([far[g, p, which] for g in range(tensors)], axis=0)
            windows[p, FAR:KEYS, :] = groups.astype(BF)
        for k in range(TILES):
            here = slice(64 * k, 64 * k + 64)
            keys = slice(TILE_AT[k], TILE_AT[k] + 128)
            s = nt(both(qb[p, here, :]), kw[p, keys, :])
            w = wt[k]
            w = jnp.concatenate([w, w], axis=0)
            s = jnp.where(w > 0.0, s, -1e30)
            m = jnp.max(s, axis=-1, keepdims=True)
            e = w * jnp.exp(s - m)
            low = e.astype(BF)
            total = jnp.sum(low.astype(F32), axis=-1, keepdims=True)
            eb[p, k] = low
            ns[here, :] = joined(nn(low, vw[p, keys, :]))
            ml[p, here, :] = joined(jnp.broadcast_to(m, (128, 128)))
            ds_[here, :] = joined(jnp.broadcast_to(total, (128, 128)))
            if fast and k == 3:

                @pl.when(p == 1)
                def _():
                    second.after_b(3)
                    second.after_a(0, 1)

                @pl.when(p == 2)
                def _():
                    second.after_a(1, 1)
                    second.after_a(0, 2)
                    third.after_z(1)
                    third.after_a(0, 0)

                @pl.when(p == 3)
                def _():
                    second.after_a(1, 2)
                    third.after_z(2)
                    third.after_b(1)
                    third.after_a(1, 0)

        rows = slice(AT[5], AT[5] + 8)
        num, top, den = ns[rows, :], ml[p, rows, :], ds_[rows, :]
        for level in range(LEVELS - 2, -1, -1):
            n = COUNT[level]
            rows = slice(AT[level], AT[level] + n)
            num, top, den = doubled(tmp_a, num, n // 2), doubled(tmp_b, top, n // 2), doubled(tmp_c, den, n // 2)
            own = ml[p, rows, :]
            both_top = jnp.maximum(own, top)
            left, right = jnp.exp(own - both_top), jnp.exp(top - both_top)
            num = ns[rows, :] * left + num * right
            den = ds_[rows, :] * left + den * right
            top = both_top
        inverse = 1.0 / den
        att[p] = num * inverse
        mm[p] = top
        dacc[p] = inverse
        if fast:

            @pl.when(p == 0)
            def _():
                second.after_z(2)
                second.after_b(1)
                second.after_a(1, 0)

            @pl.when(p == 1)
            def _():
                second.after_b(2)
                second.after_a(0, 3)
                third.after_b(0)

            @pl.when(p == 2)
            def _():
                second.after_a(1, 3)
                third.after_z(3)

            @pl.when(p == 3)
            def _():
                third.after_a(0, 1)
                third.after_b(3)

        return carry

    lax.fori_loop(0, PAIRS, attend, 0)

    if fast:
        second.after_across()
    attb = [att[t].astype(BF) for t in range(PAIRS)]
    branch = []
    for y in range(2):
        total = nt(attb[0], get(wm, 0, y, 0, 128))
        for t in range(1, PAIRS):
            total = total + nt(attb[t], get(wm, t, y, 0, 128))
        branch.append(total)
    branch = jnp.concatenate(branch, axis=1)
    middle = ref["xs"][...] + branch
    n2, r2 = normalised(middle)
    n2s[...] = n2
    n2b = n2.astype(BF)
    n2t = n2b.T
    if fast:
        third.after_b(2)
        third.after_a(0, 3)
        third.after_a(1, 1)
    cotb = ref["cots"][...].astype(BF)
    cott = cotb.T

    acts, slopes = ref["acts"], ref["slopes"]
    for t in range(PAIRS):
        pre = nn(n2b[:, :256], get(wm, t, 0, 128, 640)) + nn(n2b[:, 256:], get(wm, t, 1, 128, 640))
        act, slope = gelu_both(pre)
        act = act.astype(BF)
        acts[t] = act
        slopes[t] = slope
        for y in range(2):
            put(gl, t, y, 0, 512, nn(cott[256 * y : 256 * y + 256, :], act))
        if fast:
            late.across(t, 0, 512, 0)
            if t == 1:
                third.after_a(0, 2)
            if t == 2:
                third.after_a(1, 3)
    if fast:
        third.after_a(1, 2)
        third.after_across()
        late.across_all(late_parts)
    dense, dn2 = [0.0, 0.0], [0.0, 0.0]
    for t in range(PAIRS):
        if fast:
            late.far((1, 3, 2, 0)[t])
        act_grad = nn(cotb[:, :256], get(wl, t, 0, 0, 512)) + nn(cotb[:, 256:], get(wl, t, 1, 0, 512))
        pre_grad = (act_grad * slopes[t]).astype(BF)
        act = acts[t]
        for y in range(2):
            dense[y] = dense[y] + nt(act, get(wl, t, y, 0, 512))
            dn2[y] = dn2[y] + nt(pre_grad, get(wm, t, y, 128, 640))
            put(gm, t, y, 128, 640, nn(n2t[256 * y : 256 * y + 256, :], pre_grad))
        if fast:
            middle_sum.across(t, 128, 640, 0)
    dense = jnp.concatenate(dense, axis=1)
    dn2 = jnp.concatenate(dn2, axis=1)
    result = middle + dense
    out_ref[...] = (mixed(result, False) if fast else result).astype(BF)
    live = (iota((ROWS, 512), 0) + me * ROWS < valid_len).astype(F32)
    small_ref[2:3, :] = jnp.sum(live * result * result, axis=0, keepdims=True)
    small_ref[3:4, :] = jnp.sum(live * branch * branch, axis=0, keepdims=True)
    small_ref[4:5, :] = jnp.sum(live * dense * dense, axis=0, keepdims=True)
    small_ref[5:6, :] = jnp.sum(live, axis=0, keepdims=True)
    small_ref[6:8, :] = jnp.zeros((2, 512), F32)
    n2 = n2s[...]
    small_ref[1:2, :] = jnp.sum(dn2 * n2, axis=0, keepdims=True)
    middle_grad = ref["cots"][...] + norm_back(n2, r2, dn2)
    n2s[...] = middle_grad
    mgb = middle_grad.astype(BF)
    mgt = mgb.T
    for t in range(PAIRS):
        us[t, 0:ROWS, :] = nn(mgb[:, :256], get(wm, t, 0, 0, 128)) + nn(mgb[:, 256:], get(wm, t, 1, 0, 128))
        for y in range(2):
            put(gm, t, y, 0, 128, nn(mgt[256 * y : 256 * y + 256, :], att[t].astype(BF)))
        if fast:
            middle_sum.across(t, 0, 128, 4)
    if fast:
        late.near(1, 3)

    def head_sums(v):
        first = jnp.sum(jnp.where(iota(v.shape, 1) < 64, v, 0.0), axis=-1, keepdims=True)
        second = jnp.sum(jnp.where(iota(v.shape, 1) < 64, 0.0, v), axis=-1, keepdims=True)
        return jnp.where(iota(v.shape, 1) < 64, first, second)

    def attend_back(p, carry):
        up = us.at[p]
        grad, inverse = up[0:ROWS, :], dacc[p]
        delta = head_sums(grad * att[p])
        up[0:ROWS, :] = grad * inverse
        ns[0:ROWS, :] = delta * inverse
        mus[0:ROWS, :] = mm[p]
        for level in range(LEVELS - 1):
            n = COUNT[level + 1]
            after = slice(AT[level + 1], AT[level + 1] + n)
            top_e, top_o = pairs_of(mus, AT[level], n)
            top = jnp.minimum(top_e, top_o)
            fe, fo = jnp.exp(top - top_e), jnp.exp(top - top_o)
            u_e, u_o = pairs_of(up, AT[level], n)
            d_e, d_o = pairs_of(ns, AT[level], n)
            up[after, :] = u_e * fe + u_o * fo
            ns[after, :] = d_e * fe + d_o * fo
            mus[after, :] = top
        for rows in (slice(504, STACK),):
            up[rows, :] = jnp.zeros((8, 128), F32)
            ns[rows, :] = jnp.zeros((8, 128), F32)
            mus[rows, :] = jnp.zeros((8, 128), F32)
        for which in range(2):
            dkw[which * PAIRS + p, 0:512, :] = jnp.zeros((512, 128), F32)
        for k in range(TILES):
            here = slice(64 * k, 64 * k + 64)
            keys = slice(TILE_AT[k], TILE_AT[k] + 128)
            factor = jnp.exp(ml[p, here, :] - mus[here, :])
            g = up[here, :] * factor
            g_high = g.astype(BF)
            g2 = both(g_high)
            g4 = jnp.concatenate([g2, both((g - g_high.astype(F32)).astype(BF))], axis=1)
            v2 = vw[p, keys, :]
            v2 = jnp.concatenate([v2, v2], axis=1)
            h = ns[here, :] * factor
            h2 = jnp.concatenate([h[:, 0:1], h[:, 64:65]], axis=0)
            q2 = both(qb[p, here, :])
            low = eb[p, k]
            d = low.astype(F32) * (nt(g4, v2) - h2)
            d = d.astype(BF)
            dv = tn(low, g2)
            dk = tn(d, q2)
            if k < 6:
                dkw[p, keys, :] = dkw[p, keys, :] + dk
                dkw[PAIRS + p, keys, :] = dkw[PAIRS + p, keys, :] + dv
            else:
                dkw[p, keys, :] = dk
                dkw[PAIRS + p, keys, :] = dv
            dqs[p, here, :] = joined(nn(d, kw[p, keys, :]))
            if fast and k == 3:

                @pl.when(p == 0)
                def _():
                    late.near(2)

                @pl.when(p == 1)
                def _():
                    late.own(ref["out_l"], 1)
                    middle_sum.far(3)

                @pl.when(p == 2)
                def _():
                    middle_sum.far(2)
                    late.own(ref["out_l"], 2)

                @pl.when(p == 3)
                def _():
                    late.own(ref["out_l"], 0)
                    middle_sum.far(0)

        for which in range(2):
            row = which * PAIRS + p
            for level in range(LEVELS - 1):
                part = slice(16 * level, 16 * level + 16)
                back_l[p, which, part, :] = dkw[row, LEFT[level] : LEFT[level] + 16, :].astype(BF)
                back_r[p, which, part, :] = dkw[row, RIGHT[level] : RIGHT[level] + 16, :].astype(BF)
            for g in range(tensors):
                dfar[g, p, which] = dkw[row, FAR + 8 * g : FAR + 8 * g + 8, :]
        exchange(*back(p))
        if fast:

            @pl.when(p == 0)
            def _():
                middle_sum.across_all(middle_parts)
                middle_sum.far(1)
                late.near(0)

            @pl.when(p == 1)
            def _():
                late.own(ref["out_l"], 3)

            @pl.when(p == 2)
            def _():
                middle_sum.near(1)

            @pl.when(p == 3)
            def _():
                middle_sum.near(3)

        return carry

    def back(p):
        return (
            20 + 5 * p,
            back_l.at[p],
            got_r.at[p],
            back_r.at[p],
            got_l.at[p],
            lambda k: dfar.at[lax.rem(me + k, tensors), p],
            lambda k: gfar.at[k, p],
        )

    lax.fori_loop(0, PAIRS, attend_back, 0)
    def unpool(p, carry):
        exchanged(*back(p))
        factors = stack_factors()
        cur = dqs[p, AT[5] : AT[5] + 8, :] * factors[AT[5] : AT[5] + 8]
        for level in range(LEVELS - 2, -1, -1):
            rows = slice(AT[level], AT[level] + COUNT[level])
            cur = doubled(tmp_a, cur, COUNT[level] // 2) + dqs[p, rows, :] * factors[rows]
        qs[p, 0:ROWS, :] = cur
        for which, raw in enumerate((ks, vs)):
            row = which * PAIRS + p
            raw_p = raw.at[p]
            cur = gfar[1, p, which]
            for k in range(2, tensors):
                cur = cur + gfar[k, p, which]
            cur = cur * rdiv[AT[5] : AT[5] + 8, :]
            for level in range(LEVELS - 2, -1, -1):
                n = COUNT[level]
                rows = slice(AT[level], AT[level] + n)
                part = slice(16 * level, 16 * level + 16)
                if level < 4:
                    raw_p[rows, :] = dkw[row, OWN[level] : OWN[level] + n, :]
                else:
                    raw_p[rows, :] = jnp.zeros((n, 128), F32)
                first = slice(AT[level], AT[level] + 16)
                last = slice(AT[level] + n - 16, AT[level] + n)
                raw_p[first, :] = raw_p[first, :] + got_l[p, which, part, :].astype(F32)
                raw_p[last, :] = raw_p[last, :] + got_r[p, which, part, :].astype(F32)
                cur = doubled(tmp_a, cur, n // 2) + raw_p[rows, :] * rdiv[rows, :]
            raw_p[0:ROWS, :] = cur * (iota((ROWS, 128), 0) + me * ROWS < valid_len).astype(F32)
        return carry

    lax.fori_loop(0, PAIRS, unpool, 0)
    if fast:
        middle_sum.own(ref["out_m"], 1)

    n1 = n1s[...]
    n1t = n1.astype(BF).T
    dn1 = [0.0, 0.0]
    for t in range(PAIRS):
        joint = jnp.concatenate(
            [qs[t, 0:ROWS, :].astype(BF), ks[t, 0:ROWS, :].astype(BF), vs[t, 0:ROWS, :].astype(BF)], axis=1
        )
        for y in range(2):
            put(ga, t, y, 0, 384, nn(n1t[256 * y : 256 * y + 256, :], joint))
            dn1[y] = dn1[y] + nt(joint, get(wa, t, y, 0, 384))
        if fast:
            early.across(t, 0, 384, 0)
    dn1 = jnp.concatenate(dn1, axis=1)
    small_ref[0:1, :] = jnp.sum(dn1 * n1, axis=0, keepdims=True)
    if fast:
        sums = Remote(ref["sum_send"], ref["sum_recv"])
        got = ref["sums"]
        ways = (at.to_other, at.to_x, at.to_y)

        def sum_send(i):
            got[2 * i] = small_ref[...]
            sums.send(i, got.at[2 * i], got.at[2 * i + 1], ways[i])

        def sum_add(i):
            sums.arrived(i, got.at[2 * i + 1], ways[i])
            small_ref[...] = got[2 * i] + got[2 * i + 1]

        sum_send(0)
        middle_sum.near(2)
        early.across_all(early_parts)
        early.far(1, 3, 2, 0)
        sum_add(0)
        sum_send(1)
        middle_sum.own(ref["out_m"], 3)
        middle_sum.near(0)
        sum_add(1)
        sum_send(2)
        middle_sum.own(ref["out_m"], 2)
        early.near(1, 3, 2, 0)
        sum_add(2)
        got[6 + at.z] = small_ref[...]
        for k in range(1, 4):
            sums.send(2 + k, got.at[6 + at.z], got.at[6 + at.z], at.to_z(k))
        middle_sum.own(ref["out_m"], 0)
        early.own(ref["out_a"], 1, 3, 2, 0)
    r1 = lax.rsqrt(row_variance(ref["xs"][...]) + EPS)
    in_grad = n2s[...] + norm_back(n1, r1, dn1)
    ingrad_ref[...] = (mixed(in_grad, False) if fast else in_grad).astype(BF)
    if fast:
        late.finish(ref["out_l"])
        middle_sum.finish(ref["out_m"])
        early.finish(ref["out_a"])
        for k in range(1, 4):
            sums.arrived(2 + k, got.at[6], at.to_b)
        small_ref[...] = ((got[6] + got[7]) + got[8]) + got[9]
        for remote, parts in ((early, early_parts), (middle_sum, middle_parts), (late, late_parts)):
            for lo, hi, base in parts:
                remote.across_drain(lo, hi, base)
            remote.drain(remote.r2.at[0], at.to_x)
        for remote in (first, second, third):
            remote.drain(remote.own, at.to_x)
        sums.drain(small_ref, at.to_x)


def row_variance(v):
    centred = v - jnp.mean(v, axis=-1, keepdims=True)
    return jnp.mean(centred * centred, axis=-1, keepdims=True)


def run_layer(fast, tensors, lengths, inputs, cotangent, *weights):
    vmem = pl.BlockSpec(memory_space=pltpu.VMEM)
    f = lambda *shape: pltpu.VMEM(shape, F32)
    b = lambda *shape: pltpu.VMEM(shape, BF)
    full = (2, 2, 2, 4, 64) if fast else (tensors, 2, 256)
    groups = dict(zip("aml", weights, strict=True))
    outs = {"out": ((ROWS, 512), BF), "ingrad": ((ROWS, 512), BF), "small": ((8, 512), F32)}
    scratch = {
        "qs": f(PAIRS, STACK, 128),
        "ks": f(PAIRS, STACK, 128),
        "vs": f(PAIRS, STACK, 128),
        "qb": b(PAIRS, STACK, 128),
        "kw": b(PAIRS, KEYS, 128),
        "vw": b(PAIRS, KEYS, 128),
        "wt": f(TILES, 64, 128),
        "rdiv": f(STACK, 128),
        "edge_l": b(PAIRS, 2, HALO, 128),
        "edge_r": b(PAIRS, 2, HALO, 128),
        "halo_l": b(PAIRS, 2, HALO, 128),
        "halo_r": b(PAIRS, 2, HALO, 128),
        "far": f(tensors, PAIRS, 2, 8, 128),
        "eb": b(PAIRS, TILES, 128, 128),
        "ns": f(STACK, 128),
        "ml": f(PAIRS, STACK, 128),
        "ds": f(STACK, 128),
        "att": f(PAIRS, ROWS, 128),
        "mm": f(PAIRS, ROWS, 128),
        "tmp_a": f(ROWS, 128),
        "tmp_b": f(ROWS, 128),
        "tmp_c": f(ROWS, 128),
        "xs": f(ROWS, 512),
        "cots": f(ROWS, 512),
        "n1s": f(ROWS, 512),
        "n2s": f(ROWS, 512),
        "dacc": f(PAIRS, ROWS, 128),
        "us": f(PAIRS, STACK, 128),
        "mus": f(STACK, 128),
        "dqs": f(PAIRS, STACK, 128),
        "acts": b(PAIRS, ROWS, 512),
        "slopes": f(PAIRS, ROWS, 512),
        "dkw": f(2 * PAIRS, KEYS, 128),
        "back_l": b(PAIRS, 2, HALO, 128),
        "back_r": b(PAIRS, 2, HALO, 128),
        "got_l": b(PAIRS, 2, HALO, 128),
        "got_r": b(PAIRS, 2, HALO, 128),
        "dfar": f(tensors, PAIRS, 2, 8, 128),
        "gfar": f(tensors, PAIRS, 2, 8, 128),
        "send_sem": pltpu.SemaphoreType.DMA((40,)),
        "recv_sem": pltpu.SemaphoreType.DMA((40,)),
    }
    if fast:
        ins = ("lengths", "x", "cot", "part_a", "part_m", "part_l")
        for name, part in groups.items():
            c = part.shape[-1]
            outs |= {"out_" + name: ((64, c), F32)}
            scratch |= {
                "w" + name: b(*full, c),
                "g" + name: b(*full, c),
                name + "0": b(2, 2, 4, 64, c),
                name + "1": b(2, 4, 64, c),
                name + "2": b(4, 64, c),
                name + "3": b(3, 64, c),
            }
        scratch |= {
            "sums": f(10, 8, 512),
            "gather_send": pltpu.SemaphoreType.DMA((3, 31)),
            "gather_recv": pltpu.SemaphoreType.DMA((3, 31)),
            "reduce_send": pltpu.SemaphoreType.DMA((3, 23)),
            "reduce_recv": pltpu.SemaphoreType.DMA((3, 23)),
            "sum_send": pltpu.SemaphoreType.DMA((6,)),
            "sum_recv": pltpu.SemaphoreType.DMA((6,)),
        }
    else:
        ins = ("lengths", "x", "cot", "wa", "wm", "wl")
        outs |= {"g" + name: (w.shape, BF) for name, w in groups.items()}
    return pl.pallas_call(
        functools.partial(layer_kernel, fast, tensors, (*ins, *outs, *scratch)),
        out_shape=tuple(jax.ShapeDtypeStruct(*shape) for shape in outs.values()),
        in_specs=[pl.BlockSpec(memory_space=pltpu.SMEM)] + [vmem] * 5,
        out_specs=(vmem,) * 6,
        scratch_shapes=list(scratch.values()),
        compiler_params=pltpu.CompilerParams(
            collective_id=0, has_side_effects=True, vmem_limit_bytes=62 * 1024 * 1024
        ),
        name="layer",
    )(lengths, inputs, cotangent, *weights)


def per_device(
    fast,
    inputs,
    lengths,
    cotangent,
    query_weight,
    key_weight,
    value_weight,
    output_weight,
    inner_weight,
    outer_weight,
    first_gain,
    second_gain,
):
    tensors, groups = lax.axis_size("tensor"), lax.axis_size("dp")
    everyone = ("tensor", "dp")
    g1 = first_gain.astype(F32)[:, None]
    g2 = second_gain.astype(F32)[:, None]
    scaled = lambda g, w: (g * w.astype(F32)).astype(BF)
    part_a = scaled(g1, jnp.concatenate([query_weight, key_weight, value_weight], axis=1))
    part_m = jnp.concatenate([output_weight.T, scaled(g2, inner_weight)], axis=1)
    parts = (part_a, part_m, outer_weight.T)
    width, group = first_gain.shape[0], lax.axis_index("dp")
    if fast:
        out, input_grad, small, ga, gm, gl = run_layer(fast, tensors, lengths, inputs, cotangent, *parts)
        at = (group % 2) * 256 + (group // 2) * 64
    else:
        full = [lax.all_gather(p, everyone, axis=0, tiled=True).reshape(tensors, 2, 256, -1) for p in parts]
        out, input_grad, small, *grads = run_layer(fast, tensors, lengths, inputs, cotangent, *full)

        def reduced(g):
            return lax.psum_scatter(
                g.reshape(tensors * 512, g.shape[-1]).astype(F32), everyone, scatter_dimension=0, tiled=True
            )

        ga, gm, gl = (reduced(g) for g in grads)
        small = lax.psum(small, everyone)
        at = group * width
    gains = lax.dynamic_slice(small, (0, at), (2, width))
    sums = jnp.sum(small, axis=1)
    root_mean_squares = jnp.sqrt(sums[2:5] / sums[5])
    ga = ga * g1
    return (
        out,
        input_grad,
        ga[:, 0:128],
        ga[:, 128:256],
        ga[:, 256:384],
        gm[:, 0:128].T,
        gm[:, 128:640] * g2,
        gl.T,
        gains[0] / first_gain.astype(F32),
        gains[1] / second_gain.astype(F32),
        root_mean_squares,
    )


def solution(mesh):
    fast = (mesh.shape["dp"], mesh.shape["tensor"]) == (8, 4)
    return jax.shard_map(
        functools.partial(per_device, fast),
        mesh=mesh,
        in_specs=(
            P(("dp", "tensor"), None),
            P("dp"),
            P(("dp", "tensor"), None),
            P("dp", "tensor"),
            P("dp", "tensor"),
            P("dp", "tensor"),
            P("tensor", "dp"),
            P("dp", "tensor"),
            P("tensor", "dp"),
            P("dp"),
            P("dp"),
        ),
        out_specs=(
            P(("dp", "tensor"), None),
            P(("dp", "tensor"), None),
            P("dp", "tensor"),
            P("dp", "tensor"),
            P("dp", "tensor"),
            P("tensor", "dp"),
            P("dp", "tensor"),
            P("tensor", "dp"),
            P("dp"),
            P("dp"),
            P(),
        ),
        check_vma=False,
    )
```

```python
import functools

import jax
import jax.numpy as jnp
from jax import lax
from jax.experimental import pallas as pl
from jax.experimental.pallas import tpu as pltpu
from jax.sharding import PartitionSpec as P

MESH = pl.DeviceIdType.MESH
F32, BF = jnp.float32, jnp.bfloat16
HEAD_DIM = 64
EPS = 1e-05

ROWS, PAIRS, LEVELS = 256, 4, 6
COUNT = (256, 128, 64, 32, 16, 8)
AT = (0, 256, 384, 448, 480, 496)
STACK = 512
OWN = (32, 352, 544, 656)
LEFT = (16, 336, 528, 640, 704)
RIGHT = (288, 480, 608, 688, 720)
FAR = 736
KEYS = 768
BLANK = ((0, 16), (304, 32), (496, 32), (624, 16))
TILE_AT = (0, 64, 128, 192, 320, 384, 512, 640)
TILES = 8
HALO = 80
LOADS = (
    ("g1", (64,)),
    ("g2", (64,)),
    ("q", (64, 128)),
    ("k", (64, 128)),
    ("v", (64, 128)),
    ("o", (64, 128)),
    ("w1", (64, 512)),
    ("part_l", (64, 512)),
    ("x", (ROWS, 512)),
    ("cot", (ROWS, 512)),
)


def nn(a, b):
    return lax.dot_general(a, b, (((1,), (0,)), ((), ())), preferred_element_type=F32)


def nt(a, b):
    return lax.dot_general(a, b, (((1,), (1,)), ((), ())), preferred_element_type=F32)


def tn(a, b):
    return lax.dot_general(a, b, (((0,), (0,)), ((), ())), preferred_element_type=F32)


def iota(shape, dim):
    return lax.broadcasted_iota(jnp.int32, shape, dim)


def level_counts(index, level, total, valid_len):
    factor = 1 << level
    c = jnp.clip(valid_len - index * factor, 0, factor)
    return jnp.where((index >= 0) & (index < total), c, 0).astype(F32)


def tile_weights(k, me, tensors, valid_len):
    i, j = iota((64, 128), 0), iota((64, 128), 1)
    if k < 7:
        level = 0 if k < 4 else 1 if k < 6 else 2
        first = 64 * (k - AT[level] // 64)
        n = COUNT[level]
        c = level_counts(me * n + first - 32 + j, level, n * tensors, valid_len)
        near = jnp.abs((i >> 4) - (j >> 4) + 2) <= 1
        if level:
            near = near & (jnp.abs((i >> 3) - (j >> 3) + 4) > 1)
        return jnp.where(near, c, 0.0)
    c3 = level_counts(me * 32 + j - 16, 3, 32 * tensors, valid_len)
    near3 = (jnp.abs((i >> 4) - (j >> 4) + 1) <= 1) & (jnp.abs((i >> 3) - (j >> 3) + 2) > 1)
    near3 = near3 & (i < 32) & (j < 64)
    key4 = jnp.where(j < 80, j - 80, j - 64)
    c4 = level_counts(me * 16 + key4, 4, 16 * tensors, valid_len)
    near4 = (jnp.abs(((i - 32) >> 3) - (key4 >> 3)) > 1) & (i >= 32) & (i < 48) & (j >= 64) & (j < 96)
    key5 = j - 96
    c5 = level_counts(key5, 5, 8 * tensors, valid_len)
    near5 = (jnp.abs(me - (key5 >> 3)) > 1) & (i >= 48) & (i < 56) & (j >= 96)
    return jnp.where(near3, c3, 0.0) + jnp.where(near4, c4, 0.0) + jnp.where(near5, c5, 0.0)


def row_divisors(me, tensors, valid_len):
    i = iota((STACK, 128), 0)
    out = jnp.ones((STACK, 128), F32)
    for level in range(1, LEVELS):
        c = level_counts(i - AT[level] + me * COUNT[level], level, COUNT[level] * tensors, valid_len)
        here = (i >= AT[level]) & (i < AT[level] + COUNT[level])
        out = jnp.where(here, 1.0 / jnp.maximum(c, 1.0), out)
    return out


def stack_factors():
    i = iota((STACK, 128), 0)
    out = jnp.full((STACK, 128), HEAD_DIM ** (-0.5), F32)
    for level in range(1, LEVELS):
        out = jnp.where(i >= AT[level], HEAD_DIM ** (-0.5) / (1 << level), out)
    return out


def pairs_of(ref, start, n):
    return ref[pl.ds(start, n, stride=2), :], ref[pl.ds(start + 1, n, stride=2), :]


def pool(ref):
    for level in range(LEVELS - 1):
        n = COUNT[level + 1]
        even, odd = pairs_of(ref, AT[level], n)
        ref[AT[level + 1] : AT[level + 1] + n, :] = even + odd


def doubled(ref, value, n):
    ref[pl.ds(0, n, stride=2), :] = value
    ref[pl.ds(1, n, stride=2), :] = value
    return ref[0 : 2 * n, :]


def normalised(v):
    centred = v - jnp.mean(v, axis=-1, keepdims=True)
    r = lax.rsqrt(jnp.mean(centred * centred, axis=-1, keepdims=True) + EPS)
    return centred * r, r


def norm_back(n, r, hg):
    return r * (hg - jnp.mean(hg, axis=-1, keepdims=True) - n * jnp.mean(hg * n, axis=-1, keepdims=True))


def gelu_both(u):
    c = 0.7978845608028654
    square = u * u
    th = jnp.tanh(c * (u + 0.044715 * (square * u)))
    half = 0.5 * (1.0 + th)
    slope = half + (0.5 * c) * u * (1.0 - th * th) * (1.0 + 0.134145 * square)
    return u * half, slope


class Place:
    def __init__(self):
        self.d, self.t = lax.axis_index("dp"), lax.axis_index("tensor")
        self.z, self.y = self.d // 2, self.d % 2
        self.x, self.c = self.t // 2, self.t % 2
        self.a = self.x + self.c * (self.y - self.x)
        self.b = self.y + self.c * (self.x - self.y)
        flip_x, flip_y = 2 - 4 * self.x, 1 - 2 * self.y
        self.to_x, self.to_y = (self.d, self.t + flip_x), (self.d + flip_y, self.t)
        self.to_a = (self.d + self.c * flip_y, self.t + (1 - self.c) * flip_x)
        self.to_b = (self.d + (1 - self.c) * flip_y, self.t + self.c * flip_x)
        self.to_other = (self.d, self.t + 1 - 2 * self.c)
        self.to_across = (self.d, 3 - self.t)

    def to_z(self, k):
        return (2 * ((self.z + k) % 4) + self.y, self.t)


def flipped(bit, by):
    return 1 - bit if by else bit


class Remote:
    def __init__(self, send_sem, recv_sem):
        self.send_sem, self.recv_sem, self.started = send_sem, recv_sem, set()

    def copy(self, i, src, dst, to):
        return pltpu.make_async_remote_copy(
            src, dst, self.send_sem.at[i], self.recv_sem.at[i], device_id=to, device_id_type=MESH
        )

    def send(self, i, src, dst, to):
        self.copy(i, src, dst, to).start()
        self.started.add(i)

    def arrived(self, i, dst, to):
        self.copy(i, dst, dst, to).wait_recv()

    def drain(self, like, to):
        for i in sorted(self.started):
            self.copy(i, like, like, to).wait_send()


class Gather(Remote):
    def __init__(self, at, own, w, send_sem, recv_sem):
        super().__init__(send_sem, recv_sem)
        self.at, self.own, self.w = at, own, w

    def shard(self, j, aa=0, bb=0, plane=0):
        at = self.at
        a, b = (at.b, at.a) if plane else (at.a, at.b)
        return self.w.at[flipped(at.c, plane), flipped(a, aa), flipped(b, bb), (at.z + 4 - j) % 4]

    def source(self, j, aa=0, bb=0):
        return self.own if (j, aa, bb) == (0, 0, 0) else self.shard(j, aa, bb)

    def along_z(self):
        for k in (1, 3, 2):
            self.send(k - 1, self.own, self.shard(0), self.at.to_z(k))

    def along_b(self, j):
        self.send(3 + j, self.source(j), self.shard(j), self.at.to_b)

    def along_a(self, j, bb):
        self.send(7 + 4 * bb + j, self.source(j, 0, bb), self.shard(j, 0, bb), self.at.to_a)

    def across(self, j, aa, bb):
        self.send(15 + 8 * aa + 4 * bb + j, self.source(j, aa, bb), self.shard(j, aa, bb), self.at.to_other)

    def own_on(self):
        self.along_b(0)
        self.along_a(0, 0)
        self.across(0, 0, 0)

    def after_z(self, *js):
        for j in js:
            self.arrived(j - 1, self.shard(j), self.at.to_b)
            self.along_b(j)
            self.along_a(j, 0)
            self.across(j, 0, 0)

    def after_b(self, *js):
        for j in js:
            self.arrived(3 + j, self.shard(j, 0, 1), self.at.to_b)
            self.along_a(j, 1)
            self.across(j, 0, 1)

    def after_a(self, bb, *js):
        for j in js:
            self.arrived(7 + 4 * bb + j, self.shard(j, 1, bb), self.at.to_b)
            self.across(j, 1, bb)

    def after_across(self):
        for aa in range(2):
            for bb in range(2):
                for j in range(4):
                    self.arrived(15 + 8 * aa + 4 * bb + j, self.shard(j, aa, bb, 1), self.at.to_b)


class Reduce(Remote):
    def __init__(self, at, g, r0, r1, r2, r3, send_sem, recv_sem):
        super().__init__(send_sem, recv_sem)
        self.at, self.g, self.r0, self.r1, self.r2, self.r3 = at, g, r0, r1, r2, r3

    def across(self, t, lo, hi, base):
        @pl.when(self.at.c != t % 2)
        def _():
            for a, b in ((t // 2, 0), (t // 2, 1)) if t % 2 == 0 else ((0, t // 2), (1, t // 2)):
                self.copy(
                    base + 2 * a + b,
                    self.g.at[t % 2, a, b, :, :, lo:hi],
                    self.r0.at[a, b, :, :, lo:hi],
                    self.at.to_other,
                ).start()

    def across_wait(self, a, b, lo, hi, base):
        piece = self.r0.at[a, b, :, :, lo:hi]
        copy = self.copy(base + 2 * a + b, piece, piece, self.at.to_other)
        copy.wait_recv()

    def across_drain(self, lo, hi, base):
        for i in range(4):
            piece = self.r0.at[i // 2, i % 2, :, :, lo:hi]
            self.copy(base + i, piece, piece, self.at.to_other).wait_send()

    def across_all(self, parts):
        for a in range(2):
            for b in range(2):
                for lo, hi, base in parts:
                    self.across_wait(a, b, lo, hi, base)

    def far(self, *js):
        at = self.at
        for j in js:
            z = (at.z + j) % 4
            for bb in (1, 0):
                b = flipped(at.b, bb)
                here = self.g.at[at.c, 1 - at.a, b, z]
                here[...] = (here[...].astype(F32) + self.r0[1 - at.a, b, z].astype(F32)).astype(BF)
                self.send(8 + 4 * bb + j, here, self.r1.at[b, z], at.to_a)

    def near(self, *js):
        at = self.at
        b = 1 - at.b
        for j in js:
            z = (at.z + j) % 4
            here = self.g.at[at.c, at.a, b, z]
            self.arrived(12 + j, self.r1.at[b, z], at.to_a)
            total = here[...].astype(F32) + self.r0[at.a, b, z].astype(F32) + self.r1[b, z].astype(F32)
            here[...] = total.astype(BF)
            self.send(16 + j, here, self.r2.at[z], at.to_b)

    def own(self, out, *js):
        at = self.at
        b = at.b
        for j in js:
            z = (at.z + j) % 4
            here = self.g.at[at.c, at.a, b, z]
            self.arrived(8 + j, self.r1.at[b, z], at.to_a)
            self.arrived(16 + j, self.r2.at[z], at.to_b)
            total = here[...].astype(F32) + self.r0[at.a, b, z].astype(F32)
            total = total + self.r1[b, z].astype(F32) + self.r2[z].astype(F32)
            if j:
                here[...] = total.astype(BF)
                self.send(20 + j - 1, here, self.r3.at[j - 1], at.to_z(j))
            else:
                out[...] = total

    def finish(self, out):
        for k in (1, 3, 2):
            self.arrived(20 + k - 1, self.r3.at[k - 1], self.at.to_b)
        total = out[...] + self.r3[0].astype(F32)
        out[...] = total + self.r3[1].astype(F32) + self.r3[2].astype(F32)


def mixed(v, into):
    tiles = [v[:, 128 * i : 128 * i + 128] for i in range(4)]
    rolled = [pltpu.roll(tile, 64, 1) for tile in tiles]
    low = iota(tiles[0].shape, 1) < 64
    if into:
        pairs = ((0, 1, 0), (2, 3, 0), (0, 1, 1), (2, 3, 1))
    else:
        pairs = ((0, 2, 0), (0, 2, 1), (1, 3, 0), (1, 3, 1))
    out = []
    for i, k, high in pairs:
        out.append(jnp.where(low, rolled[i], tiles[k]) if high else jnp.where(low, tiles[i], rolled[k]))
    return jnp.concatenate(out, axis=1)


def layer_kernel(fast, tensors, names, *refs):
    ref = dict(zip(names, refs, strict=True))
    if fast:
        loads = {
            n: pltpu.make_async_copy(ref["in_" + n], ref[n], ref["in_sem"].at[i]) for i, (n, _) in enumerate(LOADS)
        }
        for load in loads.values():
            load.start()
    me = lax.axis_index("tensor")
    valid_len = ref["lengths"][0]
    barrier = pltpu.get_barrier_semaphore()
    if fast:
        at = Place()
        peers = [at.to_z(1), at.to_z(2), at.to_z(3), at.to_y, at.to_x, at.to_other, at.to_across]
    else:
        peers = [{"tensor": lax.rem(me + k, tensors)} for k in range(1, tensors)]
    for peer in peers:
        pl.semaphore_signal(barrier, inc=1, device_id=peer, device_id_type=MESH)
    len_ref, x_ref, cot_ref = (ref[n] for n in ("lengths", "x", "cot"))
    if fast:
        out_ref, ingrad_ref = ref["rows"].at[:, 0:512], ref["rows"].at[:, 512:1024]
        outs = {"a": ref["grads"].at[:, 0:384], "m": ref["grads"].at[:, 384:1024], "l": ref["grads"].at[:, 1024:1536]}
        for n, _ in LOADS[:8]:
            loads[n].wait()
        g1, g2 = (ref[n][...].astype(F32).reshape(1, 64) for n in ("g1", "g2"))
        column = lambda g: jnp.sum(jnp.where(iota((64, 64), 0) == iota((64, 64), 1), g, 0.0), axis=1, keepdims=True)
        g1c, g2c = column(g1), column(g2)
        for i, n in enumerate("qkv"):
            ref["part_a"][:, 128 * i : 128 * i + 128] = (g1c * ref[n][...].astype(F32)).astype(BF)
        ref["part_m"][:, 0:128] = ref["o"][...]
        ref["part_m"][:, 128:640] = (g2c * ref["w1"][...].astype(F32)).astype(BF)
    else:
        out_ref, ingrad_ref = ref["out"], ref["ingrad"]
    qs, ks, vs, qb, kw, vw, wt, rdiv = (ref[n] for n in ("qs", "ks", "vs", "qb", "kw", "vw", "wt", "rdiv"))
    edge_l, edge_r, halo_l, halo_r, far = (ref[n] for n in ("edge_l", "edge_r", "halo_l", "halo_r", "far"))
    eb, ns, ml, ds_, att, mm = (ref[n] for n in ("eb", "ns", "ml", "ds", "att", "mm"))
    tmp_a, tmp_b, tmp_c, n1s, n2s, dacc = (ref[n] for n in ("tmp_a", "tmp_b", "tmp_c", "n1s", "n2s", "dacc"))
    us, mus, dqs, dkw = (ref[n] for n in ("us", "mus", "dqs", "dkw"))
    back_l, back_r, got_l, got_r, dfar, gfar = (
        ref[n] for n in ("back_l", "back_r", "got_l", "got_r", "dfar", "gfar")
    )
    send_sem, recv_sem, small_ref = ref["send_sem"], ref["recv_sem"], ref["small"]
    ga, gm, gl = ref["ga"], ref["gm"], ref["gl"]
    wa, wm, wl = ref["wa"], ref["wm"], ref["wl"]

    def view(r, t, y):
        if not fast:
            return r.at[t, y]
        return r.at[0, t // 2, y] if t % 2 == 0 else r.at[1, y, t // 2]

    def get(r, t, y, lo, hi):
        return view(r, t, y)[..., lo:hi].reshape(256, hi - lo)

    def put(r, t, y, lo, hi, value):
        v = view(r, t, y)
        v[..., lo:hi] = value.astype(BF).reshape(*v.shape[:-1], hi - lo)

    pl.semaphore_wait(barrier, len(peers))
    if fast:
        first, second, third = (
            Gather(at, ref["part_" + n], ref["w" + n], ref["gather_send"].at[i], ref["gather_recv"].at[i])
            for i, n in enumerate("aml")
        )
        early, middle_sum, late = (
            Reduce(
                at,
                ref["g" + n],
                *(ref[n + str(k)] for k in range(4)),
                ref["reduce_send"].at[i],
                ref["reduce_recv"].at[i],
            )
            for i, n in enumerate("aml")
        )
        early_parts, middle_parts, late_parts = ((0, 384, 0),), ((128, 640, 0), (0, 128, 4)), ((0, 512, 0),)
        first.along_z()
        first.own_on()
        second.own_on()
        for n in "aml":
            ref["w" + n][at.c, at.a, at.b, at.z] = ref["part_" + n][...]

    lane = iota((64, 128), 1)
    low_lanes = lane < 64
    low_b = low_lanes.astype(F32).astype(BF)
    high_b = (1.0 - low_lanes.astype(F32)).astype(BF)

    def both(v):
        return jnp.concatenate([v * low_b, v * high_b], axis=0)

    def joined(v):
        return jnp.where(low_lanes, v[:64], v[64:])

    if fast:
        loads["x"].wait()
        loads["cot"].wait()
    x = x_ref[...].astype(F32)
    cot = cot_ref[...].astype(F32)
    if fast:
        x, cot = mixed(x, True), mixed(cot, True)
    ref["xs"][...] = x
    ref["cots"][...] = cot
    n1, r1 = normalised(x)
    n1s[...] = n1
    n1b = n1.astype(BF)
    valid = (iota((ROWS, 128), 0) + me * ROWS < valid_len).astype(F32)
    rdiv[...] = row_divisors(me, tensors, valid_len)
    for k in range(TILES):
        wt[k] = tile_weights(k, me, tensors, valid_len)
    if fast:
        first.after_z(1, 3, 2)
        second.along_z()
        first.after_b(0, 1, 3, 2)
        second.after_b(0)
        first.after_a(0, 0, 1, 3, 2)
        first.after_a(1, 0, 1, 3, 2)
        second.after_a(0, 0)
        third.own_on()
        first.after_across()
    for t in range(PAIRS):
        joint = nn(n1b[:, :256], get(wa, t, 0, 0, 384)) + nn(n1b[:, 256:], get(wa, t, 1, 0, 384))
        joint = joint.astype(BF).astype(F32)
        qs[t, 0:ROWS, :] = joint[:, :128]
        ks[t, 0:ROWS, :] = joint[:, 128:256] * valid
        vs[t, 0:ROWS, :] = joint[:, 256:] * valid

    def pooling(p, carry):
        pool(qs.at[p])
        qs[p, 504:STACK, :] = jnp.zeros((8, 128), F32)
        qb[p] = (qs[p] * stack_factors()).astype(BF)
        for which, (raw, windows) in enumerate(((ks, kw), (vs, vw))):
            raw_p = raw.at[p]
            pool(raw_p)
            for start, n in BLANK:
                windows[p, start : start + n, :] = jnp.zeros((n, 128), BF)
            for level in range(LEVELS - 1):
                n = COUNT[level]
                rows = slice(AT[level], AT[level] + n)
                coarse = (raw_p[rows, :] * rdiv[rows, :]).astype(BF)
                if level < 4:
                    windows[p, OWN[level] : OWN[level] + n, :] = coarse
                edge_l[p, which, 16 * level : 16 * level + 16, :] = coarse[:16]
                edge_r[p, which, 16 * level : 16 * level + 16, :] = coarse[n - 16 :]
            rows = slice(AT[5], AT[5] + 8)
            far[me, p, which] = raw_p[rows, :] * rdiv[rows, :]
        exchange(*halos(p))
        return carry

    def to_left(src, dst, sem):
        return pltpu.make_async_remote_copy(
            src, dst, send_sem.at[sem], recv_sem.at[sem], device_id={"tensor": jnp.maximum(me - 1, 0)}, device_id_type=MESH
        )

    def to_right(src, dst, sem):
        return pltpu.make_async_remote_copy(
            src,
            dst,
            send_sem.at[sem],
            recv_sem.at[sem],
            device_id={"tensor": jnp.minimum(me + 1, tensors - 1)},
            device_id_type=MESH,
        )

    def to_peer(k, src, dst, sem):
        return pltpu.make_async_remote_copy(
            src, dst, send_sem.at[sem], recv_sem.at[sem], device_id={"tensor": lax.rem(me + k, tensors)}, device_id_type=MESH
        )

    def exchange(base, left_src, left_dst, right_src, right_dst, far_src, far_dst):
        for k in range(1, tensors):
            to_peer(k, far_src(k), far_dst(k), base + 1 + k).start()

        @pl.when(me > 0)
        def _():
            to_left(left_src, left_dst, base).start()

        @pl.when(me < tensors - 1)
        def _():
            to_right(right_src, right_dst, base + 1).start()

    def exchanged(base, left_src, left_dst, right_src, right_dst, far_src, far_dst):
        @pl.when(me > 0)
        def _():
            to_left(left_src, left_dst, base).wait_send()
            to_right(right_src, right_dst, base + 1).wait_recv()

        @pl.when(me == 0)
        def _():
            right_dst[...] = jnp.zeros(right_dst.shape, BF)

        @pl.when(me < tensors - 1)
        def _():
            to_right(right_src, right_dst, base + 1).wait_send()
            to_left(left_src, left_dst, base).wait_recv()

        @pl.when(me == tensors - 1)
        def _():
            left_dst[...] = jnp.zeros(left_dst.shape, BF)

        for k in range(1, tensors):
            to_peer(k, far_src(k), far_dst(k), base + 1 + k).wait()

    def halos(p):
        block = lambda k: far.at[me, p]
        return (5 * p, edge_l.at[p], halo_r.at[p], edge_r.at[p], halo_l.at[p], block, block)

    lax.fori_loop(0, PAIRS, pooling, 0)
    if fast:
        second.after_z(1, 3)
        third.along_z()

    def attend(p, carry):
        exchanged(*halos(p))
        for which, windows in enumerate((kw, vw)):
            for level in range(LEVELS - 1):
                windows[p, LEFT[level] : LEFT[level] + 16, :] = halo_l[p, which, 16 * level : 16 * level + 16, :]
                windows[p, RIGHT[level] : RIGHT[level] + 16, :] = halo_r[p, which, 16 * level : 16 * level + 16, :]
            groups = jnp.concatenate([far[g, p, which] for g in range(tensors)], axis=0)
            windows[p, FAR:KEYS, :] = groups.astype(BF)
        for k in range(TILES):
            here = slice(64 * k, 64 * k + 64)
            keys = slice(TILE_AT[k], TILE_AT[k] + 128)
            s = nt(both(qb[p, here, :]), kw[p, keys, :])
            w = wt[k]
            w = jnp.concatenate([w, w], axis=0)
            s = jnp.where(w > 0.0, s, -1e30)
            m = jnp.max(s, axis=-1, keepdims=True)
            e = w * jnp.exp(s - m)
            low = e.astype(BF)
            total = jnp.sum(low.astype(F32), axis=-1, keepdims=True)
            eb[p, k] = low
            ns[here, :] = joined(nn(low, vw[p, keys, :]))
            ml[p, here, :] = joined(jnp.broadcast_to(m, (128, 128)))
            ds_[here, :] = joined(jnp.broadcast_to(total, (128, 128)))
            if fast and k == 3:

                @pl.when(p == 1)
                def _():
                    second.after_b(3)
                    second.after_a(0, 1)

                @pl.when(p == 2)
                def _():
                    second.after_a(1, 1)
                    second.after_a(0, 2)
                    third.after_z(1)
                    third.after_a(0, 0)

                @pl.when(p == 3)
                def _():
                    second.after_a(1, 2)
                    third.after_z(2)
                    third.after_b(1)
                    third.after_a(1, 0)

        rows = slice(AT[5], AT[5] + 8)
        num, top, den = ns[rows, :], ml[p, rows, :], ds_[rows, :]
        for level in range(LEVELS - 2, -1, -1):
            n = COUNT[level]
            rows = slice(AT[level], AT[level] + n)
            num, top, den = doubled(tmp_a, num, n // 2), doubled(tmp_b, top, n // 2), doubled(tmp_c, den, n // 2)
            own = ml[p, rows, :]
            both_top = jnp.maximum(own, top)
            left, right = jnp.exp(own - both_top), jnp.exp(top - both_top)
            num = ns[rows, :] * left + num * right
            den = ds_[rows, :] * left + den * right
            top = both_top
        inverse = 1.0 / den
        att[p] = num * inverse
        mm[p] = top
        dacc[p] = inverse
        if fast:

            @pl.when(p == 0)
            def _():
                second.after_z(2)
                second.after_b(1)
                second.after_a(1, 0)

            @pl.when(p == 1)
            def _():
                second.after_b(2)
                second.after_a(0, 3)
                third.after_b(0)

            @pl.when(p == 2)
            def _():
                second.after_a(1, 3)
                third.after_z(3)

            @pl.when(p == 3)
            def _():
                third.after_a(0, 1)
                third.after_b(3)

        return carry

    lax.fori_loop(0, PAIRS, attend, 0)

    if fast:
        second.after_across()
    attb = [att[t].astype(BF) for t in range(PAIRS)]
    branch = []
    for y in range(2):
        total = nt(attb[0], get(wm, 0, y, 0, 128))
        for t in range(1, PAIRS):
            total = total + nt(attb[t], get(wm, t, y, 0, 128))
        branch.append(total)
    branch = jnp.concatenate(branch, axis=1)
    middle = ref["xs"][...] + branch
    n2, r2 = normalised(middle)
    n2s[...] = n2
    n2b = n2.astype(BF)
    n2t = n2b.T
    if fast:
        third.after_b(2)
        third.after_a(0, 3)
        third.after_a(1, 1)
    cotb = ref["cots"][...].astype(BF)
    cott = cotb.T

    acts, slopes = ref["acts"], ref["slopes"]
    for t in range(PAIRS):
        pre = nn(n2b[:, :256], get(wm, t, 0, 128, 640)) + nn(n2b[:, 256:], get(wm, t, 1, 128, 640))
        act, slope = gelu_both(pre)
        act = act.astype(BF)
        acts[t] = act
        slopes[t] = slope
        for y in range(2):
            put(gl, t, y, 0, 512, nn(cott[256 * y : 256 * y + 256, :], act))
        if fast:
            late.across(t, 0, 512, 0)
            if t == 1:
                third.after_a(0, 2)
            if t == 2:
                third.after_a(1, 3)
    if fast:
        third.after_a(1, 2)
        third.after_across()
        late.across_all(late_parts)
    dense, dn2 = [0.0, 0.0], [0.0, 0.0]
    for t in range(PAIRS):
        if fast:
            late.far((1, 3, 2, 0)[t])
        act_grad = nn(cotb[:, :256], get(wl, t, 0, 0, 512)) + nn(cotb[:, 256:], get(wl, t, 1, 0, 512))
        pre_grad = (act_grad * slopes[t]).astype(BF)
        act = acts[t]
        for y in range(2):
            dense[y] = dense[y] + nt(act, get(wl, t, y, 0, 512))
            dn2[y] = dn2[y] + nt(pre_grad, get(wm, t, y, 128, 640))
            put(gm, t, y, 128, 640, nn(n2t[256 * y : 256 * y + 256, :], pre_grad))
        if fast:
            middle_sum.across(t, 128, 640, 0)
    dense = jnp.concatenate(dense, axis=1)
    dn2 = jnp.concatenate(dn2, axis=1)
    result = middle + dense
    out_ref[...] = (mixed(result, False) if fast else result).astype(BF)
    live = (iota((ROWS, 512), 0) + me * ROWS < valid_len).astype(F32)
    small_ref[2:3, :] = jnp.sum(live * result * result, axis=0, keepdims=True)
    small_ref[3:4, :] = jnp.sum(live * branch * branch, axis=0, keepdims=True)
    small_ref[4:5, :] = jnp.sum(live * dense * dense, axis=0, keepdims=True)
    small_ref[5:6, :] = jnp.sum(live, axis=0, keepdims=True)
    small_ref[6:8, :] = jnp.zeros((2, 512), F32)
    n2 = n2s[...]
    small_ref[1:2, :] = jnp.sum(dn2 * n2, axis=0, keepdims=True)
    middle_grad = ref["cots"][...] + norm_back(n2, r2, dn2)
    n2s[...] = middle_grad
    mgb = middle_grad.astype(BF)
    mgt = mgb.T
    for t in range(PAIRS):
        us[t, 0:ROWS, :] = nn(mgb[:, :256], get(wm, t, 0, 0, 128)) + nn(mgb[:, 256:], get(wm, t, 1, 0, 128))
        for y in range(2):
            put(gm, t, y, 0, 128, nn(mgt[256 * y : 256 * y + 256, :], att[t].astype(BF)))
        if fast:
            middle_sum.across(t, 0, 128, 4)
    if fast:
        late.near(1, 3)

    def head_sums(v):
        first = jnp.sum(jnp.where(iota(v.shape, 1) < 64, v, 0.0), axis=-1, keepdims=True)
        second = jnp.sum(jnp.where(iota(v.shape, 1) < 64, 0.0, v), axis=-1, keepdims=True)
        return jnp.where(iota(v.shape, 1) < 64, first, second)

    def attend_back(p, carry):
        up = us.at[p]
        grad, inverse = up[0:ROWS, :], dacc[p]
        delta = head_sums(grad * att[p])
        up[0:ROWS, :] = grad * inverse
        ns[0:ROWS, :] = delta * inverse
        mus[0:ROWS, :] = mm[p]
        for level in range(LEVELS - 1):
            n = COUNT[level + 1]
            after = slice(AT[level + 1], AT[level + 1] + n)
            top_e, top_o = pairs_of(mus, AT[level], n)
            top = jnp.minimum(top_e, top_o)
            fe, fo = jnp.exp(top - top_e), jnp.exp(top - top_o)
            u_e, u_o = pairs_of(up, AT[level], n)
            d_e, d_o = pairs_of(ns, AT[level], n)
            up[after, :] = u_e * fe + u_o * fo
            ns[after, :] = d_e * fe + d_o * fo
            mus[after, :] = top
        for rows in (slice(504, STACK),):
            up[rows, :] = jnp.zeros((8, 128), F32)
            ns[rows, :] = jnp.zeros((8, 128), F32)
            mus[rows, :] = jnp.zeros((8, 128), F32)
        for which in range(2):
            dkw[which * PAIRS + p, 0:512, :] = jnp.zeros((512, 128), F32)
        for k in range(TILES):
            here = slice(64 * k, 64 * k + 64)
            keys = slice(TILE_AT[k], TILE_AT[k] + 128)
            factor = jnp.exp(ml[p, here, :] - mus[here, :])
            g = up[here, :] * factor
            g_high = g.astype(BF)
            g2 = both(g_high)
            g4 = jnp.concatenate([g2, both((g - g_high.astype(F32)).astype(BF))], axis=1)
            v2 = vw[p, keys, :]
            v2 = jnp.concatenate([v2, v2], axis=1)
            h = ns[here, :] * factor
            h2 = jnp.concatenate([h[:, 0:1], h[:, 64:65]], axis=0)
            q2 = both(qb[p, here, :])
            low = eb[p, k]
            d = low.astype(F32) * (nt(g4, v2) - h2)
            d = d.astype(BF)
            dv = tn(low, g2)
            dk = tn(d, q2)
            if k < 6:
                dkw[p, keys, :] = dkw[p, keys, :] + dk
                dkw[PAIRS + p, keys, :] = dkw[PAIRS + p, keys, :] + dv
            else:
                dkw[p, keys, :] = dk
                dkw[PAIRS + p, keys, :] = dv
            dqs[p, here, :] = joined(nn(d, kw[p, keys, :]))
            if fast and k == 3:

                @pl.when(p == 0)
                def _():
                    late.near(2)

                @pl.when(p == 1)
                def _():
                    late.own(outs["l"], 1)
                    middle_sum.far(3)

                @pl.when(p == 2)
                def _():
                    middle_sum.far(2)
                    late.own(outs["l"], 2)

                @pl.when(p == 3)
                def _():
                    late.own(outs["l"], 0)
                    middle_sum.far(0)

        for which in range(2):
            row = which * PAIRS + p
            for level in range(LEVELS - 1):
                part = slice(16 * level, 16 * level + 16)
                back_l[p, which, part, :] = dkw[row, LEFT[level] : LEFT[level] + 16, :].astype(BF)
                back_r[p, which, part, :] = dkw[row, RIGHT[level] : RIGHT[level] + 16, :].astype(BF)
            for g in range(tensors):
                dfar[g, p, which] = dkw[row, FAR + 8 * g : FAR + 8 * g + 8, :]
        exchange(*back(p))
        if fast:

            @pl.when(p == 0)
            def _():
                middle_sum.across_all(middle_parts)
                middle_sum.far(1)
                late.near(0)

            @pl.when(p == 1)
            def _():
                late.own(outs["l"], 3)

            @pl.when(p == 2)
            def _():
                middle_sum.near(1)

            @pl.when(p == 3)
            def _():
                middle_sum.near(3)

        return carry

    def back(p):
        return (
            20 + 5 * p,
            back_l.at[p],
            got_r.at[p],
            back_r.at[p],
            got_l.at[p],
            lambda k: dfar.at[lax.rem(me + k, tensors), p],
            lambda k: gfar.at[k, p],
        )

    lax.fori_loop(0, PAIRS, attend_back, 0)
    def unpool(p, carry):
        exchanged(*back(p))
        factors = stack_factors()
        cur = dqs[p, AT[5] : AT[5] + 8, :] * factors[AT[5] : AT[5] + 8]
        for level in range(LEVELS - 2, -1, -1):
            rows = slice(AT[level], AT[level] + COUNT[level])
            cur = doubled(tmp_a, cur, COUNT[level] // 2) + dqs[p, rows, :] * factors[rows]
        qs[p, 0:ROWS, :] = cur
        for which, raw in enumerate((ks, vs)):
            row = which * PAIRS + p
            raw_p = raw.at[p]
            cur = gfar[1, p, which]
            for k in range(2, tensors):
                cur = cur + gfar[k, p, which]
            cur = cur * rdiv[AT[5] : AT[5] + 8, :]
            for level in range(LEVELS - 2, -1, -1):
                n = COUNT[level]
                rows = slice(AT[level], AT[level] + n)
                part = slice(16 * level, 16 * level + 16)
                if level < 4:
                    raw_p[rows, :] = dkw[row, OWN[level] : OWN[level] + n, :]
                else:
                    raw_p[rows, :] = jnp.zeros((n, 128), F32)
                first = slice(AT[level], AT[level] + 16)
                last = slice(AT[level] + n - 16, AT[level] + n)
                raw_p[first, :] = raw_p[first, :] + got_l[p, which, part, :].astype(F32)
                raw_p[last, :] = raw_p[last, :] + got_r[p, which, part, :].astype(F32)
                cur = doubled(tmp_a, cur, n // 2) + raw_p[rows, :] * rdiv[rows, :]
            raw_p[0:ROWS, :] = cur * (iota((ROWS, 128), 0) + me * ROWS < valid_len).astype(F32)
        return carry

    lax.fori_loop(0, PAIRS, unpool, 0)
    if fast:
        middle_sum.own(outs["m"], 1)

    n1 = n1s[...]
    n1t = n1.astype(BF).T
    dn1 = [0.0, 0.0]
    for t in range(PAIRS):
        joint = jnp.concatenate(
            [qs[t, 0:ROWS, :].astype(BF), ks[t, 0:ROWS, :].astype(BF), vs[t, 0:ROWS, :].astype(BF)], axis=1
        )
        for y in range(2):
            put(ga, t, y, 0, 384, nn(n1t[256 * y : 256 * y + 256, :], joint))
            dn1[y] = dn1[y] + nt(joint, get(wa, t, y, 0, 384))
        if fast:
            early.across(t, 0, 384, 0)
    dn1 = jnp.concatenate(dn1, axis=1)
    small_ref[0:1, :] = jnp.sum(dn1 * n1, axis=0, keepdims=True)
    if fast:
        sums = Remote(ref["sum_send"], ref["sum_recv"])
        got = ref["sums"]
        ways = (at.to_other, at.to_x, at.to_y)

        def sum_send(i):
            got[2 * i] = small_ref[...]
            sums.send(i, got.at[2 * i], got.at[2 * i + 1], ways[i])

        def sum_add(i):
            sums.arrived(i, got.at[2 * i + 1], ways[i])
            small_ref[...] = got[2 * i] + got[2 * i + 1]

        sum_send(0)
        middle_sum.near(2)
        early.across_all(early_parts)
        early.far(1, 3, 2, 0)
        sum_add(0)
        sum_send(1)
        middle_sum.own(outs["m"], 3)
        middle_sum.near(0)
        sum_add(1)
        sum_send(2)
        middle_sum.own(outs["m"], 2)
        early.near(1, 3, 2, 0)
        sum_add(2)
        got[6 + at.z] = small_ref[...]
        for k in range(1, 4):
            sums.send(2 + k, got.at[6 + at.z], got.at[6 + at.z], at.to_z(k))
        middle_sum.own(outs["m"], 0)
        early.own(outs["a"], 1, 3, 2, 0)
    r1 = lax.rsqrt(row_variance(ref["xs"][...]) + EPS)
    in_grad = n2s[...] + norm_back(n1, r1, dn1)
    ingrad_ref[...] = (mixed(in_grad, False) if fast else in_grad).astype(BF)
    if fast:
        late.finish(outs["l"])
        middle_sum.finish(outs["m"])
        outs["m"][:, 128:640] = outs["m"][:, 128:640] * g2c
        early.finish(outs["a"])
        outs["a"][...] = outs["a"][...] * g1c
        for k in range(1, 4):
            sums.arrived(2 + k, got.at[6], at.to_b)
        total = ((got[6] + got[7]) + got[8]) + got[9]
        gains = jnp.zeros((2, 64), F32)
        for i in range(8):
            gains = gains + jnp.where(4 * at.y + at.z == i, total[0:2, 64 * i : 64 * i + 64], 0.0)
        squares = jnp.sum(total[2:6], axis=1, keepdims=True)
        root = jnp.sqrt(squares[0:3] / squares[3:4])
        lanes = iota((1, 128), 1)
        tail = ref["grads"].at[:, 1536:1664]
        tail[...] = jnp.zeros(tail.shape, F32)
        tail[0:1, 0:64] = gains[0:1] / g1
        tail[1:2, 0:64] = gains[1:2] / g2
        tail[2:3, :] = sum(jnp.where(lanes == i, root[i : i + 1], 0.0) for i in range(3))
        for remote, parts in ((early, early_parts), (middle_sum, middle_parts), (late, late_parts)):
            for lo, hi, base in parts:
                remote.across_drain(lo, hi, base)
            remote.drain(remote.r2.at[0], at.to_x)
        for remote in (first, second, third):
            remote.drain(remote.own, at.to_x)
        sums.drain(small_ref, at.to_x)


def row_variance(v):
    centred = v - jnp.mean(v, axis=-1, keepdims=True)
    return jnp.mean(centred * centred, axis=-1, keepdims=True)


def run_layer(fast, tensors, lengths, inputs, cotangent, *weights):
    vmem = pl.BlockSpec(memory_space=pltpu.VMEM)
    f = lambda *shape: pltpu.VMEM(shape, F32)
    b = lambda *shape: pltpu.VMEM(shape, BF)
    full = (2, 2, 2, 4, 64) if fast else (tensors, 2, 256)
    scratch = {
        "qs": f(PAIRS, STACK, 128),
        "ks": f(PAIRS, STACK, 128),
        "vs": f(PAIRS, STACK, 128),
        "qb": b(PAIRS, STACK, 128),
        "kw": b(PAIRS, KEYS, 128),
        "vw": b(PAIRS, KEYS, 128),
        "wt": f(TILES, 64, 128),
        "rdiv": f(STACK, 128),
        "edge_l": b(PAIRS, 2, HALO, 128),
        "edge_r": b(PAIRS, 2, HALO, 128),
        "halo_l": b(PAIRS, 2, HALO, 128),
        "halo_r": b(PAIRS, 2, HALO, 128),
        "far": f(tensors, PAIRS, 2, 8, 128),
        "eb": b(PAIRS, TILES, 128, 128),
        "ns": f(STACK, 128),
        "ml": f(PAIRS, STACK, 128),
        "ds": f(STACK, 128),
        "att": f(PAIRS, ROWS, 128),
        "mm": f(PAIRS, ROWS, 128),
        "tmp_a": f(ROWS, 128),
        "tmp_b": f(ROWS, 128),
        "tmp_c": f(ROWS, 128),
        "xs": f(ROWS, 512),
        "cots": f(ROWS, 512),
        "n1s": f(ROWS, 512),
        "n2s": f(ROWS, 512),
        "dacc": f(PAIRS, ROWS, 128),
        "us": f(PAIRS, STACK, 128),
        "mus": f(STACK, 128),
        "dqs": f(PAIRS, STACK, 128),
        "acts": b(PAIRS, ROWS, 512),
        "slopes": f(PAIRS, ROWS, 512),
        "dkw": f(2 * PAIRS, KEYS, 128),
        "back_l": b(PAIRS, 2, HALO, 128),
        "back_r": b(PAIRS, 2, HALO, 128),
        "got_l": b(PAIRS, 2, HALO, 128),
        "got_r": b(PAIRS, 2, HALO, 128),
        "dfar": f(tensors, PAIRS, 2, 8, 128),
        "gfar": f(tensors, PAIRS, 2, 8, 128),
        "send_sem": pltpu.SemaphoreType.DMA((40,)),
        "recv_sem": pltpu.SemaphoreType.DMA((40,)),
    }
    if fast:
        ins = ("lengths", *("in_" + n for n in ("x", "cot", "q", "k", "v", "o", "w1", "part_l", "g1", "g2")))
        outs = {"rows": ((ROWS, 1024), BF), "grads": ((64, 1664), F32)}
        scratch |= {n: b(*shape) for n, shape in LOADS}
        scratch |= {"in_sem": pltpu.SemaphoreType.DMA((len(LOADS),))}
        scratch |= {"part_a": b(64, 384), "part_m": b(64, 640), "small": f(8, 512)}
        for name, c in zip("aml", (384, 640, 512), strict=True):
            scratch |= {
                "w" + name: b(*full, c),
                "g" + name: b(*full, c),
                name + "0": b(2, 2, 4, 64, c),
                name + "1": b(2, 4, 64, c),
                name + "2": b(4, 64, c),
                name + "3": b(3, 64, c),
            }
        scratch |= {
            "sums": f(10, 8, 512),
            "gather_send": pltpu.SemaphoreType.DMA((3, 31)),
            "gather_recv": pltpu.SemaphoreType.DMA((3, 31)),
            "reduce_send": pltpu.SemaphoreType.DMA((3, 23)),
            "reduce_recv": pltpu.SemaphoreType.DMA((3, 23)),
            "sum_send": pltpu.SemaphoreType.DMA((6,)),
            "sum_recv": pltpu.SemaphoreType.DMA((6,)),
        }
    else:
        ins = ("lengths", "x", "cot", "wa", "wm", "wl")
        outs = {"out": ((ROWS, 512), BF), "ingrad": ((ROWS, 512), BF), "small": ((8, 512), F32)}
        outs |= {"g" + name: (w.shape, BF) for name, w in zip("aml", weights, strict=True)}
    return pl.pallas_call(
        functools.partial(layer_kernel, fast, tensors, (*ins, *outs, *scratch)),
        out_shape=tuple(jax.ShapeDtypeStruct(*shape) for shape in outs.values()),
        in_specs=[pl.BlockSpec(memory_space=pltpu.SMEM)] + [pl.BlockSpec(memory_space=pltpu.HBM) if fast else vmem] * (len(ins) - 1),
        out_specs=(vmem,) * len(outs),
        scratch_shapes=list(scratch.values()),
        compiler_params=pltpu.CompilerParams(
            collective_id=0, has_side_effects=True, vmem_limit_bytes=62 * 1024 * 1024
        ),
        name="layer",
    )(lengths, inputs, cotangent, *weights)


def hand_out_kernel(rows, grads, *refs):
    outs, tail, sem = refs[:11], refs[11], refs[12]
    edges = (0, 128, 256, 384, 512, 1024, 1536)
    parts = [rows.at[:, 0:512], rows.at[:, 512:1024]]
    parts += [grads.at[:, lo:hi] for lo, hi in zip(edges, edges[1:])]
    copies = [pltpu.make_async_copy(grads.at[0:8, 1536:1664], tail, sem.at[8])]
    copies += [pltpu.make_async_copy(part, out, sem.at[i]) for i, (part, out) in enumerate(zip(parts, outs))]
    for copy in copies:
        copy.start()
    copies[0].wait()
    for i in range(3):
        outs[8 + i][...] = tail[i, 0 : outs[8 + i].shape[0]]
    for copy in copies[1:]:
        copy.wait()


def hand_out(rows, grads):
    shapes = [(ROWS, 512)] * 2 + [(64, 128)] * 4 + [(64, 512)] * 2 + [(64,)] * 2 + [(3,)]
    return pl.pallas_call(
        hand_out_kernel,
        out_shape=tuple(jax.ShapeDtypeStruct(shape, BF if i < 2 else F32) for i, shape in enumerate(shapes)),
        in_specs=[pl.BlockSpec(memory_space=pltpu.HBM)] * 2,
        out_specs=tuple(pl.BlockSpec(memory_space=pltpu.VMEM) for _ in shapes),
        scratch_shapes=[pltpu.VMEM((8, 128), F32), pltpu.SemaphoreType.DMA((9,))],
        name="hand_out",
    )(rows, grads)


def per_device(
    fast,
    inputs,
    lengths,
    cotangent,
    query_weight,
    key_weight,
    value_weight,
    output_weight,
    inner_weight,
    outer_weight,
    first_gain,
    second_gain,
):
    tensors = lax.axis_size("tensor")
    everyone = ("tensor", "dp")
    if fast:
        rows, grads = run_layer(
            fast,
            tensors,
            lengths,
            inputs,
            cotangent,
            query_weight,
            key_weight,
            value_weight,
            output_weight.T,
            inner_weight,
            outer_weight.T,
            first_gain,
            second_gain,
        )
        out, input_grad, gq, gk, gv, go, gi, gl, gain_one, gain_two, root = hand_out(rows, grads)
        return out, input_grad, gq, gk, gv, go.T, gi, gl.T, gain_one, gain_two, root
    g1 = first_gain.astype(F32)[:, None]
    g2 = second_gain.astype(F32)[:, None]
    scaled = lambda g, w: (g * w.astype(F32)).astype(BF)
    part_a = scaled(g1, jnp.concatenate([query_weight, key_weight, value_weight], axis=1))
    part_m = jnp.concatenate([output_weight.T, scaled(g2, inner_weight)], axis=1)
    parts = (part_a, part_m, outer_weight.T)
    full = [lax.all_gather(p, everyone, axis=0, tiled=True).reshape(tensors, 2, 256, -1) for p in parts]
    out, input_grad, small, *grads = run_layer(fast, tensors, lengths, inputs, cotangent, *full)

    def reduced(g):
        return lax.psum_scatter(
            g.reshape(tensors * 512, g.shape[-1]).astype(F32), everyone, scatter_dimension=0, tiled=True
        )

    ga, gm, gl = (reduced(g) for g in grads)
    small = lax.psum(small, everyone)
    width = first_gain.shape[0]
    gains = lax.dynamic_slice(small, (0, lax.axis_index("dp") * width), (2, width))
    sums = jnp.sum(small, axis=1)
    root_mean_squares = jnp.sqrt(sums[2:5] / sums[5])
    ga = ga * g1
    return (
        out,
        input_grad,
        ga[:, 0:128],
        ga[:, 128:256],
        ga[:, 256:384],
        gm[:, 0:128].T,
        gm[:, 128:640] * g2,
        gl.T,
        gains[0] / first_gain.astype(F32),
        gains[1] / second_gain.astype(F32),
        root_mean_squares,
    )


def solution(mesh):
    fast = (mesh.shape["dp"], mesh.shape["tensor"]) == (8, 4)
    return jax.shard_map(
        functools.partial(per_device, fast),
        mesh=mesh,
        in_specs=(
            P(("dp", "tensor"), None),
            P("dp"),
            P(("dp", "tensor"), None),
            P("dp", "tensor"),
            P("dp", "tensor"),
            P("dp", "tensor"),
            P("tensor", "dp"),
            P("dp", "tensor"),
            P("tensor", "dp"),
            P("dp"),
            P("dp"),
        ),
        out_specs=(
            P(("dp", "tensor"), None),
            P(("dp", "tensor"), None),
            P("dp", "tensor"),
            P("dp", "tensor"),
            P("dp", "tensor"),
            P("tensor", "dp"),
            P("dp", "tensor"),
            P("tensor", "dp"),
            P("dp"),
            P("dp"),
            P(),
        ),
        check_vma=False,
    )
```

```python
import functools

import jax
import jax.numpy as jnp
from jax import lax
from jax.experimental import pallas as pl
from jax.experimental.pallas import tpu as pltpu
from jax.sharding import PartitionSpec as P

MESH = pl.DeviceIdType.MESH
F32, BF = jnp.float32, jnp.bfloat16
HEAD_DIM = 64
EPS = 1e-05

ROWS, PAIRS, LEVELS = 256, 4, 6
COUNT = (256, 128, 64, 32, 16, 8)
AT = (0, 256, 384, 448, 480, 496)
STACK = 512
OWN = (32, 352, 544, 656)
LEFT = (16, 336, 528, 640, 704)
RIGHT = (288, 480, 608, 688, 720)
FAR = 736
KEYS = 768
BLANK = ((0, 16), (304, 32), (496, 32), (624, 16))
TILE_AT = (0, 64, 128, 192, 320, 384, 512, 640)
TILES = 8
HALO = 80
LOADS = (
    ("g1", (64,)),
    ("g2", (64,)),
    ("q", (64, 128)),
    ("k", (64, 128)),
    ("v", (64, 128)),
    ("o", (64, 128)),
    ("w1", (64, 512)),
    ("part_l", (64, 512)),
    ("x", (ROWS, 512)),
    ("cot", (ROWS, 512)),
)


def nn(a, b):
    return lax.dot_general(a, b, (((1,), (0,)), ((), ())), preferred_element_type=F32)


def nt(a, b):
    return lax.dot_general(a, b, (((1,), (1,)), ((), ())), preferred_element_type=F32)


def tn(a, b):
    return lax.dot_general(a, b, (((0,), (0,)), ((), ())), preferred_element_type=F32)


def iota(shape, dim):
    return lax.broadcasted_iota(jnp.int32, shape, dim)


def level_counts(index, level, total, valid_len):
    factor = 1 << level
    c = jnp.clip(valid_len - index * factor, 0, factor)
    return jnp.where((index >= 0) & (index < total), c, 0).astype(F32)


def tile_weights(k, me, tensors, valid_len):
    i, j = iota((64, 128), 0), iota((64, 128), 1)
    if k < 7:
        level = 0 if k < 4 else 1 if k < 6 else 2
        first = 64 * (k - AT[level] // 64)
        n = COUNT[level]
        c = level_counts(me * n + first - 32 + j, level, n * tensors, valid_len)
        near = jnp.abs((i >> 4) - (j >> 4) + 2) <= 1
        if level:
            near = near & (jnp.abs((i >> 3) - (j >> 3) + 4) > 1)
        return jnp.where(near, c, 0.0)
    c3 = level_counts(me * 32 + j - 16, 3, 32 * tensors, valid_len)
    near3 = (jnp.abs((i >> 4) - (j >> 4) + 1) <= 1) & (jnp.abs((i >> 3) - (j >> 3) + 2) > 1)
    near3 = near3 & (i < 32) & (j < 64)
    key4 = jnp.where(j < 80, j - 80, j - 64)
    c4 = level_counts(me * 16 + key4, 4, 16 * tensors, valid_len)
    near4 = (jnp.abs(((i - 32) >> 3) - (key4 >> 3)) > 1) & (i >= 32) & (i < 48) & (j >= 64) & (j < 96)
    key5 = j - 96
    c5 = level_counts(key5, 5, 8 * tensors, valid_len)
    near5 = (jnp.abs(me - (key5 >> 3)) > 1) & (i >= 48) & (i < 56) & (j >= 96)
    return jnp.where(near3, c3, 0.0) + jnp.where(near4, c4, 0.0) + jnp.where(near5, c5, 0.0)


def row_divisors(me, tensors, valid_len):
    i = iota((STACK, 128), 0)
    out = jnp.ones((STACK, 128), F32)
    for level in range(1, LEVELS):
        c = level_counts(i - AT[level] + me * COUNT[level], level, COUNT[level] * tensors, valid_len)
        here = (i >= AT[level]) & (i < AT[level] + COUNT[level])
        out = jnp.where(here, 1.0 / jnp.maximum(c, 1.0), out)
    return out


def stack_factors():
    i = iota((STACK, 128), 0)
    out = jnp.full((STACK, 128), HEAD_DIM ** (-0.5), F32)
    for level in range(1, LEVELS):
        out = jnp.where(i >= AT[level], HEAD_DIM ** (-0.5) / (1 << level), out)
    return out


def pairs_of(ref, start, n):
    return ref[pl.ds(start, n, stride=2), :], ref[pl.ds(start + 1, n, stride=2), :]


def pool(ref):
    for level in range(LEVELS - 1):
        n = COUNT[level + 1]
        even, odd = pairs_of(ref, AT[level], n)
        ref[AT[level + 1] : AT[level + 1] + n, :] = even + odd


def doubled(ref, value, n):
    ref[pl.ds(0, n, stride=2), :] = value
    ref[pl.ds(1, n, stride=2), :] = value
    return ref[0 : 2 * n, :]


def normalised(v):
    centred = v - jnp.mean(v, axis=-1, keepdims=True)
    r = lax.rsqrt(jnp.mean(centred * centred, axis=-1, keepdims=True) + EPS)
    return centred * r, r


def norm_back(n, r, hg):
    return r * (hg - jnp.mean(hg, axis=-1, keepdims=True) - n * jnp.mean(hg * n, axis=-1, keepdims=True))


def gelu_both(u):
    c = 0.7978845608028654
    square = u * u
    th = jnp.tanh(c * (u + 0.044715 * (square * u)))
    half = 0.5 * (1.0 + th)
    slope = half + (0.5 * c) * u * (1.0 - th * th) * (1.0 + 0.134145 * square)
    return u * half, slope


class Place:
    def __init__(self):
        self.d, self.t = lax.axis_index("dp"), lax.axis_index("tensor")
        self.z, self.y = self.d // 2, self.d % 2
        self.x, self.c = self.t // 2, self.t % 2
        self.a = self.x + self.c * (self.y - self.x)
        self.b = self.y + self.c * (self.x - self.y)
        flip_x, flip_y = 2 - 4 * self.x, 1 - 2 * self.y
        self.to_x, self.to_y = (self.d, self.t + flip_x), (self.d + flip_y, self.t)
        self.to_a = (self.d + self.c * flip_y, self.t + (1 - self.c) * flip_x)
        self.to_b = (self.d + (1 - self.c) * flip_y, self.t + self.c * flip_x)
        self.to_other = (self.d, self.t + 1 - 2 * self.c)
        self.to_across = (self.d, 3 - self.t)

    def to_z(self, k):
        return (2 * ((self.z + k) % 4) + self.y, self.t)


def flipped(bit, by):
    return 1 - bit if by else bit


class Remote:
    def __init__(self, send_sem, recv_sem):
        self.send_sem, self.recv_sem, self.started = send_sem, recv_sem, set()

    def copy(self, i, src, dst, to):
        return pltpu.make_async_remote_copy(
            src, dst, self.send_sem.at[i], self.recv_sem.at[i], device_id=to, device_id_type=MESH
        )

    def send(self, i, src, dst, to):
        self.copy(i, src, dst, to).start()
        self.started.add(i)

    def arrived(self, i, dst, to):
        self.copy(i, dst, dst, to).wait_recv()

    def drain(self, like, to):
        for i in sorted(self.started):
            self.copy(i, like, like, to).wait_send()


class Gather(Remote):
    def __init__(self, at, own, w, send_sem, recv_sem):
        super().__init__(send_sem, recv_sem)
        self.at, self.own, self.w = at, own, w

    def shard(self, j, aa=0, bb=0, plane=0):
        at = self.at
        a, b = (at.b, at.a) if plane else (at.a, at.b)
        return self.w.at[flipped(at.c, plane), flipped(a, aa), flipped(b, bb), (at.z + 4 - j) % 4]

    def source(self, j, aa=0, bb=0):
        return self.own if (j, aa, bb) == (0, 0, 0) else self.shard(j, aa, bb)

    def along_z(self):
        for k in (1, 3, 2):
            self.send(k - 1, self.own, self.shard(0), self.at.to_z(k))

    def along_b(self, j):
        self.send(3 + j, self.source(j), self.shard(j), self.at.to_b)

    def along_a(self, j, bb):
        self.send(7 + 4 * bb + j, self.source(j, 0, bb), self.shard(j, 0, bb), self.at.to_a)

    def across(self, j, aa, bb):
        self.send(15 + 8 * aa + 4 * bb + j, self.source(j, aa, bb), self.shard(j, aa, bb), self.at.to_other)

    def own_on(self, met=True):
        self.along_b(0)
        self.along_a(0, 0)
        if met:
            self.across(0, 0, 0)

    def after_z(self, *js, met=True):
        for j in js:
            self.arrived(j - 1, self.shard(j), self.at.to_b)
            self.along_b(j)
            self.along_a(j, 0)
            if met:
                self.across(j, 0, 0)

    def after_b(self, *js, met=True):
        for j in js:
            self.arrived(3 + j, self.shard(j, 0, 1), self.at.to_b)
            self.along_a(j, 1)
            if met:
                self.across(j, 0, 1)

    def after_a(self, bb, *js):
        for j in js:
            self.arrived(7 + 4 * bb + j, self.shard(j, 1, bb), self.at.to_b)
            self.across(j, 1, bb)

    def after_across(self):
        for aa in range(2):
            for bb in range(2):
                for j in range(4):
                    self.arrived(15 + 8 * aa + 4 * bb + j, self.shard(j, aa, bb, 1), self.at.to_b)


class Reduce(Remote):
    def __init__(self, at, g, r0, r1, r2, r3, send_sem, recv_sem):
        super().__init__(send_sem, recv_sem)
        self.at, self.g, self.r0, self.r1, self.r2, self.r3 = at, g, r0, r1, r2, r3

    def across(self, t, lo, hi, base):
        @pl.when(self.at.c != t % 2)
        def _():
            for a, b in ((t // 2, 0), (t // 2, 1)) if t % 2 == 0 else ((0, t // 2), (1, t // 2)):
                self.copy(
                    base + 2 * a + b,
                    self.g.at[t % 2, a, b, :, :, lo:hi],
                    self.r0.at[a, b, :, :, lo:hi],
                    self.at.to_other,
                ).start()

    def across_wait(self, a, b, lo, hi, base):
        piece = self.r0.at[a, b, :, :, lo:hi]
        copy = self.copy(base + 2 * a + b, piece, piece, self.at.to_other)
        copy.wait_recv()

    def across_drain(self, lo, hi, base):
        for i in range(4):
            piece = self.r0.at[i // 2, i % 2, :, :, lo:hi]
            self.copy(base + i, piece, piece, self.at.to_other).wait_send()

    def across_all(self, parts):
        for a in range(2):
            for b in range(2):
                for lo, hi, base in parts:
                    self.across_wait(a, b, lo, hi, base)

    def far(self, *js):
        at = self.at
        for j in js:
            z = (at.z + j) % 4
            for bb in (1, 0):
                b = flipped(at.b, bb)
                here = self.g.at[at.c, 1 - at.a, b, z]
                here[...] = (here[...].astype(F32) + self.r0[1 - at.a, b, z].astype(F32)).astype(BF)
                self.send(8 + 4 * bb + j, here, self.r1.at[b, z], at.to_a)

    def near(self, *js):
        at = self.at
        b = 1 - at.b
        for j in js:
            z = (at.z + j) % 4
            here = self.g.at[at.c, at.a, b, z]
            self.arrived(12 + j, self.r1.at[b, z], at.to_a)
            total = here[...].astype(F32) + self.r0[at.a, b, z].astype(F32) + self.r1[b, z].astype(F32)
            here[...] = total.astype(BF)
            self.send(16 + j, here, self.r2.at[z], at.to_b)

    def own(self, out, *js):
        at = self.at
        b = at.b
        for j in js:
            z = (at.z + j) % 4
            here = self.g.at[at.c, at.a, b, z]
            self.arrived(8 + j, self.r1.at[b, z], at.to_a)
            self.arrived(16 + j, self.r2.at[z], at.to_b)
            total = here[...].astype(F32) + self.r0[at.a, b, z].astype(F32)
            total = total + self.r1[b, z].astype(F32) + self.r2[z].astype(F32)
            if j:
                here[...] = total.astype(BF)
                self.send(20 + j - 1, here, self.r3.at[j - 1], at.to_z(j))
            else:
                out[...] = total

    def finish(self, out):
        for k in (1, 3, 2):
            self.arrived(20 + k - 1, self.r3.at[k - 1], self.at.to_b)
        total = out[...] + self.r3[0].astype(F32)
        out[...] = total + self.r3[1].astype(F32) + self.r3[2].astype(F32)


def mixed(v, into):
    tiles = [v[:, 128 * i : 128 * i + 128] for i in range(4)]
    rolled = [pltpu.roll(tile, 64, 1) for tile in tiles]
    low = iota(tiles[0].shape, 1) < 64
    if into:
        pairs = ((0, 1, 0), (2, 3, 0), (0, 1, 1), (2, 3, 1))
    else:
        pairs = ((0, 2, 0), (0, 2, 1), (1, 3, 0), (1, 3, 1))
    out = []
    for i, k, high in pairs:
        out.append(jnp.where(low, rolled[i], tiles[k]) if high else jnp.where(low, tiles[i], rolled[k]))
    return jnp.concatenate(out, axis=1)


def layer_kernel(fast, tensors, names, *refs):
    ref = dict(zip(names, refs, strict=True))
    if fast:
        loads = {
            n: pltpu.make_async_copy(ref["in_" + n], ref[n], ref["in_sem"].at[i]) for i, (n, _) in enumerate(LOADS)
        }
        for load in loads.values():
            load.start()
    me = lax.axis_index("tensor")
    valid_len = ref["lengths"][0]
    barrier = pltpu.get_barrier_semaphore()
    if fast:
        at = Place()
        same = [at.to_z(1), at.to_z(2), at.to_z(3), at.to_y, at.to_x]
        others = [at.to_other, at.to_across]
        for peer in same:
            pl.semaphore_signal(barrier, inc=1, device_id=peer, device_id_type=MESH)

        @pl.when(at.c == 0)
        def _():
            for peer in others:
                pl.semaphore_signal(barrier, inc=1, device_id=peer, device_id_type=MESH)
    else:
        peers = [{"tensor": lax.rem(me + k, tensors)} for k in range(1, tensors)]
        for peer in peers:
            pl.semaphore_signal(barrier, inc=1, device_id=peer, device_id_type=MESH)
    len_ref, x_ref, cot_ref = (ref[n] for n in ("lengths", "x", "cot"))
    if fast:
        out_ref, ingrad_ref = ref["rows"].at[:, 0:512], ref["rows"].at[:, 512:1024]
        outs = {"a": ref["grads"].at[:, 0:384], "m": ref["grads"].at[:, 384:1024], "l": ref["grads"].at[:, 1024:1536]}
        for n, _ in LOADS[:8]:
            loads[n].wait()
        g1, g2 = (ref[n][...].astype(F32).reshape(1, 64) for n in ("g1", "g2"))
        column = lambda g: jnp.sum(jnp.where(iota((64, 64), 0) == iota((64, 64), 1), g, 0.0), axis=1, keepdims=True)
        g1c, g2c = column(g1), column(g2)
        for i, n in enumerate("qkv"):
            ref["part_a"][:, 128 * i : 128 * i + 128] = (g1c * ref[n][...].astype(F32)).astype(BF)
        ref["part_m"][:, 0:128] = ref["o"][...]
        ref["part_m"][:, 128:640] = (g2c * ref["w1"][...].astype(F32)).astype(BF)
    else:
        out_ref, ingrad_ref = ref["out"], ref["ingrad"]
    qs, ks, vs, qb, kw, vw, wt, rdiv = (ref[n] for n in ("qs", "ks", "vs", "qb", "kw", "vw", "wt", "rdiv"))
    edge_l, edge_r, halo_l, halo_r, far = (ref[n] for n in ("edge_l", "edge_r", "halo_l", "halo_r", "far"))
    eb, ns, ml, ds_, att, mm = (ref[n] for n in ("eb", "ns", "ml", "ds", "att", "mm"))
    tmp_a, tmp_b, tmp_c, n1s, n2s, dacc = (ref[n] for n in ("tmp_a", "tmp_b", "tmp_c", "n1s", "n2s", "dacc"))
    us, mus, dqs, dkw = (ref[n] for n in ("us", "mus", "dqs", "dkw"))
    back_l, back_r, got_l, got_r, dfar, gfar = (
        ref[n] for n in ("back_l", "back_r", "got_l", "got_r", "dfar", "gfar")
    )
    send_sem, recv_sem, small_ref = ref["send_sem"], ref["recv_sem"], ref["small"]
    ga, gm, gl = ref["ga"], ref["gm"], ref["gl"]
    wa, wm, wl = ref["wa"], ref["wm"], ref["wl"]

    def view(r, t, y):
        if not fast:
            return r.at[t, y]
        return r.at[0, t // 2, y] if t % 2 == 0 else r.at[1, y, t // 2]

    def get(r, t, y, lo, hi):
        return view(r, t, y)[..., lo:hi].reshape(256, hi - lo)

    def put(r, t, y, lo, hi, value):
        v = view(r, t, y)
        v[..., lo:hi] = value.astype(BF).reshape(*v.shape[:-1], hi - lo)

    if fast:
        @pl.when(at.c == 0)
        def _():
            pl.semaphore_wait(barrier, len(same))

        @pl.when(at.c == 1)
        def _():
            pl.semaphore_wait(barrier, len(same) + len(others))
            for peer in others:
                pl.semaphore_signal(ref["ready"], inc=1, device_id=peer, device_id_type=MESH)

        first, second, third = (
            Gather(at, ref["part_" + n], ref["w" + n], ref["gather_send"].at[i], ref["gather_recv"].at[i])
            for i, n in enumerate("aml")
        )
        early, middle_sum, late = (
            Reduce(
                at,
                ref["g" + n],
                *(ref[n + str(k)] for k in range(4)),
                ref["reduce_send"].at[i],
                ref["reduce_recv"].at[i],
            )
            for i, n in enumerate("aml")
        )
        early_parts, middle_parts, late_parts = ((0, 384, 0),), ((128, 640, 0), (0, 128, 4)), ((0, 512, 0),)
        first.along_z()
        first.own_on(met=False)
        second.along_z()
        second.own_on(met=False)
        third.along_z()
        for n in "aml":
            ref["w" + n][at.c, at.a, at.b, at.z] = ref["part_" + n][...]

    else:
        pl.semaphore_wait(barrier, len(peers))

    lane = iota((64, 128), 1)
    low_lanes = lane < 64
    low_b = low_lanes.astype(F32).astype(BF)
    high_b = (1.0 - low_lanes.astype(F32)).astype(BF)

    def both(v):
        return jnp.concatenate([v * low_b, v * high_b], axis=0)

    def joined(v):
        return jnp.where(low_lanes, v[:64], v[64:])

    if fast:
        loads["x"].wait()
        loads["cot"].wait()
    x = x_ref[...].astype(F32)
    cot = cot_ref[...].astype(F32)
    if fast:
        x, cot = mixed(x, True), mixed(cot, True)
    ref["xs"][...] = x
    ref["cots"][...] = cot
    n1, r1 = normalised(x)
    n1s[...] = n1
    n1b = n1.astype(BF)
    valid = (iota((ROWS, 128), 0) + me * ROWS < valid_len).astype(F32)
    rdiv[...] = row_divisors(me, tensors, valid_len)
    for k in range(TILES):
        wt[k] = tile_weights(k, me, tensors, valid_len)
    if fast:
        first.after_z(1, 3, 2, met=False)
        first.after_b(0, 1, 3, 2, met=False)
        second.after_b(0, met=False)

        @pl.when(at.c == 0)
        def _():
            pl.semaphore_wait(ref["ready"], len(others))

        for j in range(4):
            first.across(j, 0, 0)
        for j in range(4):
            first.across(j, 0, 1)
        second.across(0, 0, 0)
        second.across(0, 0, 1)
        first.after_a(0, 0, 1, 3, 2)
        first.after_a(1, 0, 1, 3, 2)
        second.after_z(1, 3, 2)
        first.after_across()
    for t in range(PAIRS):
        joint = nn(n1b[:, :256], get(wa, t, 0, 0, 384)) + nn(n1b[:, 256:], get(wa, t, 1, 0, 384))
        joint = joint.astype(BF).astype(F32)
        qs[t, 0:ROWS, :] = joint[:, :128]
        ks[t, 0:ROWS, :] = joint[:, 128:256] * valid
        vs[t, 0:ROWS, :] = joint[:, 256:] * valid

    def pooling(p, carry):
        pool(qs.at[p])
        qs[p, 504:STACK, :] = jnp.zeros((8, 128), F32)
        qb[p] = (qs[p] * stack_factors()).astype(BF)
        for which, (raw, windows) in enumerate(((ks, kw), (vs, vw))):
            raw_p = raw.at[p]
            pool(raw_p)
            for start, n in BLANK:
                windows[p, start : start + n, :] = jnp.zeros((n, 128), BF)
            for level in range(LEVELS - 1):
                n = COUNT[level]
                rows = slice(AT[level], AT[level] + n)
                coarse = (raw_p[rows, :] * rdiv[rows, :]).astype(BF)
                if level < 4:
                    windows[p, OWN[level] : OWN[level] + n, :] = coarse
                edge_l[p, which, 16 * level : 16 * level + 16, :] = coarse[:16]
                edge_r[p, which, 16 * level : 16 * level + 16, :] = coarse[n - 16 :]
            rows = slice(AT[5], AT[5] + 8)
            far[me, p, which] = raw_p[rows, :] * rdiv[rows, :]
        exchange(*halos(p))
        return carry

    def to_left(src, dst, sem):
        return pltpu.make_async_remote_copy(
            src, dst, send_sem.at[sem], recv_sem.at[sem], device_id={"tensor": jnp.maximum(me - 1, 0)}, device_id_type=MESH
        )

    def to_right(src, dst, sem):
        return pltpu.make_async_remote_copy(
            src,
            dst,
            send_sem.at[sem],
            recv_sem.at[sem],
            device_id={"tensor": jnp.minimum(me + 1, tensors - 1)},
            device_id_type=MESH,
        )

    def to_peer(k, src, dst, sem):
        return pltpu.make_async_remote_copy(
            src, dst, send_sem.at[sem], recv_sem.at[sem], device_id={"tensor": lax.rem(me + k, tensors)}, device_id_type=MESH
        )

    def exchange(base, left_src, left_dst, right_src, right_dst, far_src, far_dst):
        for k in range(1, tensors):
            to_peer(k, far_src(k), far_dst(k), base + 1 + k).start()

        @pl.when(me > 0)
        def _():
            to_left(left_src, left_dst, base).start()

        @pl.when(me < tensors - 1)
        def _():
            to_right(right_src, right_dst, base + 1).start()

    def exchanged(base, left_src, left_dst, right_src, right_dst, far_src, far_dst):
        @pl.when(me > 0)
        def _():
            to_left(left_src, left_dst, base).wait_send()
            to_right(right_src, right_dst, base + 1).wait_recv()

        @pl.when(me == 0)
        def _():
            right_dst[...] = jnp.zeros(right_dst.shape, BF)

        @pl.when(me < tensors - 1)
        def _():
            to_right(right_src, right_dst, base + 1).wait_send()
            to_left(left_src, left_dst, base).wait_recv()

        @pl.when(me == tensors - 1)
        def _():
            left_dst[...] = jnp.zeros(left_dst.shape, BF)

        for k in range(1, tensors):
            to_peer(k, far_src(k), far_dst(k), base + 1 + k).wait()

    def halos(p):
        block = lambda k: far.at[me, p]
        return (5 * p, edge_l.at[p], halo_r.at[p], edge_r.at[p], halo_l.at[p], block, block)

    lax.fori_loop(0, PAIRS, pooling, 0)
    if fast:
        second.after_b(1, 3, 2)
        third.own_on()
        third.after_z(1, 3, 2)

    def attend(p, carry):
        exchanged(*halos(p))
        for which, windows in enumerate((kw, vw)):
            for level in range(LEVELS - 1):
                windows[p, LEFT[level] : LEFT[level] + 16, :] = halo_l[p, which, 16 * level : 16 * level + 16, :]
                windows[p, RIGHT[level] : RIGHT[level] + 16, :] = halo_r[p, which, 16 * level : 16 * level + 16, :]
            groups = jnp.concatenate([far[g, p, which] for g in range(tensors)], axis=0)
            windows[p, FAR:KEYS, :] = groups.astype(BF)
        for k in range(TILES):
            here = slice(64 * k, 64 * k + 64)
            keys = slice(TILE_AT[k], TILE_AT[k] + 128)
            s = nt(both(qb[p, here, :]), kw[p, keys, :])
            w = wt[k]
            w = jnp.concatenate([w, w], axis=0)
            s = jnp.where(w > 0.0, s, -1e30)
            m = jnp.max(s, axis=-1, keepdims=True)
            e = w * jnp.exp(s - m)
            low = e.astype(BF)
            total = jnp.sum(low.astype(F32), axis=-1, keepdims=True)
            eb[p, k] = low
            ns[here, :] = joined(nn(low, vw[p, keys, :]))
            ml[p, here, :] = joined(jnp.broadcast_to(m, (128, 128)))
            ds_[here, :] = joined(jnp.broadcast_to(total, (128, 128)))
        rows = slice(AT[5], AT[5] + 8)
        num, top, den = ns[rows, :], ml[p, rows, :], ds_[rows, :]
        for level in range(LEVELS - 2, -1, -1):
            n = COUNT[level]
            rows = slice(AT[level], AT[level] + n)
            num, top, den = doubled(tmp_a, num, n // 2), doubled(tmp_b, top, n // 2), doubled(tmp_c, den, n // 2)
            own = ml[p, rows, :]
            both_top = jnp.maximum(own, top)
            left, right = jnp.exp(own - both_top), jnp.exp(top - both_top)
            num = ns[rows, :] * left + num * right
            den = ds_[rows, :] * left + den * right
            top = both_top
        inverse = 1.0 / den
        att[p] = num * inverse
        mm[p] = top
        dacc[p] = inverse
        if fast:

            @pl.when(p == 0)
            def _():
                second.after_a(0, 0, 1, 3, 2)

            @pl.when(p == 1)
            def _():
                third.after_b(0, 1, 3, 2)

            @pl.when(p == 2)
            def _():
                second.after_a(1, 0, 1, 3, 2)

            @pl.when(p == 3)
            def _():
                third.after_a(0, 0, 1, 3, 2)

        return carry

    lax.fori_loop(0, PAIRS, attend, 0)

    if fast:
        second.after_across()
    attb = [att[t].astype(BF) for t in range(PAIRS)]
    branch = []
    for y in range(2):
        total = nt(attb[0], get(wm, 0, y, 0, 128))
        for t in range(1, PAIRS):
            total = total + nt(attb[t], get(wm, t, y, 0, 128))
        branch.append(total)
    branch = jnp.concatenate(branch, axis=1)
    middle = ref["xs"][...] + branch
    n2, r2 = normalised(middle)
    n2s[...] = n2
    n2b = n2.astype(BF)
    n2t = n2b.T
    cotb = ref["cots"][...].astype(BF)
    cott = cotb.T

    acts, slopes = ref["acts"], ref["slopes"]
    for t in range(PAIRS):
        pre = nn(n2b[:, :256], get(wm, t, 0, 128, 640)) + nn(n2b[:, 256:], get(wm, t, 1, 128, 640))
        act, slope = gelu_both(pre)
        act = act.astype(BF)
        acts[t] = act
        slopes[t] = slope
        for y in range(2):
            put(gl, t, y, 0, 512, nn(cott[256 * y : 256 * y + 256, :], act))
        if fast:
            late.across(t, 0, 512, 0)
    if fast:
        third.after_a(1, 0, 1, 3, 2)
        third.after_across()
        late.across_all(late_parts)
    dense, dn2 = [0.0, 0.0], [0.0, 0.0]
    for t in range(PAIRS):
        if fast:
            late.far((1, 3, 2, 0)[t])
        act_grad = nn(cotb[:, :256], get(wl, t, 0, 0, 512)) + nn(cotb[:, 256:], get(wl, t, 1, 0, 512))
        pre_grad = (act_grad * slopes[t]).astype(BF)
        act = acts[t]
        for y in range(2):
            dense[y] = dense[y] + nt(act, get(wl, t, y, 0, 512))
            dn2[y] = dn2[y] + nt(pre_grad, get(wm, t, y, 128, 640))
            put(gm, t, y, 128, 640, nn(n2t[256 * y : 256 * y + 256, :], pre_grad))
        if fast:
            middle_sum.across(t, 128, 640, 0)
    dense = jnp.concatenate(dense, axis=1)
    dn2 = jnp.concatenate(dn2, axis=1)
    result = middle + dense
    out_ref[...] = (mixed(result, False) if fast else result).astype(BF)
    live = (iota((ROWS, 512), 0) + me * ROWS < valid_len).astype(F32)
    small_ref[2:3, :] = jnp.sum(live * result * result, axis=0, keepdims=True)
    small_ref[3:4, :] = jnp.sum(live * branch * branch, axis=0, keepdims=True)
    small_ref[4:5, :] = jnp.sum(live * dense * dense, axis=0, keepdims=True)
    small_ref[5:6, :] = jnp.sum(live, axis=0, keepdims=True)
    small_ref[6:8, :] = jnp.zeros((2, 512), F32)
    n2 = n2s[...]
    small_ref[1:2, :] = jnp.sum(dn2 * n2, axis=0, keepdims=True)
    middle_grad = ref["cots"][...] + norm_back(n2, r2, dn2)
    n2s[...] = middle_grad
    mgb = middle_grad.astype(BF)
    mgt = mgb.T
    for t in range(PAIRS):
        us[t, 0:ROWS, :] = nn(mgb[:, :256], get(wm, t, 0, 0, 128)) + nn(mgb[:, 256:], get(wm, t, 1, 0, 128))
        for y in range(2):
            put(gm, t, y, 0, 128, nn(mgt[256 * y : 256 * y + 256, :], att[t].astype(BF)))
        if fast:
            middle_sum.across(t, 0, 128, 4)
    if fast:
        late.near(1, 3)

    def head_sums(v):
        first = jnp.sum(jnp.where(iota(v.shape, 1) < 64, v, 0.0), axis=-1, keepdims=True)
        second = jnp.sum(jnp.where(iota(v.shape, 1) < 64, 0.0, v), axis=-1, keepdims=True)
        return jnp.where(iota(v.shape, 1) < 64, first, second)

    def attend_back(p, carry):
        up = us.at[p]
        grad, inverse = up[0:ROWS, :], dacc[p]
        delta = head_sums(grad * att[p])
        up[0:ROWS, :] = grad * inverse
        ns[0:ROWS, :] = delta * inverse
        mus[0:ROWS, :] = mm[p]
        for level in range(LEVELS - 1):
            n = COUNT[level + 1]
            after = slice(AT[level + 1], AT[level + 1] + n)
            top_e, top_o = pairs_of(mus, AT[level], n)
            top = jnp.minimum(top_e, top_o)
            fe, fo = jnp.exp(top - top_e), jnp.exp(top - top_o)
            u_e, u_o = pairs_of(up, AT[level], n)
            d_e, d_o = pairs_of(ns, AT[level], n)
            up[after, :] = u_e * fe + u_o * fo
            ns[after, :] = d_e * fe + d_o * fo
            mus[after, :] = top
        for rows in (slice(504, STACK),):
            up[rows, :] = jnp.zeros((8, 128), F32)
            ns[rows, :] = jnp.zeros((8, 128), F32)
            mus[rows, :] = jnp.zeros((8, 128), F32)
        for which in range(2):
            dkw[which * PAIRS + p, 0:512, :] = jnp.zeros((512, 128), F32)
        for k in range(TILES):
            here = slice(64 * k, 64 * k + 64)
            keys = slice(TILE_AT[k], TILE_AT[k] + 128)
            factor = jnp.exp(ml[p, here, :] - mus[here, :])
            g = up[here, :] * factor
            g_high = g.astype(BF)
            g2 = both(g_high)
            g4 = jnp.concatenate([g2, both((g - g_high.astype(F32)).astype(BF))], axis=1)
            v2 = vw[p, keys, :]
            v2 = jnp.concatenate([v2, v2], axis=1)
            h = ns[here, :] * factor
            h2 = jnp.concatenate([h[:, 0:1], h[:, 64:65]], axis=0)
            q2 = both(qb[p, here, :])
            low = eb[p, k]
            d = low.astype(F32) * (nt(g4, v2) - h2)
            d = d.astype(BF)
            dv = tn(low, g2)
            dk = tn(d, q2)
            if k < 6:
                dkw[p, keys, :] = dkw[p, keys, :] + dk
                dkw[PAIRS + p, keys, :] = dkw[PAIRS + p, keys, :] + dv
            else:
                dkw[p, keys, :] = dk
                dkw[PAIRS + p, keys, :] = dv
            dqs[p, here, :] = joined(nn(d, kw[p, keys, :]))
            if fast and k == 3:

                @pl.when(p == 0)
                def _():
                    late.near(2)

                @pl.when(p == 1)
                def _():
                    late.near(0)

                @pl.when(p == 2)
                def _():
                    late.own(outs["l"], 1)

                @pl.when(p == 3)
                def _():
                    middle_sum.near(1)

        for which in range(2):
            row = which * PAIRS + p
            for level in range(LEVELS - 1):
                part = slice(16 * level, 16 * level + 16)
                back_l[p, which, part, :] = dkw[row, LEFT[level] : LEFT[level] + 16, :].astype(BF)
                back_r[p, which, part, :] = dkw[row, RIGHT[level] : RIGHT[level] + 16, :].astype(BF)
            for g in range(tensors):
                dfar[g, p, which] = dkw[row, FAR + 8 * g : FAR + 8 * g + 8, :]
        exchange(*back(p))
        if fast:

            @pl.when(p == 0)
            def _():
                middle_sum.across_all(middle_parts)
                middle_sum.far(1, 3, 2, 0)

            @pl.when(p == 1)
            def _():
                late.own(outs["l"], 3)

            @pl.when(p == 2)
            def _():
                late.own(outs["l"], 2)

            @pl.when(p == 3)
            def _():
                late.own(outs["l"], 0)
                middle_sum.near(3)

        return carry

    def back(p):
        return (
            20 + 5 * p,
            back_l.at[p],
            got_r.at[p],
            back_r.at[p],
            got_l.at[p],
            lambda k: dfar.at[lax.rem(me + k, tensors), p],
            lambda k: gfar.at[k, p],
        )

    lax.fori_loop(0, PAIRS, attend_back, 0)
    def unpool(p, carry):
        exchanged(*back(p))
        factors = stack_factors()
        cur = dqs[p, AT[5] : AT[5] + 8, :] * factors[AT[5] : AT[5] + 8]
        for level in range(LEVELS - 2, -1, -1):
            rows = slice(AT[level], AT[level] + COUNT[level])
            cur = doubled(tmp_a, cur, COUNT[level] // 2) + dqs[p, rows, :] * factors[rows]
        qs[p, 0:ROWS, :] = cur
        for which, raw in enumerate((ks, vs)):
            row = which * PAIRS + p
            raw_p = raw.at[p]
            cur = gfar[1, p, which]
            for k in range(2, tensors):
                cur = cur + gfar[k, p, which]
            cur = cur * rdiv[AT[5] : AT[5] + 8, :]
            for level in range(LEVELS - 2, -1, -1):
                n = COUNT[level]
                rows = slice(AT[level], AT[level] + n)
                part = slice(16 * level, 16 * level + 16)
                if level < 4:
                    raw_p[rows, :] = dkw[row, OWN[level] : OWN[level] + n, :]
                else:
                    raw_p[rows, :] = jnp.zeros((n, 128), F32)
                first = slice(AT[level], AT[level] + 16)
                last = slice(AT[level] + n - 16, AT[level] + n)
                raw_p[first, :] = raw_p[first, :] + got_l[p, which, part, :].astype(F32)
                raw_p[last, :] = raw_p[last, :] + got_r[p, which, part, :].astype(F32)
                cur = doubled(tmp_a, cur, n // 2) + raw_p[rows, :] * rdiv[rows, :]
            raw_p[0:ROWS, :] = cur * (iota((ROWS, 128), 0) + me * ROWS < valid_len).astype(F32)
        return carry

    lax.fori_loop(0, PAIRS, unpool, 0)
    if fast:
        middle_sum.near(2, 0)
        middle_sum.own(outs["m"], 1)

    n1 = n1s[...]
    n1t = n1.astype(BF).T
    dn1 = [0.0, 0.0]
    for t in range(PAIRS):
        joint = jnp.concatenate(
            [qs[t, 0:ROWS, :].astype(BF), ks[t, 0:ROWS, :].astype(BF), vs[t, 0:ROWS, :].astype(BF)], axis=1
        )
        for y in range(2):
            put(ga, t, y, 0, 384, nn(n1t[256 * y : 256 * y + 256, :], joint))
            dn1[y] = dn1[y] + nt(joint, get(wa, t, y, 0, 384))
        if fast:
            early.across(t, 0, 384, 0)
    dn1 = jnp.concatenate(dn1, axis=1)
    small_ref[0:1, :] = jnp.sum(dn1 * n1, axis=0, keepdims=True)
    if fast:
        sums = Remote(ref["sum_send"], ref["sum_recv"])
        got = ref["sums"]
        ways = (at.to_other, at.to_x, at.to_y)

        def sum_send(i):
            got[2 * i] = small_ref[...]
            sums.send(i, got.at[2 * i], got.at[2 * i + 1], ways[i])

        def sum_add(i):
            sums.arrived(i, got.at[2 * i + 1], ways[i])
            small_ref[...] = got[2 * i] + got[2 * i + 1]

        sum_send(0)
        early.across_all(early_parts)
        early.far(1, 3, 2, 0)
        sum_add(0)
        sum_send(1)
        middle_sum.own(outs["m"], 3, 2, 0)
        sum_add(1)
        sum_send(2)
        early.near(1, 3, 2, 0)
        sum_add(2)
        got[6 + at.z] = small_ref[...]
        for k in range(1, 4):
            sums.send(2 + k, got.at[6 + at.z], got.at[6 + at.z], at.to_z(k))
        early.own(outs["a"], 1, 3, 2, 0)
    r1 = lax.rsqrt(row_variance(ref["xs"][...]) + EPS)
    in_grad = n2s[...] + norm_back(n1, r1, dn1)
    ingrad_ref[...] = (mixed(in_grad, False) if fast else in_grad).astype(BF)
    if fast:
        late.finish(outs["l"])
        middle_sum.finish(outs["m"])
        outs["m"][:, 128:640] = outs["m"][:, 128:640] * g2c
        early.finish(outs["a"])
        outs["a"][...] = outs["a"][...] * g1c
        for k in range(1, 4):
            sums.arrived(2 + k, got.at[6], at.to_b)
        total = ((got[6] + got[7]) + got[8]) + got[9]
        gains = jnp.zeros((2, 64), F32)
        for i in range(8):
            gains = gains + jnp.where(4 * at.y + at.z == i, total[0:2, 64 * i : 64 * i + 64], 0.0)
        squares = jnp.sum(total[2:6], axis=1, keepdims=True)
        root = jnp.sqrt(squares[0:3] / squares[3:4])
        lanes = iota((1, 128), 1)
        tail = ref["grads"].at[:, 1536:1664]
        tail[...] = jnp.zeros(tail.shape, F32)
        tail[0:1, 0:64] = gains[0:1] / g1
        tail[1:2, 0:64] = gains[1:2] / g2
        tail[2:3, :] = sum(jnp.where(lanes == i, root[i : i + 1], 0.0) for i in range(3))
        for remote, parts in ((early, early_parts), (middle_sum, middle_parts), (late, late_parts)):
            for lo, hi, base in parts:
                remote.across_drain(lo, hi, base)
            remote.drain(remote.r2.at[0], at.to_x)
        for remote in (first, second, third):
            remote.drain(remote.own, at.to_x)
        sums.drain(small_ref, at.to_x)


def row_variance(v):
    centred = v - jnp.mean(v, axis=-1, keepdims=True)
    return jnp.mean(centred * centred, axis=-1, keepdims=True)


def run_layer(fast, tensors, lengths, inputs, cotangent, *weights):
    vmem = pl.BlockSpec(memory_space=pltpu.VMEM)
    f = lambda *shape: pltpu.VMEM(shape, F32)
    b = lambda *shape: pltpu.VMEM(shape, BF)
    full = (2, 2, 2, 4, 64) if fast else (tensors, 2, 256)
    scratch = {
        "qs": f(PAIRS, STACK, 128),
        "ks": f(PAIRS, STACK, 128),
        "vs": f(PAIRS, STACK, 128),
        "qb": b(PAIRS, STACK, 128),
        "kw": b(PAIRS, KEYS, 128),
        "vw": b(PAIRS, KEYS, 128),
        "wt": f(TILES, 64, 128),
        "rdiv": f(STACK, 128),
        "edge_l": b(PAIRS, 2, HALO, 128),
        "edge_r": b(PAIRS, 2, HALO, 128),
        "halo_l": b(PAIRS, 2, HALO, 128),
        "halo_r": b(PAIRS, 2, HALO, 128),
        "far": f(tensors, PAIRS, 2, 8, 128),
        "eb": b(PAIRS, TILES, 128, 128),
        "ns": f(STACK, 128),
        "ml": f(PAIRS, STACK, 128),
        "ds": f(STACK, 128),
        "att": f(PAIRS, ROWS, 128),
        "mm": f(PAIRS, ROWS, 128),
        "tmp_a": f(ROWS, 128),
        "tmp_b": f(ROWS, 128),
        "tmp_c": f(ROWS, 128),
        "xs": f(ROWS, 512),
        "cots": f(ROWS, 512),
        "n1s": f(ROWS, 512),
        "n2s": f(ROWS, 512),
        "dacc": f(PAIRS, ROWS, 128),
        "us": f(PAIRS, STACK, 128),
        "mus": f(STACK, 128),
        "dqs": f(PAIRS, STACK, 128),
        "acts": b(PAIRS, ROWS, 512),
        "slopes": f(PAIRS, ROWS, 512),
        "dkw": f(2 * PAIRS, KEYS, 128),
        "back_l": b(PAIRS, 2, HALO, 128),
        "back_r": b(PAIRS, 2, HALO, 128),
        "got_l": b(PAIRS, 2, HALO, 128),
        "got_r": b(PAIRS, 2, HALO, 128),
        "dfar": f(tensors, PAIRS, 2, 8, 128),
        "gfar": f(tensors, PAIRS, 2, 8, 128),
        "send_sem": pltpu.SemaphoreType.DMA((40,)),
        "recv_sem": pltpu.SemaphoreType.DMA((40,)),
    }
    if fast:
        ins = ("lengths", *("in_" + n for n in ("x", "cot", "q", "k", "v", "o", "w1", "part_l", "g1", "g2")))
        outs = {"rows": ((ROWS, 1024), BF), "grads": ((64, 1664), F32)}
        scratch |= {n: b(*shape) for n, shape in LOADS}
        scratch |= {"in_sem": pltpu.SemaphoreType.DMA((len(LOADS),))}
        scratch |= {"part_a": b(64, 384), "part_m": b(64, 640), "small": f(8, 512)}
        for name, c in zip("aml", (384, 640, 512), strict=True):
            scratch |= {
                "w" + name: b(*full, c),
                "g" + name: b(*full, c),
                name + "0": b(2, 2, 4, 64, c),
                name + "1": b(2, 4, 64, c),
                name + "2": b(4, 64, c),
                name + "3": b(3, 64, c),
            }
        scratch |= {
            "sums": f(10, 8, 512),
            "gather_send": pltpu.SemaphoreType.DMA((3, 31)),
            "gather_recv": pltpu.SemaphoreType.DMA((3, 31)),
            "reduce_send": pltpu.SemaphoreType.DMA((3, 23)),
            "reduce_recv": pltpu.SemaphoreType.DMA((3, 23)),
            "ready": pltpu.SemaphoreType.REGULAR,
            "sum_send": pltpu.SemaphoreType.DMA((6,)),
            "sum_recv": pltpu.SemaphoreType.DMA((6,)),
        }
    else:
        ins = ("lengths", "x", "cot", "wa", "wm", "wl")
        outs = {"out": ((ROWS, 512), BF), "ingrad": ((ROWS, 512), BF), "small": ((8, 512), F32)}
        outs |= {"g" + name: (w.shape, BF) for name, w in zip("aml", weights, strict=True)}
    return pl.pallas_call(
        functools.partial(layer_kernel, fast, tensors, (*ins, *outs, *scratch)),
        out_shape=tuple(jax.ShapeDtypeStruct(*shape) for shape in outs.values()),
        in_specs=[pl.BlockSpec(memory_space=pltpu.SMEM)] + [pl.BlockSpec(memory_space=pltpu.HBM) if fast else vmem] * (len(ins) - 1),
        out_specs=(vmem,) * len(outs),
        scratch_shapes=list(scratch.values()),
        compiler_params=pltpu.CompilerParams(
            collective_id=0, has_side_effects=True, vmem_limit_bytes=62 * 1024 * 1024
        ),
        name="layer",
    )(lengths, inputs, cotangent, *weights)


def hand_out_kernel(rows, grads, *refs):
    outs, tail, sem = refs[:11], refs[11], refs[12]
    edges = (0, 128, 256, 384, 512, 1024, 1536)
    parts = [rows.at[:, 0:512], rows.at[:, 512:1024]]
    parts += [grads.at[:, lo:hi] for lo, hi in zip(edges, edges[1:])]
    copies = [pltpu.make_async_copy(grads.at[0:8, 1536:1664], tail, sem.at[8])]
    copies += [pltpu.make_async_copy(part, out, sem.at[i]) for i, (part, out) in enumerate(zip(parts, outs))]
    for copy in copies:
        copy.start()
    copies[0].wait()
    for i in range(3):
        outs[8 + i][...] = tail[i, 0 : outs[8 + i].shape[0]]
    for copy in copies[1:]:
        copy.wait()


def hand_out(rows, grads):
    shapes = [(ROWS, 512)] * 2 + [(64, 128)] * 4 + [(64, 512)] * 2 + [(64,)] * 2 + [(3,)]
    return pl.pallas_call(
        hand_out_kernel,
        out_shape=tuple(jax.ShapeDtypeStruct(shape, BF if i < 2 else F32) for i, shape in enumerate(shapes)),
        in_specs=[pl.BlockSpec(memory_space=pltpu.HBM)] * 2,
        out_specs=tuple(pl.BlockSpec(memory_space=pltpu.VMEM) for _ in shapes),
        scratch_shapes=[pltpu.VMEM((8, 128), F32), pltpu.SemaphoreType.DMA((9,))],
        name="hand_out",
    )(rows, grads)


def per_device(
    fast,
    inputs,
    lengths,
    cotangent,
    query_weight,
    key_weight,
    value_weight,
    output_weight,
    inner_weight,
    outer_weight,
    first_gain,
    second_gain,
):
    tensors = lax.axis_size("tensor")
    everyone = ("tensor", "dp")
    if fast:
        rows, grads = run_layer(
            fast,
            tensors,
            lengths,
            inputs,
            cotangent,
            query_weight,
            key_weight,
            value_weight,
            output_weight.T,
            inner_weight,
            outer_weight.T,
            first_gain,
            second_gain,
        )
        out, input_grad, gq, gk, gv, go, gi, gl, gain_one, gain_two, root = hand_out(rows, grads)
        return out, input_grad, gq, gk, gv, go.T, gi, gl.T, gain_one, gain_two, root
    g1 = first_gain.astype(F32)[:, None]
    g2 = second_gain.astype(F32)[:, None]
    scaled = lambda g, w: (g * w.astype(F32)).astype(BF)
    part_a = scaled(g1, jnp.concatenate([query_weight, key_weight, value_weight], axis=1))
    part_m = jnp.concatenate([output_weight.T, scaled(g2, inner_weight)], axis=1)
    parts = (part_a, part_m, outer_weight.T)
    full = [lax.all_gather(p, everyone, axis=0, tiled=True).reshape(tensors, 2, 256, -1) for p in parts]
    out, input_grad, small, *grads = run_layer(fast, tensors, lengths, inputs, cotangent, *full)

    def reduced(g):
        return lax.psum_scatter(
            g.reshape(tensors * 512, g.shape[-1]).astype(F32), everyone, scatter_dimension=0, tiled=True
        )

    ga, gm, gl = (reduced(g) for g in grads)
    small = lax.psum(small, everyone)
    width = first_gain.shape[0]
    gains = lax.dynamic_slice(small, (0, lax.axis_index("dp") * width), (2, width))
    sums = jnp.sum(small, axis=1)
    root_mean_squares = jnp.sqrt(sums[2:5] / sums[5])
    ga = ga * g1
    return (
        out,
        input_grad,
        ga[:, 0:128],
        ga[:, 128:256],
        ga[:, 256:384],
        gm[:, 0:128].T,
        gm[:, 128:640] * g2,
        gl.T,
        gains[0] / first_gain.astype(F32),
        gains[1] / second_gain.astype(F32),
        root_mean_squares,
    )


def solution(mesh):
    fast = (mesh.shape["dp"], mesh.shape["tensor"]) == (8, 4)
    return jax.shard_map(
        functools.partial(per_device, fast),
        mesh=mesh,
        in_specs=(
            P(("dp", "tensor"), None),
            P("dp"),
            P(("dp", "tensor"), None),
            P("dp", "tensor"),
            P("dp", "tensor"),
            P("dp", "tensor"),
            P("tensor", "dp"),
            P("dp", "tensor"),
            P("tensor", "dp"),
            P("dp"),
            P("dp"),
        ),
        out_specs=(
            P(("dp", "tensor"), None),
            P(("dp", "tensor"), None),
            P("dp", "tensor"),
            P("dp", "tensor"),
            P("dp", "tensor"),
            P("tensor", "dp"),
            P("dp", "tensor"),
            P("tensor", "dp"),
            P("dp"),
            P("dp"),
            P(),
        ),
        check_vma=False,
    )
```

```python
import functools

import jax
import jax.numpy as jnp
from jax import lax
from jax.experimental import pallas as pl
from jax.experimental.pallas import tpu as pltpu
from jax.sharding import PartitionSpec as P

MESH = pl.DeviceIdType.MESH
F32, BF = jnp.float32, jnp.bfloat16
HEAD_DIM = 64
EPS = 1e-05

ROWS, PAIRS, LEVELS = 256, 4, 6
COUNT = (256, 128, 64, 32, 16, 8)
AT = (0, 256, 384, 448, 480, 496)
STACK = 512
OWN = (32, 352, 544, 656)
LEFT = (16, 336, 528, 640, 704)
RIGHT = (288, 480, 608, 688, 720)
FAR = 736
KEYS = 768
BLANK = ((0, 16), (304, 32), (496, 32), (624, 16))
TILE_AT = (0, 64, 128, 192, 320, 384, 512, 640)
TILES = 8
HALO = 80
LOADS = (
    ("g1", (64,)),
    ("g2", (64,)),
    ("q", (64, 128)),
    ("k", (64, 128)),
    ("v", (64, 128)),
    ("o", (64, 128)),
    ("w1", (64, 512)),
    ("part_l", (64, 512)),
    ("x", (ROWS, 512)),
    ("cot", (ROWS, 512)),
)


def nn(a, b):
    return lax.dot_general(a, b, (((1,), (0,)), ((), ())), preferred_element_type=F32)


def nt(a, b):
    return lax.dot_general(a, b, (((1,), (1,)), ((), ())), preferred_element_type=F32)


def tn(a, b):
    return lax.dot_general(a, b, (((0,), (0,)), ((), ())), preferred_element_type=F32)


def iota(shape, dim):
    return lax.broadcasted_iota(jnp.int32, shape, dim)


def level_counts(index, level, total, valid_len):
    factor = 1 << level
    c = jnp.clip(valid_len - index * factor, 0, factor)
    return jnp.where((index >= 0) & (index < total), c, 0).astype(F32)


def tile_weights(k, me, tensors, valid_len):
    i, j = iota((64, 128), 0), iota((64, 128), 1)
    if k < 7:
        level = 0 if k < 4 else 1 if k < 6 else 2
        first = 64 * (k - AT[level] // 64)
        n = COUNT[level]
        c = level_counts(me * n + first - 32 + j, level, n * tensors, valid_len)
        near = jnp.abs((i >> 4) - (j >> 4) + 2) <= 1
        if level:
            near = near & (jnp.abs((i >> 3) - (j >> 3) + 4) > 1)
        return jnp.where(near, c, 0.0)
    c3 = level_counts(me * 32 + j - 16, 3, 32 * tensors, valid_len)
    near3 = (jnp.abs((i >> 4) - (j >> 4) + 1) <= 1) & (jnp.abs((i >> 3) - (j >> 3) + 2) > 1)
    near3 = near3 & (i < 32) & (j < 64)
    key4 = jnp.where(j < 80, j - 80, j - 64)
    c4 = level_counts(me * 16 + key4, 4, 16 * tensors, valid_len)
    near4 = (jnp.abs(((i - 32) >> 3) - (key4 >> 3)) > 1) & (i >= 32) & (i < 48) & (j >= 64) & (j < 96)
    key5 = j - 96
    c5 = level_counts(key5, 5, 8 * tensors, valid_len)
    near5 = (jnp.abs(me - (key5 >> 3)) > 1) & (i >= 48) & (i < 56) & (j >= 96)
    return jnp.where(near3, c3, 0.0) + jnp.where(near4, c4, 0.0) + jnp.where(near5, c5, 0.0)


def row_divisors(me, tensors, valid_len):
    i = iota((STACK, 128), 0)
    out = jnp.ones((STACK, 128), F32)
    for level in range(1, LEVELS):
        c = level_counts(i - AT[level] + me * COUNT[level], level, COUNT[level] * tensors, valid_len)
        here = (i >= AT[level]) & (i < AT[level] + COUNT[level])
        out = jnp.where(here, 1.0 / jnp.maximum(c, 1.0), out)
    return out


def stack_factors():
    i = iota((STACK, 128), 0)
    out = jnp.full((STACK, 128), HEAD_DIM ** (-0.5), F32)
    for level in range(1, LEVELS):
        out = jnp.where(i >= AT[level], HEAD_DIM ** (-0.5) / (1 << level), out)
    return out


def pairs_of(ref, start, n):
    return ref[pl.ds(start, n, stride=2), :], ref[pl.ds(start + 1, n, stride=2), :]


def pool(ref):
    for level in range(LEVELS - 1):
        n = COUNT[level + 1]
        even, odd = pairs_of(ref, AT[level], n)
        ref[AT[level + 1] : AT[level + 1] + n, :] = even + odd


def doubled(ref, value, n):
    ref[pl.ds(0, n, stride=2), :] = value
    ref[pl.ds(1, n, stride=2), :] = value
    return ref[0 : 2 * n, :]


def normalised(v):
    centred = v - jnp.mean(v, axis=-1, keepdims=True)
    r = lax.rsqrt(jnp.mean(centred * centred, axis=-1, keepdims=True) + EPS)
    return centred * r, r


def norm_back(n, r, hg):
    return r * (hg - jnp.mean(hg, axis=-1, keepdims=True) - n * jnp.mean(hg * n, axis=-1, keepdims=True))


def gelu_both(u):
    c = 0.7978845608028654
    square = u * u
    th = jnp.tanh(c * (u + 0.044715 * (square * u)))
    half = 0.5 * (1.0 + th)
    slope = half + (0.5 * c) * u * (1.0 - th * th) * (1.0 + 0.134145 * square)
    return u * half, slope


class Place:
    def __init__(self):
        self.d, self.t = lax.axis_index("dp"), lax.axis_index("tensor")
        self.z, self.y = self.d // 2, self.d % 2
        self.x, self.c = self.t // 2, self.t % 2
        self.a = self.x + self.c * (self.y - self.x)
        self.b = self.y + self.c * (self.x - self.y)
        flip_x, flip_y = 2 - 4 * self.x, 1 - 2 * self.y
        self.to_x, self.to_y = (self.d, self.t + flip_x), (self.d + flip_y, self.t)
        self.to_a = (self.d + self.c * flip_y, self.t + (1 - self.c) * flip_x)
        self.to_b = (self.d + (1 - self.c) * flip_y, self.t + self.c * flip_x)
        self.to_other = (self.d, self.t + 1 - 2 * self.c)
        self.to_across = (self.d, 3 - self.t)

    def to_z(self, k):
        return (2 * ((self.z + k) % 4) + self.y, self.t)


def flipped(bit, by):
    return 1 - bit if by else bit


class Remote:
    def __init__(self, send_sem, recv_sem):
        self.send_sem, self.recv_sem, self.started = send_sem, recv_sem, set()

    def copy(self, i, src, dst, to):
        return pltpu.make_async_remote_copy(
            src, dst, self.send_sem.at[i], self.recv_sem.at[i], device_id=to, device_id_type=MESH
        )

    def send(self, i, src, dst, to):
        self.copy(i, src, dst, to).start()
        self.started.add(i)

    def arrived(self, i, dst, to):
        self.copy(i, dst, dst, to).wait_recv()

    def drain(self, like, to):
        for i in sorted(self.started):
            self.copy(i, like, like, to).wait_send()


class Gather(Remote):
    def __init__(self, at, own, w, send_sem, recv_sem):
        super().__init__(send_sem, recv_sem)
        self.at, self.own, self.w = at, own, w

    def shard(self, j, aa=0, bb=0, plane=0):
        at = self.at
        a, b = (at.b, at.a) if plane else (at.a, at.b)
        return self.w.at[flipped(at.c, plane), flipped(a, aa), flipped(b, bb), (at.z + 4 - j) % 4]

    def source(self, j, aa=0, bb=0):
        return self.own if (j, aa, bb) == (0, 0, 0) else self.shard(j, aa, bb)

    def along_z(self):
        for k in (1, 3, 2):
            self.send(k - 1, self.own, self.shard(0), self.at.to_z(k))

    def along_b(self, j):
        self.send(3 + j, self.source(j), self.shard(j), self.at.to_b)

    def along_a(self, j, bb):
        self.send(7 + 4 * bb + j, self.source(j, 0, bb), self.shard(j, 0, bb), self.at.to_a)

    def across(self, j, aa, bb):
        self.send(15 + 8 * aa + 4 * bb + j, self.source(j, aa, bb), self.shard(j, aa, bb), self.at.to_other)

    def own_on(self, met=True):
        self.along_b(0)
        self.along_a(0, 0)
        if met:
            self.across(0, 0, 0)

    def after_z(self, *js, met=True):
        for j in js:
            self.arrived(j - 1, self.shard(j), self.at.to_b)
            self.along_b(j)
            self.along_a(j, 0)
            if met:
                self.across(j, 0, 0)

    def after_b(self, *js, met=True):
        for j in js:
            self.arrived(3 + j, self.shard(j, 0, 1), self.at.to_b)
            self.along_a(j, 1)
            if met:
                self.across(j, 0, 1)

    def after_a(self, bb, *js):
        for j in js:
            self.arrived(7 + 4 * bb + j, self.shard(j, 1, bb), self.at.to_b)
            self.across(j, 1, bb)

    def after_across(self):
        for aa in range(2):
            for bb in range(2):
                for j in range(4):
                    self.arrived(15 + 8 * aa + 4 * bb + j, self.shard(j, aa, bb, 1), self.at.to_b)


class Reduce(Remote):
    def __init__(self, at, g, r0, r1, r2, r3, send_sem, recv_sem):
        super().__init__(send_sem, recv_sem)
        self.at, self.g, self.r0, self.r1, self.r2, self.r3 = at, g, r0, r1, r2, r3

    def across(self, t, lo, hi, base):
        @pl.when(self.at.c != t % 2)
        def _():
            for a, b in ((t // 2, 0), (t // 2, 1)) if t % 2 == 0 else ((0, t // 2), (1, t // 2)):
                self.copy(
                    base + 2 * a + b,
                    self.g.at[t % 2, a, b, :, :, lo:hi],
                    self.r0.at[a, b, :, :, lo:hi],
                    self.at.to_other,
                ).start()

    def across_wait(self, a, b, lo, hi, base):
        piece = self.r0.at[a, b, :, :, lo:hi]
        copy = self.copy(base + 2 * a + b, piece, piece, self.at.to_other)
        copy.wait_recv()

    def across_drain(self, lo, hi, base):
        for i in range(4):
            piece = self.r0.at[i // 2, i % 2, :, :, lo:hi]
            self.copy(base + i, piece, piece, self.at.to_other).wait_send()

    def across_all(self, parts):
        for a in range(2):
            for b in range(2):
                for lo, hi, base in parts:
                    self.across_wait(a, b, lo, hi, base)

    def far(self, *js):
        at = self.at
        for j in js:
            z = (at.z + j) % 4
            for bb in (1, 0):
                b = flipped(at.b, bb)
                here = self.g.at[at.c, 1 - at.a, b, z]
                here[...] = (here[...].astype(F32) + self.r0[1 - at.a, b, z].astype(F32)).astype(BF)
                self.send(8 + 4 * bb + j, here, self.r1.at[b, z], at.to_a)

    def near(self, *js):
        at = self.at
        b = 1 - at.b
        for j in js:
            z = (at.z + j) % 4
            here = self.g.at[at.c, at.a, b, z]
            self.arrived(12 + j, self.r1.at[b, z], at.to_a)
            total = here[...].astype(F32) + self.r0[at.a, b, z].astype(F32) + self.r1[b, z].astype(F32)
            here[...] = total.astype(BF)
            self.send(16 + j, here, self.r2.at[z], at.to_b)

    def own(self, out, *js):
        at = self.at
        b = at.b
        for j in js:
            z = (at.z + j) % 4
            here = self.g.at[at.c, at.a, b, z]
            self.arrived(8 + j, self.r1.at[b, z], at.to_a)
            self.arrived(16 + j, self.r2.at[z], at.to_b)
            total = here[...].astype(F32) + self.r0[at.a, b, z].astype(F32)
            total = total + self.r1[b, z].astype(F32) + self.r2[z].astype(F32)
            if j:
                here[...] = total.astype(BF)
                self.send(20 + j - 1, here, self.r3.at[j - 1], at.to_z(j))
            else:
                out[...] = total

    def finish(self, out):
        for k in (1, 3, 2):
            self.arrived(20 + k - 1, self.r3.at[k - 1], self.at.to_b)
        total = out[...] + self.r3[0].astype(F32)
        out[...] = total + self.r3[1].astype(F32) + self.r3[2].astype(F32)


def mixed(v, into):
    tiles = [v[:, 128 * i : 128 * i + 128] for i in range(4)]
    rolled = [pltpu.roll(tile, 64, 1) for tile in tiles]
    low = iota(tiles[0].shape, 1) < 64
    if into:
        pairs = ((0, 1, 0), (2, 3, 0), (0, 1, 1), (2, 3, 1))
    else:
        pairs = ((0, 2, 0), (0, 2, 1), (1, 3, 0), (1, 3, 1))
    out = []
    for i, k, high in pairs:
        out.append(jnp.where(low, rolled[i], tiles[k]) if high else jnp.where(low, tiles[i], rolled[k]))
    return jnp.concatenate(out, axis=1)


def layer_kernel(fast, tensors, names, *refs):
    ref = dict(zip(names, refs, strict=True))
    if fast:
        loads = {
            n: pltpu.make_async_copy(ref["in_" + n], ref[n], ref["in_sem"].at[i]) for i, (n, _) in enumerate(LOADS)
        }
        for load in loads.values():
            load.start()
    me = lax.axis_index("tensor")
    valid_len = ref["lengths"][0]
    barrier = pltpu.get_barrier_semaphore()
    if fast:
        at = Place()
        same = [at.to_z(1), at.to_z(2), at.to_z(3), at.to_y, at.to_x]
        others = [at.to_other, at.to_across]
        for peer in same:
            pl.semaphore_signal(barrier, inc=1, device_id=peer, device_id_type=MESH)

        @pl.when(at.c == 0)
        def _():
            for peer in others:
                pl.semaphore_signal(barrier, inc=1, device_id=peer, device_id_type=MESH)
    else:
        peers = [{"tensor": lax.rem(me + k, tensors)} for k in range(1, tensors)]
        for peer in peers:
            pl.semaphore_signal(barrier, inc=1, device_id=peer, device_id_type=MESH)
    len_ref, x_ref, cot_ref = (ref[n] for n in ("lengths", "x", "cot"))
    if fast:
        out_ref, ingrad_ref = ref["rows"].at[:, 0:512], ref["rows"].at[:, 512:1024]
        outs = {"a": ref["grads"].at[:, 0:384], "m": ref["grads"].at[:, 384:1024], "l": ref["grads"].at[:, 1024:1536]}
        for n, _ in LOADS[:8]:
            loads[n].wait()
        g1, g2 = (ref[n][...].astype(F32).reshape(1, 64) for n in ("g1", "g2"))
        column = lambda g: jnp.sum(jnp.where(iota((64, 64), 0) == iota((64, 64), 1), g, 0.0), axis=1, keepdims=True)
        g1c, g2c = column(g1), column(g2)
        for i, n in enumerate("qkv"):
            ref["part_a"][:, 128 * i : 128 * i + 128] = (g1c * ref[n][...].astype(F32)).astype(BF)
        ref["part_m"][:, 0:128] = ref["o"][...]
        ref["part_m"][:, 128:640] = (g2c * ref["w1"][...].astype(F32)).astype(BF)
    else:
        out_ref, ingrad_ref = ref["out"], ref["ingrad"]
    qs, ks, vs, qb, kw, vw, wt, rdiv = (ref[n] for n in ("qs", "ks", "vs", "qb", "kw", "vw", "wt", "rdiv"))
    edge_l, edge_r, halo_l, halo_r, far = (ref[n] for n in ("edge_l", "edge_r", "halo_l", "halo_r", "far"))
    eb, ns, ml, ds_, att, mm = (ref[n] for n in ("eb", "ns", "ml", "ds", "att", "mm"))
    tmp_a, tmp_b, tmp_c, n1s, n2s, dacc = (ref[n] for n in ("tmp_a", "tmp_b", "tmp_c", "n1s", "n2s", "dacc"))
    us, mus, dqs, dkw = (ref[n] for n in ("us", "mus", "dqs", "dkw"))
    back_l, back_r, got_l, got_r, dfar, gfar = (
        ref[n] for n in ("back_l", "back_r", "got_l", "got_r", "dfar", "gfar")
    )
    send_sem, recv_sem, small_ref = ref["send_sem"], ref["recv_sem"], ref["small"]
    ga, gm, gl = ref["ga"], ref["gm"], ref["gl"]
    wa, wm, wl = ref["wa"], ref["wm"], ref["wl"]

    def view(r, t, y):
        if not fast:
            return r.at[t, y]
        return r.at[0, t // 2, y] if t % 2 == 0 else r.at[1, y, t // 2]

    def get(r, t, y, lo, hi):
        return view(r, t, y)[..., lo:hi].reshape(256, hi - lo)

    def put(r, t, y, lo, hi, value):
        v = view(r, t, y)
        v[..., lo:hi] = value.astype(BF).reshape(*v.shape[:-1], hi - lo)

    if fast:
        @pl.when(at.c == 0)
        def _():
            pl.semaphore_wait(barrier, len(same))

        @pl.when(at.c == 1)
        def _():
            pl.semaphore_wait(barrier, len(same) + len(others))
            for peer in others:
                pl.semaphore_signal(ref["ready"], inc=1, device_id=peer, device_id_type=MESH)

        first, second, third = (
            Gather(at, ref["part_" + n], ref["w" + n], ref["gather_send"].at[i], ref["gather_recv"].at[i])
            for i, n in enumerate("aml")
        )
        early, middle_sum, late = (
            Reduce(
                at,
                ref["g" + n],
                *(ref[n + str(k)] for k in range(4)),
                ref["reduce_send"].at[i],
                ref["reduce_recv"].at[i],
            )
            for i, n in enumerate("aml")
        )
        early_parts, middle_parts, late_parts = ((0, 384, 0),), ((128, 640, 0), (0, 128, 4)), ((0, 512, 0),)
        first.along_z()
        first.own_on(met=False)
        second.along_z()
        second.own_on(met=False)
        third.along_z()
        for n in "aml":
            ref["w" + n][at.c, at.a, at.b, at.z] = ref["part_" + n][...]

    else:
        pl.semaphore_wait(barrier, len(peers))

    lane = iota((64, 128), 1)
    low_lanes = lane < 64
    low_b = low_lanes.astype(F32).astype(BF)
    high_b = (1.0 - low_lanes.astype(F32)).astype(BF)

    def both(v):
        return jnp.concatenate([v * low_b, v * high_b], axis=0)

    def joined(v):
        return jnp.where(low_lanes, v[:64], v[64:])

    if fast:
        loads["x"].wait()
        loads["cot"].wait()
    x = x_ref[...].astype(F32)
    cot = cot_ref[...].astype(F32)
    if fast:
        x, cot = mixed(x, True), mixed(cot, True)
    ref["xs"][...] = x
    ref["cots"][...] = cot
    n1, r1 = normalised(x)
    n1s[...] = n1
    n1b = n1.astype(BF)
    valid = (iota((ROWS, 128), 0) + me * ROWS < valid_len).astype(F32)
    rdiv[...] = row_divisors(me, tensors, valid_len)
    for k in range(TILES):
        wt[k] = tile_weights(k, me, tensors, valid_len)
    if fast:
        first.after_z(1, 3, 2, met=False)
        first.after_b(0, 1, 3, 2, met=False)
        second.after_b(0, met=False)

        @pl.when(at.c == 0)
        def _():
            pl.semaphore_wait(ref["ready"], len(others))

        for j in range(4):
            first.across(j, 0, 0)
        for j in range(4):
            first.across(j, 0, 1)
        second.across(0, 0, 0)
        second.across(0, 0, 1)
        first.after_a(0, 0, 1, 3, 2)
        first.after_a(1, 0, 1, 3, 2)
        second.after_z(1, 3, 2)
        first.after_across()
    for t in range(PAIRS):
        joint = nn(n1b[:, :256], get(wa, t, 0, 0, 384)) + nn(n1b[:, 256:], get(wa, t, 1, 0, 384))
        joint = joint.astype(BF).astype(F32)
        qs[t, 0:ROWS, :] = joint[:, :128]
        ks[t, 0:ROWS, :] = joint[:, 128:256] * valid
        vs[t, 0:ROWS, :] = joint[:, 256:] * valid

    def pooling(p, carry):
        pool(qs.at[p])
        qs[p, 504:STACK, :] = jnp.zeros((8, 128), F32)
        qb[p] = (qs[p] * stack_factors()).astype(BF)
        for which, (raw, windows) in enumerate(((ks, kw), (vs, vw))):
            raw_p = raw.at[p]
            pool(raw_p)
            for start, n in BLANK:
                windows[p, start : start + n, :] = jnp.zeros((n, 128), BF)
            for level in range(LEVELS - 1):
                n = COUNT[level]
                rows = slice(AT[level], AT[level] + n)
                coarse = (raw_p[rows, :] * rdiv[rows, :]).astype(BF)
                if level < 4:
                    windows[p, OWN[level] : OWN[level] + n, :] = coarse
                edge_l[p, which, 16 * level : 16 * level + 16, :] = coarse[:16]
                edge_r[p, which, 16 * level : 16 * level + 16, :] = coarse[n - 16 :]
            rows = slice(AT[5], AT[5] + 8)
            far[me, p, which] = raw_p[rows, :] * rdiv[rows, :]
        exchange(*halos(p))
        return carry

    def to_left(src, dst, sem):
        return pltpu.make_async_remote_copy(
            src, dst, send_sem.at[sem], recv_sem.at[sem], device_id={"tensor": jnp.maximum(me - 1, 0)}, device_id_type=MESH
        )

    def to_right(src, dst, sem):
        return pltpu.make_async_remote_copy(
            src,
            dst,
            send_sem.at[sem],
            recv_sem.at[sem],
            device_id={"tensor": jnp.minimum(me + 1, tensors - 1)},
            device_id_type=MESH,
        )

    def to_peer(k, src, dst, sem):
        return pltpu.make_async_remote_copy(
            src, dst, send_sem.at[sem], recv_sem.at[sem], device_id={"tensor": lax.rem(me + k, tensors)}, device_id_type=MESH
        )

    def exchange(base, left_src, left_dst, right_src, right_dst, far_src, far_dst):
        for k in range(1, tensors):
            to_peer(k, far_src(k), far_dst(k), base + 1 + k).start()

        @pl.when(me > 0)
        def _():
            to_left(left_src, left_dst, base).start()

        @pl.when(me < tensors - 1)
        def _():
            to_right(right_src, right_dst, base + 1).start()

    def exchanged(base, left_src, left_dst, right_src, right_dst, far_src, far_dst):
        @pl.when(me > 0)
        def _():
            to_left(left_src, left_dst, base).wait_send()
            to_right(right_src, right_dst, base + 1).wait_recv()

        @pl.when(me == 0)
        def _():
            right_dst[...] = jnp.zeros(right_dst.shape, BF)

        @pl.when(me < tensors - 1)
        def _():
            to_right(right_src, right_dst, base + 1).wait_send()
            to_left(left_src, left_dst, base).wait_recv()

        @pl.when(me == tensors - 1)
        def _():
            left_dst[...] = jnp.zeros(left_dst.shape, BF)

        for k in range(1, tensors):
            to_peer(k, far_src(k), far_dst(k), base + 1 + k).wait()

    def halos(p):
        block = lambda k: far.at[me, p]
        return (5 * p, edge_l.at[p], halo_r.at[p], edge_r.at[p], halo_l.at[p], block, block)

    lax.fori_loop(0, PAIRS, pooling, 0)
    if fast:
        second.after_b(1, 3, 2)
        third.own_on()
        third.after_z(1, 3, 2)

    def attend(p, carry):
        exchanged(*halos(p))
        for which, windows in enumerate((kw, vw)):
            for level in range(LEVELS - 1):
                windows[p, LEFT[level] : LEFT[level] + 16, :] = halo_l[p, which, 16 * level : 16 * level + 16, :]
                windows[p, RIGHT[level] : RIGHT[level] + 16, :] = halo_r[p, which, 16 * level : 16 * level + 16, :]
            groups = jnp.concatenate([far[g, p, which] for g in range(tensors)], axis=0)
            windows[p, FAR:KEYS, :] = groups.astype(BF)
        for k in range(TILES):
            here = slice(64 * k, 64 * k + 64)
            keys = slice(TILE_AT[k], TILE_AT[k] + 128)
            s = nt(both(qb[p, here, :]), kw[p, keys, :])
            w = wt[k]
            w = jnp.concatenate([w, w], axis=0)
            s = jnp.where(w > 0.0, s, -1e30)
            m = jnp.max(s, axis=-1, keepdims=True)
            e = w * jnp.exp(s - m)
            low = e.astype(BF)
            total = jnp.sum(low.astype(F32), axis=-1, keepdims=True)
            eb[p, k] = low
            ns[here, :] = joined(nn(low, vw[p, keys, :]))
            ml[p, here, :] = joined(jnp.broadcast_to(m, (128, 128)))
            ds_[here, :] = joined(jnp.broadcast_to(total, (128, 128)))
        rows = slice(AT[5], AT[5] + 8)
        num, top, den = ns[rows, :], ml[p, rows, :], ds_[rows, :]
        for level in range(LEVELS - 2, -1, -1):
            n = COUNT[level]
            rows = slice(AT[level], AT[level] + n)
            num, top, den = doubled(tmp_a, num, n // 2), doubled(tmp_b, top, n // 2), doubled(tmp_c, den, n // 2)
            own = ml[p, rows, :]
            both_top = jnp.maximum(own, top)
            left, right = jnp.exp(own - both_top), jnp.exp(top - both_top)
            num = ns[rows, :] * left + num * right
            den = ds_[rows, :] * left + den * right
            top = both_top
        inverse = 1.0 / den
        att[p] = num * inverse
        mm[p] = top
        dacc[p] = inverse
        if fast:

            @pl.when(p == 0)
            def _():
                second.after_a(0, 0, 1, 3, 2)

            @pl.when(p == 1)
            def _():
                third.after_b(0, 1, 3, 2)

            @pl.when(p == 2)
            def _():
                second.after_a(1, 0, 1, 3, 2)

            @pl.when(p == 3)
            def _():
                third.after_a(0, 0, 1, 3, 2)

        return carry

    lax.fori_loop(0, PAIRS, attend, 0)

    if fast:
        second.after_across()
    attb = [att[t].astype(BF) for t in range(PAIRS)]
    branch = []
    for y in range(2):
        total = nt(attb[0], get(wm, 0, y, 0, 128))
        for t in range(1, PAIRS):
            total = total + nt(attb[t], get(wm, t, y, 0, 128))
        branch.append(total)
    branch = jnp.concatenate(branch, axis=1)
    middle = ref["xs"][...] + branch
    n2, r2 = normalised(middle)
    n2s[...] = n2
    n2b = n2.astype(BF)
    n2t = n2b.T
    cotb = ref["cots"][...].astype(BF)
    cott = cotb.T

    acts, slopes = ref["acts"], ref["slopes"]
    for t in range(PAIRS):
        pre = nn(n2b[:, :256], get(wm, t, 0, 128, 640)) + nn(n2b[:, 256:], get(wm, t, 1, 128, 640))
        act, slope = gelu_both(pre)
        act = act.astype(BF)
        acts[t] = act
        slopes[t] = slope
        for y in range(2):
            put(gl, t, y, 0, 512, nn(cott[256 * y : 256 * y + 256, :], act))
        if fast:
            late.across(t, 0, 512, 0)
    if fast:
        third.after_a(1, 0, 1, 3, 2)
        third.after_across()
        late.across_all(late_parts)
    dense, dn2 = [0.0, 0.0], [0.0, 0.0]
    for t in range(PAIRS):
        if fast:
            late.far((1, 3, 2, 0)[t])
        act_grad = nn(cotb[:, :256], get(wl, t, 0, 0, 512)) + nn(cotb[:, 256:], get(wl, t, 1, 0, 512))
        pre_grad = (act_grad * slopes[t]).astype(BF)
        act = acts[t]
        for y in range(2):
            dense[y] = dense[y] + nt(act, get(wl, t, y, 0, 512))
            dn2[y] = dn2[y] + nt(pre_grad, get(wm, t, y, 128, 640))
            put(gm, t, y, 128, 640, nn(n2t[256 * y : 256 * y + 256, :], pre_grad))
        if fast:
            middle_sum.across(t, 128, 640, 0)
    dense = jnp.concatenate(dense, axis=1)
    dn2 = jnp.concatenate(dn2, axis=1)
    result = middle + dense
    out_ref[...] = (mixed(result, False) if fast else result).astype(BF)
    live = (iota((ROWS, 512), 0) + me * ROWS < valid_len).astype(F32)
    small_ref[2:3, :] = jnp.sum(live * result * result, axis=0, keepdims=True)
    small_ref[3:4, :] = jnp.sum(live * branch * branch, axis=0, keepdims=True)
    small_ref[4:5, :] = jnp.sum(live * dense * dense, axis=0, keepdims=True)
    small_ref[5:6, :] = jnp.sum(live, axis=0, keepdims=True)
    small_ref[6:8, :] = jnp.zeros((2, 512), F32)
    n2 = n2s[...]
    small_ref[1:2, :] = jnp.sum(dn2 * n2, axis=0, keepdims=True)
    middle_grad = ref["cots"][...] + norm_back(n2, r2, dn2)
    n2s[...] = middle_grad
    mgb = middle_grad.astype(BF)
    mgt = mgb.T
    for t in range(PAIRS):
        us[t, 0:ROWS, :] = nn(mgb[:, :256], get(wm, t, 0, 0, 128)) + nn(mgb[:, 256:], get(wm, t, 1, 0, 128))
        for y in range(2):
            put(gm, t, y, 0, 128, nn(mgt[256 * y : 256 * y + 256, :], att[t].astype(BF)))
        if fast:
            middle_sum.across(t, 0, 128, 4)
    if fast:
        late.near(1, 3)

    def head_sums(v):
        first = jnp.sum(jnp.where(iota(v.shape, 1) < 64, v, 0.0), axis=-1, keepdims=True)
        second = jnp.sum(jnp.where(iota(v.shape, 1) < 64, 0.0, v), axis=-1, keepdims=True)
        return jnp.where(iota(v.shape, 1) < 64, first, second)

    def attend_back(p, carry):
        up = us.at[p]
        grad, inverse = up[0:ROWS, :], dacc[p]
        delta = head_sums(grad * att[p])
        up[0:ROWS, :] = grad * inverse
        ns[0:ROWS, :] = delta * inverse
        mus[0:ROWS, :] = mm[p]
        for level in range(LEVELS - 1):
            n = COUNT[level + 1]
            after = slice(AT[level + 1], AT[level + 1] + n)
            top_e, top_o = pairs_of(mus, AT[level], n)
            top = jnp.minimum(top_e, top_o)
            fe, fo = jnp.exp(top - top_e), jnp.exp(top - top_o)
            u_e, u_o = pairs_of(up, AT[level], n)
            d_e, d_o = pairs_of(ns, AT[level], n)
            up[after, :] = u_e * fe + u_o * fo
            ns[after, :] = d_e * fe + d_o * fo
            mus[after, :] = top
        for rows in (slice(504, STACK),):
            up[rows, :] = jnp.zeros((8, 128), F32)
            ns[rows, :] = jnp.zeros((8, 128), F32)
            mus[rows, :] = jnp.zeros((8, 128), F32)
        for which in range(2):
            dkw[which * PAIRS + p, 0:512, :] = jnp.zeros((512, 128), F32)
        for k in range(TILES):
            here = slice(64 * k, 64 * k + 64)
            keys = slice(TILE_AT[k], TILE_AT[k] + 128)
            factor = jnp.exp(ml[p, here, :] - mus[here, :])
            g = up[here, :] * factor
            g_high = g.astype(BF)
            g2 = both(g_high)
            g4 = jnp.concatenate([g2, both((g - g_high.astype(F32)).astype(BF))], axis=1)
            v2 = vw[p, keys, :]
            v2 = jnp.concatenate([v2, v2], axis=1)
            h = ns[here, :] * factor
            h2 = jnp.concatenate([h[:, 0:1], h[:, 64:65]], axis=0)
            q2 = both(qb[p, here, :])
            low = eb[p, k]
            d = low.astype(F32) * (nt(g4, v2) - h2)
            d = d.astype(BF)
            dv = tn(low, g2)
            dk = tn(d, q2)
            if k < 6:
                dkw[p, keys, :] = dkw[p, keys, :] + dk
                dkw[PAIRS + p, keys, :] = dkw[PAIRS + p, keys, :] + dv
            else:
                dkw[p, keys, :] = dk
                dkw[PAIRS + p, keys, :] = dv
            dqs[p, here, :] = joined(nn(d, kw[p, keys, :]))
            if fast and k == 3:

                @pl.when(p == 0)
                def _():
                    late.near(2)

                @pl.when(p == 1)
                def _():
                    late.near(0)

                @pl.when(p == 2)
                def _():
                    late.own(outs["l"], 1)

                @pl.when(p == 3)
                def _():
                    late.own(outs["l"], 0)

        for which in range(2):
            row = which * PAIRS + p
            for level in range(LEVELS - 1):
                part = slice(16 * level, 16 * level + 16)
                back_l[p, which, part, :] = dkw[row, LEFT[level] : LEFT[level] + 16, :].astype(BF)
                back_r[p, which, part, :] = dkw[row, RIGHT[level] : RIGHT[level] + 16, :].astype(BF)
            for g in range(tensors):
                dfar[g, p, which] = dkw[row, FAR + 8 * g : FAR + 8 * g + 8, :]
        exchange(*back(p))
        if fast:

            @pl.when(p == 0)
            def _():
                middle_sum.across_all(middle_parts)
                middle_sum.far(1, 3, 2, 0)

            @pl.when(p == 1)
            def _():
                late.own(outs["l"], 3)

            @pl.when(p == 2)
            def _():
                late.own(outs["l"], 2)

            @pl.when(p == 3)
            def _():
                middle_sum.near(1)

        return carry

    def back(p):
        return (
            20 + 5 * p,
            back_l.at[p],
            got_r.at[p],
            back_r.at[p],
            got_l.at[p],
            lambda k: dfar.at[lax.rem(me + k, tensors), p],
            lambda k: gfar.at[k, p],
        )

    lax.fori_loop(0, PAIRS, attend_back, 0)
    def unpool(p, carry):
        exchanged(*back(p))
        factors = stack_factors()
        cur = dqs[p, AT[5] : AT[5] + 8, :] * factors[AT[5] : AT[5] + 8]
        for level in range(LEVELS - 2, -1, -1):
            rows = slice(AT[level], AT[level] + COUNT[level])
            cur = doubled(tmp_a, cur, COUNT[level] // 2) + dqs[p, rows, :] * factors[rows]
        qs[p, 0:ROWS, :] = cur
        for which, raw in enumerate((ks, vs)):
            row = which * PAIRS + p
            raw_p = raw.at[p]
            cur = gfar[1, p, which]
            for k in range(2, tensors):
                cur = cur + gfar[k, p, which]
            cur = cur * rdiv[AT[5] : AT[5] + 8, :]
            for level in range(LEVELS - 2, -1, -1):
                n = COUNT[level]
                rows = slice(AT[level], AT[level] + n)
                part = slice(16 * level, 16 * level + 16)
                if level < 4:
                    raw_p[rows, :] = dkw[row, OWN[level] : OWN[level] + n, :]
                else:
                    raw_p[rows, :] = jnp.zeros((n, 128), F32)
                first = slice(AT[level], AT[level] + 16)
                last = slice(AT[level] + n - 16, AT[level] + n)
                raw_p[first, :] = raw_p[first, :] + got_l[p, which, part, :].astype(F32)
                raw_p[last, :] = raw_p[last, :] + got_r[p, which, part, :].astype(F32)
                cur = doubled(tmp_a, cur, n // 2) + raw_p[rows, :] * rdiv[rows, :]
            raw_p[0:ROWS, :] = cur * (iota((ROWS, 128), 0) + me * ROWS < valid_len).astype(F32)
        return carry

    lax.fori_loop(0, PAIRS, unpool, 0)
    if fast:
        middle_sum.near(3, 2)

    n1 = n1s[...]
    n1t = n1.astype(BF).T
    dn1 = [0.0, 0.0]
    for t in range(PAIRS):
        joint = jnp.concatenate(
            [qs[t, 0:ROWS, :].astype(BF), ks[t, 0:ROWS, :].astype(BF), vs[t, 0:ROWS, :].astype(BF)], axis=1
        )
        for y in range(2):
            put(ga, t, y, 0, 384, nn(n1t[256 * y : 256 * y + 256, :], joint))
            dn1[y] = dn1[y] + nt(joint, get(wa, t, y, 0, 384))
        if fast:
            early.across(t, 0, 384, 0)
    dn1 = jnp.concatenate(dn1, axis=1)
    small_ref[0:1, :] = jnp.sum(dn1 * n1, axis=0, keepdims=True)
    if fast:
        sums = Remote(ref["sum_send"], ref["sum_recv"])
        got = ref["sums"]
        ways = (at.to_other, at.to_x, at.to_y)

        def sum_send(i):
            got[2 * i] = small_ref[...]
            sums.send(i, got.at[2 * i], got.at[2 * i + 1], ways[i])

        def sum_add(i):
            sums.arrived(i, got.at[2 * i + 1], ways[i])
            small_ref[...] = got[2 * i] + got[2 * i + 1]

        middle_sum.near(0)
        middle_sum.own(outs["m"], 1)
        sum_send(0)
        early.across_all(early_parts)
        early.far(1, 3, 2, 0)
        sum_add(0)
        sum_send(1)
        middle_sum.own(outs["m"], 3, 2, 0)
        sum_add(1)
        sum_send(2)
        early.near(1, 3, 2, 0)
        sum_add(2)
        got[6 + at.z] = small_ref[...]
        for k in range(1, 4):
            sums.send(2 + k, got.at[6 + at.z], got.at[6 + at.z], at.to_z(k))
        early.own(outs["a"], 1, 3, 2, 0)
    r1 = lax.rsqrt(row_variance(ref["xs"][...]) + EPS)
    in_grad = n2s[...] + norm_back(n1, r1, dn1)
    ingrad_ref[...] = (mixed(in_grad, False) if fast else in_grad).astype(BF)
    if fast:
        late.finish(outs["l"])
        middle_sum.finish(outs["m"])
        outs["m"][:, 128:640] = outs["m"][:, 128:640] * g2c
        early.finish(outs["a"])
        outs["a"][...] = outs["a"][...] * g1c
        for k in range(1, 4):
            sums.arrived(2 + k, got.at[6], at.to_b)
        total = ((got[6] + got[7]) + got[8]) + got[9]
        gains = jnp.zeros((2, 64), F32)
        for i in range(8):
            gains = gains + jnp.where(4 * at.y + at.z == i, total[0:2, 64 * i : 64 * i + 64], 0.0)
        squares = jnp.sum(total[2:6], axis=1, keepdims=True)
        root = jnp.sqrt(squares[0:3] / squares[3:4])
        lanes = iota((1, 128), 1)
        tail = ref["grads"].at[:, 1536:1664]
        tail[...] = jnp.zeros(tail.shape, F32)
        tail[0:1, 0:64] = gains[0:1] / g1
        tail[1:2, 0:64] = gains[1:2] / g2
        tail[2:3, :] = sum(jnp.where(lanes == i, root[i : i + 1], 0.0) for i in range(3))
        for remote, parts in ((early, early_parts), (middle_sum, middle_parts), (late, late_parts)):
            for lo, hi, base in parts:
                remote.across_drain(lo, hi, base)
            remote.drain(remote.r2.at[0], at.to_x)
        for remote in (first, second, third):
            remote.drain(remote.own, at.to_x)
        sums.drain(small_ref, at.to_x)


def row_variance(v):
    centred = v - jnp.mean(v, axis=-1, keepdims=True)
    return jnp.mean(centred * centred, axis=-1, keepdims=True)


def run_layer(fast, tensors, lengths, inputs, cotangent, *weights):
    vmem = pl.BlockSpec(memory_space=pltpu.VMEM)
    f = lambda *shape: pltpu.VMEM(shape, F32)
    b = lambda *shape: pltpu.VMEM(shape, BF)
    full = (2, 2, 2, 4, 64) if fast else (tensors, 2, 256)
    scratch = {
        "qs": f(PAIRS, STACK, 128),
        "ks": f(PAIRS, STACK, 128),
        "vs": f(PAIRS, STACK, 128),
        "qb": b(PAIRS, STACK, 128),
        "kw": b(PAIRS, KEYS, 128),
        "vw": b(PAIRS, KEYS, 128),
        "wt": f(TILES, 64, 128),
        "rdiv": f(STACK, 128),
        "edge_l": b(PAIRS, 2, HALO, 128),
        "edge_r": b(PAIRS, 2, HALO, 128),
        "halo_l": b(PAIRS, 2, HALO, 128),
        "halo_r": b(PAIRS, 2, HALO, 128),
        "far": f(tensors, PAIRS, 2, 8, 128),
        "eb": b(PAIRS, TILES, 128, 128),
        "ns": f(STACK, 128),
        "ml": f(PAIRS, STACK, 128),
        "ds": f(STACK, 128),
        "att": f(PAIRS, ROWS, 128),
        "mm": f(PAIRS, ROWS, 128),
        "tmp_a": f(ROWS, 128),
        "tmp_b": f(ROWS, 128),
        "tmp_c": f(ROWS, 128),
        "xs": f(ROWS, 512),
        "cots": f(ROWS, 512),
        "n1s": f(ROWS, 512),
        "n2s": f(ROWS, 512),
        "dacc": f(PAIRS, ROWS, 128),
        "us": f(PAIRS, STACK, 128),
        "mus": f(STACK, 128),
        "dqs": f(PAIRS, STACK, 128),
        "acts": b(PAIRS, ROWS, 512),
        "slopes": f(PAIRS, ROWS, 512),
        "dkw": f(2 * PAIRS, KEYS, 128),
        "back_l": b(PAIRS, 2, HALO, 128),
        "back_r": b(PAIRS, 2, HALO, 128),
        "got_l": b(PAIRS, 2, HALO, 128),
        "got_r": b(PAIRS, 2, HALO, 128),
        "dfar": f(tensors, PAIRS, 2, 8, 128),
        "gfar": f(tensors, PAIRS, 2, 8, 128),
        "send_sem": pltpu.SemaphoreType.DMA((40,)),
        "recv_sem": pltpu.SemaphoreType.DMA((40,)),
    }
    if fast:
        ins = ("lengths", *("in_" + n for n in ("x", "cot", "q", "k", "v", "o", "w1", "part_l", "g1", "g2")))
        outs = {"rows": ((ROWS, 1024), BF), "grads": ((64, 1664), F32)}
        scratch |= {n: b(*shape) for n, shape in LOADS}
        scratch |= {"in_sem": pltpu.SemaphoreType.DMA((len(LOADS),))}
        scratch |= {"part_a": b(64, 384), "part_m": b(64, 640), "small": f(8, 512)}
        for name, c in zip("aml", (384, 640, 512), strict=True):
            scratch |= {
                "w" + name: b(*full, c),
                "g" + name: b(*full, c),
                name + "0": b(2, 2, 4, 64, c),
                name + "1": b(2, 4, 64, c),
                name + "2": b(4, 64, c),
                name + "3": b(3, 64, c),
            }
        scratch |= {
            "sums": f(10, 8, 512),
            "gather_send": pltpu.SemaphoreType.DMA((3, 31)),
            "gather_recv": pltpu.SemaphoreType.DMA((3, 31)),
            "reduce_send": pltpu.SemaphoreType.DMA((3, 23)),
            "reduce_recv": pltpu.SemaphoreType.DMA((3, 23)),
            "ready": pltpu.SemaphoreType.REGULAR,
            "sum_send": pltpu.SemaphoreType.DMA((6,)),
            "sum_recv": pltpu.SemaphoreType.DMA((6,)),
        }
    else:
        ins = ("lengths", "x", "cot", "wa", "wm", "wl")
        outs = {"out": ((ROWS, 512), BF), "ingrad": ((ROWS, 512), BF), "small": ((8, 512), F32)}
        outs |= {"g" + name: (w.shape, BF) for name, w in zip("aml", weights, strict=True)}
    return pl.pallas_call(
        functools.partial(layer_kernel, fast, tensors, (*ins, *outs, *scratch)),
        out_shape=tuple(jax.ShapeDtypeStruct(*shape) for shape in outs.values()),
        in_specs=[pl.BlockSpec(memory_space=pltpu.SMEM)] + [pl.BlockSpec(memory_space=pltpu.HBM) if fast else vmem] * (len(ins) - 1),
        out_specs=(vmem,) * len(outs),
        scratch_shapes=list(scratch.values()),
        compiler_params=pltpu.CompilerParams(
            collective_id=0, has_side_effects=True, vmem_limit_bytes=62 * 1024 * 1024
        ),
        name="layer",
    )(lengths, inputs, cotangent, *weights)


def hand_out_kernel(rows, grads, *refs):
    outs, tail, sem = refs[:11], refs[11], refs[12]
    edges = (0, 128, 256, 384, 512, 1024, 1536)
    parts = [rows.at[:, 0:512], rows.at[:, 512:1024]]
    parts += [grads.at[:, lo:hi] for lo, hi in zip(edges, edges[1:])]
    copies = [pltpu.make_async_copy(grads.at[0:8, 1536:1664], tail, sem.at[8])]
    copies += [pltpu.make_async_copy(part, out, sem.at[i]) for i, (part, out) in enumerate(zip(parts, outs))]
    for copy in copies:
        copy.start()
    copies[0].wait()
    for i in range(3):
        outs[8 + i][...] = tail[i, 0 : outs[8 + i].shape[0]]
    for copy in copies[1:]:
        copy.wait()


def hand_out(rows, grads):
    shapes = [(ROWS, 512)] * 2 + [(64, 128)] * 4 + [(64, 512)] * 2 + [(64,)] * 2 + [(3,)]
    return pl.pallas_call(
        hand_out_kernel,
        out_shape=tuple(jax.ShapeDtypeStruct(shape, BF if i < 2 else F32) for i, shape in enumerate(shapes)),
        in_specs=[pl.BlockSpec(memory_space=pltpu.HBM)] * 2,
        out_specs=tuple(pl.BlockSpec(memory_space=pltpu.VMEM) for _ in shapes),
        scratch_shapes=[pltpu.VMEM((8, 128), F32), pltpu.SemaphoreType.DMA((9,))],
        name="hand_out",
    )(rows, grads)


def per_device(
    fast,
    inputs,
    lengths,
    cotangent,
    query_weight,
    key_weight,
    value_weight,
    output_weight,
    inner_weight,
    outer_weight,
    first_gain,
    second_gain,
):
    tensors = lax.axis_size("tensor")
    everyone = ("tensor", "dp")
    if fast:
        rows, grads = run_layer(
            fast,
            tensors,
            lengths,
            inputs,
            cotangent,
            query_weight,
            key_weight,
            value_weight,
            output_weight.T,
            inner_weight,
            outer_weight.T,
            first_gain,
            second_gain,
        )
        out, input_grad, gq, gk, gv, go, gi, gl, gain_one, gain_two, root = hand_out(rows, grads)
        return out, input_grad, gq, gk, gv, go.T, gi, gl.T, gain_one, gain_two, root
    g1 = first_gain.astype(F32)[:, None]
    g2 = second_gain.astype(F32)[:, None]
    scaled = lambda g, w: (g * w.astype(F32)).astype(BF)
    part_a = scaled(g1, jnp.concatenate([query_weight, key_weight, value_weight], axis=1))
    part_m = jnp.concatenate([output_weight.T, scaled(g2, inner_weight)], axis=1)
    parts = (part_a, part_m, outer_weight.T)
    full = [lax.all_gather(p, everyone, axis=0, tiled=True).reshape(tensors, 2, 256, -1) for p in parts]
    out, input_grad, small, *grads = run_layer(fast, tensors, lengths, inputs, cotangent, *full)

    def reduced(g):
        return lax.psum_scatter(
            g.reshape(tensors * 512, g.shape[-1]).astype(F32), everyone, scatter_dimension=0, tiled=True
        )

    ga, gm, gl = (reduced(g) for g in grads)
    small = lax.psum(small, everyone)
    width = first_gain.shape[0]
    gains = lax.dynamic_slice(small, (0, lax.axis_index("dp") * width), (2, width))
    sums = jnp.sum(small, axis=1)
    root_mean_squares = jnp.sqrt(sums[2:5] / sums[5])
    ga = ga * g1
    return (
        out,
        input_grad,
        ga[:, 0:128],
        ga[:, 128:256],
        ga[:, 256:384],
        gm[:, 0:128].T,
        gm[:, 128:640] * g2,
        gl.T,
        gains[0] / first_gain.astype(F32),
        gains[1] / second_gain.astype(F32),
        root_mean_squares,
    )


def solution(mesh):
    fast = (mesh.shape["dp"], mesh.shape["tensor"]) == (8, 4)
    return jax.shard_map(
        functools.partial(per_device, fast),
        mesh=mesh,
        in_specs=(
            P(("dp", "tensor"), None),
            P("dp"),
            P(("dp", "tensor"), None),
            P("dp", "tensor"),
            P("dp", "tensor"),
            P("dp", "tensor"),
            P("tensor", "dp"),
            P("dp", "tensor"),
            P("tensor", "dp"),
            P("dp"),
            P("dp"),
        ),
        out_specs=(
            P(("dp", "tensor"), None),
            P(("dp", "tensor"), None),
            P("dp", "tensor"),
            P("dp", "tensor"),
            P("dp", "tensor"),
            P("tensor", "dp"),
            P("dp", "tensor"),
            P("tensor", "dp"),
            P("dp"),
            P("dp"),
            P(),
        ),
        check_vma=False,
    )
```
